32 devices in a mesh: dp: 4 (over z), fsdp: 8 (over y, x, core).
Axes of the slice: x: 2, y: 2, z: 4, core: 2. Of those that a mesh axis runs over, the one named last changes fastest.
Arguments:
- tokens: bfloat16 [32, 1024, 768], P(('dp', 'fsdp')), may hold values from -6 to 6
- encoder_states: bfloat16 [32, 128, 768], P(('dp', 'fsdp')), may hold values from -6 to 6
- lengths: int32 [32], replicated, may hold values from 1 to 1024, as said below
- dealing: int32 [32], replicated, may hold values from 0 to 31, as said below
- cotangent: bfloat16 [32, 1024, 768], P(('dp', 'fsdp')), may hold values from -6 to 6
- w_query: bfloat16 [768, 768], P(('dp', 'fsdp')), may hold values from -0.109375 to 0.109375
- w_key: bfloat16 [768, 768], P(('dp', 'fsdp')), may hold values from -0.109375 to 0.109375
- w_value: bfloat16 [768, 768], P(('dp', 'fsdp')), may hold values from -0.21875 to 0.21875
- w_out: bfloat16 [768, 768], P(('dp', 'fsdp')), may hold values from -1 to 1
- c_query: bfloat16 [768, 768], P(('dp', 'fsdp')), may hold values from -0.109375 to 0.109375
- c_key: bfloat16 [768, 768], P(('dp', 'fsdp')), may hold values from -0.109375 to 0.109375
- c_value: bfloat16 [768, 768], P(('dp', 'fsdp')), may hold values from -0.21875 to 0.21875
- c_out: bfloat16 [768, 768], P(('dp', 'fsdp')), may hold values from -1 to 1
- w_in: bfloat16 [768, 3072], P(None, ('dp', 'fsdp')), may hold values from -0.21875 to 0.21875
- w_down: bfloat16 [3072, 768], P(('dp', 'fsdp')), may hold values from -0.15625 to 0.15625
- gain_self: bfloat16 [768], P(('dp', 'fsdp')), may hold values from 0.5 to 1.5
- gain_cross: bfloat16 [768], P(('dp', 'fsdp')), may hold values from 0.5 to 1.5
- gain_ffn: bfloat16 [768], P(('dp', 'fsdp')), may hold values from 0.5 to 1.5
- bias_table: bfloat16 [384], P(('dp', 'fsdp')), may hold values from -4 to 4
Outputs:
- output: float32 [32, 1024, 768], P(('dp', 'fsdp'))
- input_grad: float32 [32, 1024, 768], P(('dp', 'fsdp'))
- encoder_grad: float32 [32, 128, 768], P(('dp', 'fsdp'))
- grad_w_query: float32 [768, 768], P(('dp', 'fsdp'))
- grad_w_key: float32 [768, 768], P(('dp', 'fsdp'))
- grad_w_value: float32 [768, 768], P(('dp', 'fsdp'))
- grad_w_out: float32 [768, 768], P(('dp', 'fsdp'))
- grad_c_query: float32 [768, 768], P(('dp', 'fsdp'))
- grad_c_key: float32 [768, 768], P(('dp', 'fsdp'))
- grad_c_value: float32 [768, 768], P(('dp', 'fsdp'))
- grad_c_out: float32 [768, 768], P(('dp', 'fsdp'))
- grad_w_in: float32 [768, 3072], P(None, ('dp', 'fsdp'))
- grad_w_down: float32 [3072, 768], P(('dp', 'fsdp'))
- grad_gain_self: float32 [768], P(('dp', 'fsdp'))
- grad_gain_cross: float32 [768], P(('dp', 'fsdp'))
- grad_gain_ffn: float32 [768], P(('dp', 'fsdp'))
- grad_bias_table: float32 [384], P(('dp', 'fsdp'))
The draws below stay inside these ranges and needn't reach their ends.
Inputs may be any that keep to these rules, and one draw needn't show every extreme that they name: `lengths`: the largest length equals 1024. dealing is a permutation. Slot p sits on device p of the joined axes dp+fsdp, sequence g on device g. Devices whose dp indices differ only in the lowest bit and whose fsdp index is equal form a pair; dealing either leaves the two sequences of a pair in place or exchanges them.
All inputs are finite; a program needn't handle non-finite values.
Results may differ from the reference program's by a relative error of at most 0.029.
Values may be sent and summed in bfloat16 or wider, within the bound.
A program may use at most 512 MiB of HBM per device.

```python
import math
import jax
import jax.numpy as jnp
from jax import lax

D = 768
H = 12
DH = 64
FF = 3072
NB = 32
MAXDIST = 128
LMAX = 1024
ENC = 128
NSEQ = 32
N_DP = 4
N_FSDP = 8


def common_lengths(key):
    base_key = jax.random.fold_in(key, 11)
    first_key, second_key = jax.random.split(base_key, 2)
    drawn = jax.random.randint(first_key, (NSEQ,), 1, LMAX + 1).astype(jnp.int32)
    longest = jax.random.randint(second_key, (), 0, NSEQ).astype(jnp.int32)
    return jnp.where(jnp.arange(NSEQ, dtype=jnp.int32) == longest, LMAX, drawn).astype(jnp.int32)


def draw_lengths(key, part):
    return common_lengths(key)


def draw_dealing(key, part):
    half_dp = N_DP // 2
    pair_idx = jnp.arange(half_dp, dtype=jnp.int32)[:, None, None]
    column_idx = jnp.arange(N_FSDP, dtype=jnp.int32)[None, :, None]
    member_idx = jnp.arange(2, dtype=jnp.int32)[None, None, :]
    device_ids = jnp.broadcast_to((2 * pair_idx + member_idx) * N_FSDP + column_idx, (half_dp, N_FSDP, 2))
    coin_key = jax.random.fold_in(key, 23)
    coins = jax.random.randint(coin_key, (half_dp, N_FSDP, 1), 0, 2).astype(jnp.int32)
    coins = coins.at[0, 0, 0].set(1)
    chosen = jnp.where(coins == 1, device_ids[..., ::-1], device_ids)
    dealt = jnp.zeros((NSEQ,), jnp.int32).at[device_ids.reshape(NSEQ)].set(chosen.reshape(NSEQ))
    return dealt.astype(jnp.int32)


def shard_levels(key, shape, shards, smallest, high):
    def one(position, parts):
        heights = jax.random.uniform(jax.random.fold_in(jax.random.fold_in(key, 6), position), (parts,), jnp.float32, smallest / len(shards), high / len(shards))
        return jnp.repeat(jnp.exp(heights), shape[position] // parts).reshape((-1,) + (1,) * (len(shape) - position - 1))

    gain = one(*shards[0])
    for cut in shards[1:]:
        gain = gain * one(*cut)
    return gain


def gaussian(key, extent, scale, most, cuts=(), kind=jnp.bfloat16):
    loudness = shard_levels(key, extent, cuts, -0.22, 0.18) if cuts else 1.0
    values = jax.random.normal(key, extent, jnp.float32) * scale * loudness
    return jnp.minimum(jnp.maximum(values, -most), most).astype(kind)


def setup_inputs(seed: int = 0) -> dict:
    arg_keys = jax.random.split(jax.random.key(seed), 20)
    tokens = gaussian(arg_keys[0], (NSEQ, LMAX, D), 1.0, 6.0, ((0, 32),))
    encoder_states = gaussian(arg_keys[1], (NSEQ, ENC, D), 1.0, 6.0, ((0, 32),))
    lengths = draw_lengths(jax.random.fold_in(arg_keys[19], 71), 0)
    dealing = draw_dealing(jax.random.fold_in(arg_keys[19], 71), 0)
    cotangent = gaussian(arg_keys[4], (NSEQ, LMAX, D), 1.0, 6.0, ((0, 32),))
    w_query = gaussian(arg_keys[5], (D, D), (4 * D) ** -0.5, 0.109375, ((0, 32),))
    w_key = gaussian(arg_keys[6], (D, D), (4 * D) ** -0.5, 0.109375, ((0, 32),))
    w_value = gaussian(arg_keys[7], (D, D), D ** -0.5, 0.21875, ((0, 32),))
    w_out = gaussian(arg_keys[8], (D, D), (DH // 2) ** -0.5, 1.0, ((0, 32),))
    c_query = gaussian(arg_keys[9], (D, D), (4 * D) ** -0.5, 0.109375, ((0, 32),))
    c_key = gaussian(arg_keys[10], (D, D), (4 * D) ** -0.5, 0.109375, ((0, 32),))
    c_value = gaussian(arg_keys[11], (D, D), D ** -0.5, 0.21875, ((0, 32),))
    c_out = gaussian(arg_keys[12], (D, D), (DH // 2) ** -0.5, 1.0, ((0, 32),))
    w_in = gaussian(arg_keys[13], (D, FF), D ** -0.5, 0.21875, ((1, 32),))
    w_down = gaussian(arg_keys[14], (FF, D), (FF // 2) ** -0.5, 0.15625, ((0, 32),))
    gain_self = jnp.clip(1.0 + 0.1 * jax.random.normal(arg_keys[15], (D,), jnp.float32), 0.5, 1.5).astype(jnp.bfloat16)
    gain_cross = jnp.clip(1.0 + 0.1 * jax.random.normal(arg_keys[16], (D,), jnp.float32), 0.5, 1.5).astype(jnp.bfloat16)
    gain_ffn = jnp.clip(1.0 + 0.1 * jax.random.normal(arg_keys[17], (D,), jnp.float32), 0.5, 1.5).astype(jnp.bfloat16)
    bias_table = gaussian(arg_keys[18], (NB * H,), 1.0, 4.0, ((0, 32),))
    return {"tokens": tokens, "encoder_states": encoder_states, "lengths": lengths, "dealing": dealing, "cotangent": cotangent, "w_query": w_query, "w_key": w_key, "w_value": w_value, "w_out": w_out, "c_query": c_query, "c_key": c_key, "c_value": c_value, "c_out": c_out, "w_in": w_in, "w_down": w_down, "gain_self": gain_self, "gain_cross": gain_cross, "gain_ffn": gain_ffn, "bias_table": bias_table}


@jax.custom_vjp
def low(v):
    return lax.optimization_barrier(v.astype(jnp.bfloat16)).astype(jnp.float32)

@jax.custom_vjp
def low_back(v):
    return v

def low_keep(v):
    return (low(v), None)

def low_pass(kept, grad):
    return (grad,)

def back_keep(v):
    return (v, None)

def back_low(kept, grad):
    return (low(grad),)
low.defvjp(low_keep, low_pass)
low_back.defvjp(back_keep, back_low)
EPSILON = 1e-06
MASKED = -1e+30

def bucket_of(distance):
    exact_count = NB // 2
    bucket = jnp.minimum(distance, exact_count)
    for level_idx in range(1, exact_count):
        threshold = int(math.ceil(exact_count * (MAXDIST / exact_count) ** (level_idx / exact_count)))
        bucket = bucket + (distance >= threshold).astype(jnp.int32)
    return bucket

def normed(values_in, gain_vec):
    return values_in * lax.rsqrt(lax.optimization_barrier(jnp.mean(values_in * values_in, axis=-1, keepdims=True)) + EPSILON) * gain_vec

def matmul(left_op, right_op):
    return jnp.dot(left_op, right_op, precision=lax.Precision.HIGHEST)

def self_attend(queries, key_rows, value_rows, bias_table, seq_length):
    positions = jnp.arange(LMAX, dtype=jnp.int32)
    distance = positions[:, None] - positions[None, :]
    allowed = (distance >= 0) & (positions[None, :] < seq_length)
    near_bias = jnp.transpose(bias_table[bucket_of(jnp.maximum(distance, 0))], (2, 0, 1))
    q_heads = queries.reshape(LMAX, H, DH)
    k_heads = key_rows.reshape(LMAX, H, DH)
    v_heads = value_rows.reshape(LMAX, H, DH)
    scores = low_back(jnp.einsum('qhd,khd->hqk', q_heads, k_heads, precision=lax.Precision.HIGHEST)) + near_bias
    scores = jnp.where(allowed[None], scores, MASKED)
    attn_probs = jax.nn.softmax(scores, axis=-1)
    mixed = jnp.einsum('hqk,khd->qhd', low(attn_probs), v_heads, precision=lax.Precision.HIGHEST)
    return mixed.reshape(LMAX, D)

def cross_attend(queries, key_rows, value_rows):
    q_heads = queries.reshape(LMAX, H, DH)
    k_heads = key_rows.reshape(ENC, H, DH)
    v_heads = value_rows.reshape(ENC, H, DH)
    scores = low_back(jnp.einsum('qhd,khd->hqk', q_heads, k_heads, precision=lax.Precision.HIGHEST))
    attn_probs = jax.nn.softmax(scores, axis=-1)
    mixed = jnp.einsum('hqk,khd->qhd', low(attn_probs), v_heads, precision=lax.Precision.HIGHEST)
    return mixed.reshape(LMAX, D)

def layer(params_in, token_rows, encoder_rows, seq_length):
    w_query, w_key, w_value, w_out, c_query, c_key, c_value, c_out, w_in, w_down, gain_self, gain_cross, gain_ffn, bias_table = params_in
    positions = jnp.arange(LMAX, dtype=jnp.int32)
    row_valid = (positions < seq_length).astype(jnp.float32)[:, None]
    normed_one = low(normed(token_rows, gain_self))
    queries = low(low_back(matmul(normed_one, w_query)))
    key_rows = low(low_back(matmul(normed_one, w_key)))
    value_rows = low(low_back(matmul(normed_one, w_value)))
    attended = low(low_back(jax.checkpoint(self_attend)(queries, key_rows, value_rows, bias_table, seq_length)))
    after_self = token_rows + low_back(matmul(attended, w_out))
    normed_two = low(normed(after_self, gain_cross))
    cross_queries = low(low_back(matmul(normed_two, c_query)))
    cross_keys = low(low_back(matmul(encoder_rows, c_key)))
    cross_values = low(low_back(matmul(encoder_rows, c_value)))
    mixed = low(low_back(jax.checkpoint(cross_attend)(cross_queries, cross_keys, cross_values)))
    after_cross = after_self + low_back(matmul(mixed, c_out))
    normed_three = low(normed(after_cross, gain_ffn))
    hidden = low(jax.nn.gelu(low_back(matmul(normed_three, w_in))))
    return (after_cross + low_back(matmul(hidden, w_down))) * row_valid

def reference(tokens, encoder_states, lengths, dealing, cotangent, w_query, w_key, w_value, w_out, c_query, c_key, c_value, c_out, w_in, w_down, gain_self, gain_cross, gain_ffn, bias_table):
    params_in = (w_query.astype(jnp.float32), w_key.astype(jnp.float32), w_value.astype(jnp.float32), w_out.astype(jnp.float32), c_query.astype(jnp.float32), c_key.astype(jnp.float32), c_value.astype(jnp.float32), c_out.astype(jnp.float32), w_in.astype(jnp.float32), w_down.astype(jnp.float32), gain_self.astype(jnp.float32), gain_cross.astype(jnp.float32), gain_ffn.astype(jnp.float32), bias_table.astype(jnp.float32).reshape(NB, H))

    def visit(grad_total, slot_idx):
        source = dealing[slot_idx]
        token_rows = tokens[source].astype(jnp.float32)
        encoder_rows = encoder_states[slot_idx].astype(jnp.float32)
        grad_rows = cotangent[source].astype(jnp.float32)
        seq_length = lengths[source]

        def apply_layer(params_here, rows_here, enc_here):
            return layer(params_here, rows_here, enc_here, seq_length)
        result, pull_back = jax.vjp(apply_layer, params_in, token_rows, encoder_rows)
        grad_params, grad_tokens, grad_encoder = pull_back(grad_rows)
        grad_total = jax.tree.map(jnp.add, grad_total, grad_params)
        return (grad_total, (result, grad_tokens, grad_encoder))
    zero_grads = jax.tree.map(jnp.zeros_like, params_in)
    grad_total, (results, grad_tokens, grad_encoder) = lax.scan(visit, zero_grads, jnp.arange(NSEQ, dtype=jnp.int32))
    output = jnp.zeros(tokens.shape, results.dtype).at[dealing].set(results)
    input_grad = jnp.zeros(tokens.shape, grad_tokens.dtype).at[dealing].set(grad_tokens)
    return (output, input_grad, grad_encoder, grad_total[0], grad_total[1], grad_total[2], grad_total[3], grad_total[4], grad_total[5], grad_total[6], grad_total[7], grad_total[8], grad_total[9], grad_total[10], grad_total[11], grad_total[12], grad_total[13].reshape(NB * H))
```

```python
import functools
import math

import jax
import jax.numpy as jnp
from jax import lax
from jax.experimental import pallas as pl
from jax.experimental.pallas import tpu as pltpu
from jax.sharding import PartitionSpec as P

H = 12
DH = 64
NB = 32
MAXDIST = 128
EPSILON = 1e-06
MASKED = -1e30
LANES = 128
ROWS = 256
F32 = jnp.float32
BF16 = jnp.bfloat16
GELU_C = math.sqrt(2.0 / math.pi)
GELU_A = 0.044715


def bucket_of(distance):
    exact_count = NB // 2
    bucket = jnp.minimum(distance, exact_count)
    for level_idx in range(1, exact_count):
        threshold = int(
            math.ceil(exact_count * (MAXDIST / exact_count) ** (level_idx / exact_count))
        )
        bucket = bucket + (distance >= threshold).astype(jnp.int32)
    return bucket


def nn(left_op, right_op):
    return lax.dot_general(
        left_op, right_op, (((1,), (0,)), ((), ())), preferred_element_type=F32
    )


def nt(left_op, right_op):
    return lax.dot_general(
        left_op, right_op, (((1,), (1,)), ((), ())), preferred_element_type=F32
    )


def tn(left_op, right_op):
    return lax.dot_general(
        left_op, right_op, (((0,), (0,)), ((), ())), preferred_element_type=F32
    )


def unit_rows(values_in):
    inv_rms = lax.rsqrt(jnp.mean(values_in * values_in, axis=-1, keepdims=True) + EPSILON)
    return values_in * inv_rms, inv_rms


def norm_back(grad_in, unit, inv_rms, gain_vec):
    scaled = grad_in * gain_vec
    through = inv_rms * (scaled - unit * jnp.mean(scaled * unit, axis=-1, keepdims=True))
    return through, jnp.sum(grad_in * unit, axis=0, keepdims=True)


def head_lane(shape, which):
    lane = lax.broadcasted_iota(jnp.int32, shape, len(shape) - 1)
    return (lane // DH) == which


def self_forward_kernel(
    length_ref, x_ref, gain_ref, wq_ref, wk_ref, wv_ref, far_ref, near_ref,
    q_ref, k_ref, v_ref, o_ref, p_ref, a_ref, tile_ref,
):
    step = pl.program_id(0)
    seq = x_ref.shape[0]
    width = wq_ref.shape[1]

    @pl.when(step == 0)
    def _():
        unit, _inv = unit_rows(x_ref[...].astype(F32))
        a_ref[...] = (unit * gain_ref[...]).astype(BF16)

    for w_ref, out_ref in ((wq_ref, q_ref), (wk_ref, k_ref), (wv_ref, v_ref)):
        out_ref[...] = nn(a_ref[...], w_ref[...]).astype(BF16)

    key_pos = lax.broadcasted_iota(jnp.int32, (seq, 1), 0)
    key_dead = key_pos >= length_ref[0]
    row = lax.broadcasted_iota(jnp.int32, (ROWS, ROWS + LANES), 0)
    col = lax.broadcasted_iota(jnp.int32, (ROWS, ROWS + LANES), 1)
    ahead = col - LANES > row
    for pair in range(width // LANES):
        cols = slice(pair * LANES, (pair + 1) * LANES)
        outs = [None] * (seq // ROWS)
        for which in range(2):
            local = pair * 2 + which
            head = step * (width // DH) + local
            spun = pltpu.roll(
                jnp.broadcast_to(near_ref[pl.ds(head, 1), :], (ROWS, 4 * LANES)),
                0, 1, stride=1, stride_axis=0,
            )
            tile_ref[...] = jnp.where(ahead, MASKED, spun[:, : ROWS + LANES])
            own = head_lane((seq, LANES), which)
            extra = lax.broadcasted_iota(jnp.int32, (seq, LANES), 1) == (DH if which == 0 else 0)
            far = jnp.where(key_dead, MASKED, far_ref[head]).astype(BF16)
            keys = jnp.where(own, k_ref[:, cols], jnp.where(extra, far, jnp.zeros((), BF16)))
            values = jnp.where(own, v_ref[:, cols], jnp.zeros((), BF16))
            queries = jnp.where(own, q_ref[:, cols], jnp.where(extra, 1.0, 0.0).astype(BF16))
            for blk in range(seq // ROWS):
                rows = slice(blk * ROWS, (blk + 1) * ROWS)
                span = (blk + 1) * ROWS
                cut = max(span - ROWS - LANES, 0)
                scores = nt(queries[rows], keys[:span])
                if cut:
                    near = scores[:, cut:] + tile_ref[...]
                    scores = jnp.concatenate([scores[:, :cut], near], axis=1)
                elif span == ROWS:
                    scores = scores + tile_ref[:, LANES:]
                else:
                    near = scores[:, ROWS - LANES :] + tile_ref[...]
                    scores = jnp.concatenate([scores[:, : ROWS - LANES], near], axis=1)
                top = jnp.max(scores, axis=1, keepdims=True)
                weights = jnp.exp(scores - top)
                total = jnp.sum(weights, axis=1, keepdims=True)
                probs = (weights * (1.0 / total)).astype(BF16)
                p_ref[local, rows, :span] = probs
                mixed = nn(probs, values[:span])
                outs[blk] = mixed if outs[blk] is None else outs[blk] + mixed
        for blk in range(seq // ROWS):
            o_ref[blk * ROWS : (blk + 1) * ROWS, cols] = outs[blk].astype(BF16)


def self_forward(length, x, gain, wq, wk, wv, far, near):
    seq, model = x.shape
    width = 256
    steps = model // width
    whole = lambda shape: pl.BlockSpec(shape, lambda i: (0,) * len(shape))
    smem = pl.BlockSpec(memory_space=pltpu.SMEM)
    columns = pl.BlockSpec((seq, width), lambda i: (0, i))
    weight = pl.BlockSpec((model, width), lambda i: (0, i))
    heads = width // DH
    return pl.pallas_call(
        self_forward_kernel,
        grid=(steps,),
        in_specs=[
            smem, whole((seq, model)), whole((1, model)), weight, weight, weight,
            smem, whole(near.shape),
        ],
        out_specs=[
            columns, columns, columns, columns,
            pl.BlockSpec((heads, seq, seq), lambda i: (i, 0, 0)),
            whole((seq, model)),
        ],
        out_shape=[jax.ShapeDtypeStruct((seq, model), BF16)] * 4
        + [
            jax.ShapeDtypeStruct((H, seq, seq), BF16),
            jax.ShapeDtypeStruct((seq, model), BF16),
        ],
        scratch_shapes=[pltpu.VMEM((ROWS, ROWS + LANES), F32)],
        compiler_params=pltpu.CompilerParams(vmem_limit_bytes=60 * 1024 * 1024),
        cost_estimate=pl.CostEstimate(
            flops=6 * seq * model * model + 4 * seq * seq * model,
            bytes_accessed=2 * H * seq * seq + 16 * seq * model,
            transcendentals=H * seq * seq,
        ),
        name="self_forward",
    )(length, x, gain, wq, wk, wv, far, near)


def middle_kernel(
    length_ref, x_ref, o_ref, cot_ref, enc_ref, gain_ref, wo_ref, cq_ref, ck_ref, cv_ref,
    co_ref, win_ref, wdown_ref,
    out_ref, g1_ref, a2_ref, mix_ref, a3_ref, r_ref, du_ref, g_ref, g2_ref, dcq_ref,
    dck_ref, dcv_ref, egrad_ref, gain_grad_ref,
    keys_ref, values_ref, dk_acc, dv_acc,
):
    step = pl.program_id(0)
    last = pl.num_programs(0) - 1
    rows = x_ref.shape[0]
    model = x_ref.shape[1]
    pairs = model // LANES

    @pl.when(step == 0)
    def _():
        keys_ref[...] = nn(enc_ref[...], ck_ref[...]).astype(BF16)
        values_ref[...] = nn(enc_ref[...], cv_ref[...]).astype(BF16)
        dk_acc[...] = jnp.zeros_like(dk_acc)
        dv_acc[...] = jnp.zeros_like(dv_acc)
        gain_grad_ref[...] = jnp.zeros_like(gain_grad_ref)

    gain_cross = gain_ref[0:1, :]
    gain_ffn = gain_ref[1:2, :]
    pos = step * rows + lax.broadcasted_iota(jnp.int32, (rows, 1), 0)
    valid = jnp.where(pos < length_ref[0], 1.0, 0.0).astype(F32)

    x1 = x_ref[...].astype(F32) + nn(o_ref[...], wo_ref[...])
    unit2, inv2 = unit_rows(x1)
    a2 = (unit2 * gain_cross).astype(BF16)
    a2_ref[...] = a2
    cq = nn(a2, cq_ref[...]).astype(BF16)
    probs = []
    mixed = []
    zero = jnp.zeros((), BF16)
    for pair in range(pairs):
        cols = slice(pair * LANES, (pair + 1) * LANES)
        total_out = None
        for which in range(2):
            own = head_lane((rows, LANES), which)
            own_key = head_lane((keys_ref.shape[0], LANES), which)
            scores = nt(jnp.where(own, cq[:, cols], zero), keys_ref[:, cols])
            top = jnp.max(scores, axis=1, keepdims=True)
            weights = jnp.exp(scores - top)
            prob = weights * (1.0 / jnp.sum(weights, axis=1, keepdims=True))
            probs.append(prob)
            part = nn(prob.astype(BF16), jnp.where(own_key, values_ref[:, cols], zero))
            total_out = part if total_out is None else total_out + part
        mixed.append(total_out.astype(BF16))
    mix = jnp.concatenate(mixed, axis=1)
    mix_ref[...] = mix
    x2 = x1 + nn(mix, co_ref[...])
    unit3, inv3 = unit_rows(x2)
    a3 = (unit3 * gain_ffn).astype(BF16)
    a3_ref[...] = a3
    grad = cot_ref[...].astype(F32) * valid
    grad_low = grad.astype(BF16)
    g_ref[...] = grad_low
    result = x2
    dy3 = None
    hidden_count = win_ref.shape[0]
    chunk = model
    for start in range(0, hidden_count, chunk):
        part = slice(start, start + chunk)
        z = nt(a3, win_ref[part, :])
        zz = z * z
        t = jnp.tanh(GELU_C * z * (1.0 + GELU_A * zz))
        half = 0.5 + 0.5 * t
        r = (z * half).astype(BF16)
        r_ref[:, part] = r
        slope = half + (0.5 * GELU_C) * z * (1.0 - t * t) * (1.0 + (3.0 * GELU_A) * zz)
        du = (nt(grad_low, wdown_ref[part, :]) * slope).astype(BF16)
        du_ref[:, part] = du
        result = result + nn(r, wdown_ref[part, :])
        back = nn(du, win_ref[part, :])
        dy3 = back if dy3 is None else dy3 + back
    out_ref[...] = result * valid
    through, gain_part = norm_back(dy3, unit3, inv3, gain_ffn)
    gain_grad_ref[1:2, :] += gain_part
    g2 = grad + through
    g2_low = g2.astype(BF16)
    g2_ref[...] = g2_low
    dmix = nt(g2_low, co_ref[...]).astype(BF16)
    dq_parts = []
    for pair in range(pairs):
        cols = slice(pair * LANES, (pair + 1) * LANES)
        dq = None
        for which in range(2):
            own = head_lane((rows, LANES), which)
            own_key = head_lane((keys_ref.shape[0], LANES), which)
            prob = probs[2 * pair + which]
            d_out = jnp.where(own, dmix[:, cols], zero)
            dp = nt(d_out, values_ref[:, cols])
            ds = prob * (dp - jnp.sum(prob * dp, axis=1, keepdims=True))
            ds_low = ds.astype(BF16)
            dv_acc[:, cols] += tn(prob.astype(BF16), d_out)
            dk_acc[:, cols] += tn(ds_low, jnp.where(own, cq[:, cols], zero))
            part = nn(ds_low, jnp.where(own_key, keys_ref[:, cols], zero))
            dq = part if dq is None else dq + part
        dq_parts.append(dq.astype(BF16))
    dcq = jnp.concatenate(dq_parts, axis=1)
    dcq_ref[...] = dcq
    through, gain_part = norm_back(nt(dcq, cq_ref[...]), unit2, inv2, gain_cross)
    gain_grad_ref[0:1, :] += gain_part
    g1_ref[...] = g2 + through

    @pl.when(step == last)
    def _():
        dk = dk_acc[...].astype(BF16)
        dv = dv_acc[...].astype(BF16)
        dck_ref[...] = dk
        dcv_ref[...] = dv
        egrad_ref[...] = nt(dk, ck_ref[...]) + nt(dv, cv_ref[...])


def middle(length, x, o, cot, enc, gains, wo, cq, ck, cv, co, win_t, wdown):
    seq, model = x.shape
    hidden = win_t.shape[0]
    enc_len = enc.shape[0]
    steps = seq // ROWS
    whole = lambda shape: pl.BlockSpec(shape, lambda i: (0,) * len(shape))
    held = lambda shape: pl.BlockSpec(
        shape, lambda i: (0,) * len(shape), pipeline_mode=pl.Buffered(1)
    )
    smem = pl.BlockSpec(memory_space=pltpu.SMEM)
    block = lambda width: pl.BlockSpec((ROWS, width), lambda i: (i, 0))
    square = held((model, model))
    wide = held((hidden, model))
    low = lambda width: jax.ShapeDtypeStruct((seq, width), BF16)
    return pl.pallas_call(
        middle_kernel,
        grid=(steps,),
        in_specs=[
            smem, block(model), block(model), block(model), held((enc_len, model)),
            held((2, model)), square, square, square, square, square, wide, wide,
        ],
        out_specs=[
            block(model), block(model), block(model), block(model), block(model),
            block(hidden), block(hidden), block(model), block(model), block(model),
            whole((enc_len, model)), whole((enc_len, model)), whole((enc_len, model)),
            whole((2, model)),
        ],
        out_shape=[
            jax.ShapeDtypeStruct((seq, model), F32),
            jax.ShapeDtypeStruct((seq, model), F32),
            low(model), low(model), low(model), low(hidden), low(hidden),
            low(model), low(model), low(model),
            jax.ShapeDtypeStruct((enc_len, model), BF16),
            jax.ShapeDtypeStruct((enc_len, model), BF16),
            jax.ShapeDtypeStruct((enc_len, model), F32),
            jax.ShapeDtypeStruct((2, model), F32),
        ],
        scratch_shapes=[
            pltpu.VMEM((enc_len, model), BF16),
            pltpu.VMEM((enc_len, model), BF16),
            pltpu.VMEM((enc_len, model), F32),
            pltpu.VMEM((enc_len, model), F32),
        ],
        compiler_params=pltpu.CompilerParams(vmem_limit_bytes=60 * 1024 * 1024),
        cost_estimate=pl.CostEstimate(
            flops=12 * seq * model * model + 8 * seq * model * hidden,
            bytes_accessed=40 * seq * model + 10 * model * model + 4 * hidden * model,
            transcendentals=seq * hidden,
        ),
        name="middle",
    )(length, x, o, cot, enc, gains, wo, cq, ck, cv, co, win_t, wdown)


def self_backward_kernel(
    x_ref, gain_ref, a_ref, g1_ref, q_ref, k_ref, v_ref, o_ref, p_ref,
    wo_ref, wq_ref, wk_ref, wv_ref,
    ingrad_ref, gwq_ref, gwk_ref, gwv_ref, gwo_ref, gain_grad_ref, hist_ref,
    low_ref, dy_acc, near_acc, dk_acc, dv_acc, dq_scr,
):
    step = pl.program_id(0)
    last = pl.num_programs(0) - 1
    seq = x_ref.shape[0]
    width = wq_ref.shape[1]

    @pl.when(step == 0)
    def _():
        low_ref[...] = g1_ref[...].astype(BF16)
        dy_acc[...] = jnp.zeros_like(dy_acc)

    d_all = nt(low_ref[...], wo_ref[...]).astype(BF16)
    gwo_ref[...] = tn(o_ref[...], low_ref[...]).astype(BF16)
    zero = jnp.zeros((), BF16)
    for pair in range(width // LANES):
        cols = slice(pair * LANES, (pair + 1) * LANES)
        dk_acc[...] = jnp.zeros_like(dk_acc)
        dv_acc[...] = jnp.zeros_like(dv_acc)
        dq_blocks = [None] * (seq // ROWS)
        for which in range(2):
            local = pair * 2 + which
            head = step * (width // DH) + local
            own = head_lane((seq, LANES), which)
            d_out = jnp.where(own, d_all[:, cols], zero)
            queries = jnp.where(own, q_ref[:, cols], zero)
            keys = jnp.where(own, k_ref[:, cols], zero)
            for blk in range(seq // ROWS):
                rows = slice(blk * ROWS, (blk + 1) * ROWS)
                span = (blk + 1) * ROWS
                prob_low = p_ref[local, rows, :span]
                prob = prob_low.astype(F32)
                dp = nt(d_out[rows], v_ref[:span, cols])
                ds = prob * (dp - jnp.sum(prob * dp, axis=1, keepdims=True))
                if blk == 0:
                    near_acc[:, :LANES] = jnp.zeros((ROWS, LANES), F32)
                    near_acc[:, LANES:] = ds
                else:
                    near_acc[...] += ds[:, span - ROWS - LANES :]
                ds_low = ds.astype(BF16)
                part = nn(ds_low, keys[:span])
                dq_blocks[blk] = part if which == 0 else dq_blocks[blk] + part
                dk_acc[:span, :] += tn(ds_low, queries[rows])
                dv_acc[:span, :] += tn(prob_low, d_out[rows])
            padded = jnp.concatenate(
                [near_acc[...], jnp.zeros((ROWS, LANES), F32)], axis=1
            )
            count = ROWS
            while count > 1:
                count //= 2
                padded = padded[:count] + pltpu.roll(padded[count:], 4 * LANES - count, 1)
            hist_ref[pl.ds(head, 1), :] = padded
        for blk in range(seq // ROWS):
            rows = slice(blk * ROWS, (blk + 1) * ROWS)
            dq_scr[0, rows, cols] = dq_blocks[blk].astype(BF16)
        dq_scr[1, :, cols] = dk_acc[...].astype(BF16)
        dq_scr[2, :, cols] = dv_acc[...].astype(BF16)
    dy_acc[...] += (
        nt(dq_scr[0], wq_ref[...]) + nt(dq_scr[1], wk_ref[...]) + nt(dq_scr[2], wv_ref[...])
    )
    gwq_ref[...] = tn(a_ref[...], dq_scr[0]).astype(BF16)
    gwk_ref[...] = tn(a_ref[...], dq_scr[1]).astype(BF16)
    gwv_ref[...] = tn(a_ref[...], dq_scr[2]).astype(BF16)

    @pl.when(step == last)
    def _():
        unit, inv = unit_rows(x_ref[...].astype(F32))
        through, gain_part = norm_back(dy_acc[...], unit, inv, gain_ref[...])
        ingrad_ref[...] = g1_ref[...] + through
        gain_grad_ref[...] = gain_part


def self_backward(x, gain, a1, g1, q, k, v, o, p, wo, wq, wk, wv):
    seq, model = x.shape
    width = 256
    heads = width // DH
    steps = model // width
    held = lambda shape: pl.BlockSpec(
        shape, lambda i: (0,) * len(shape), pipeline_mode=pl.Buffered(1)
    )
    whole = lambda shape: pl.BlockSpec(shape, lambda i: (0,) * len(shape))
    columns = pl.BlockSpec((seq, width), lambda i: (0, i))
    weight = pl.BlockSpec((model, width), lambda i: (0, i))
    weight_rows = pl.BlockSpec((width, model), lambda i: (i, 0))
    square = jax.ShapeDtypeStruct((model, model), BF16)
    return pl.pallas_call(
        self_backward_kernel,
        grid=(steps,),
        in_specs=[
            held((seq, model)), held((1, model)), held((seq, model)), held((seq, model)),
            columns, columns, columns, columns,
            pl.BlockSpec((heads, seq, seq), lambda i: (i, 0, 0)),
            weight_rows, weight, weight, weight,
        ],
        out_specs=[
            whole((seq, model)), weight, weight, weight, weight_rows, whole((1, model)),
            whole((16, 4 * LANES)),
        ],
        out_shape=[
            jax.ShapeDtypeStruct((seq, model), F32), square, square, square, square,
            jax.ShapeDtypeStruct((1, model), F32),
            jax.ShapeDtypeStruct((16, 4 * LANES), F32),
        ],
        scratch_shapes=[
            pltpu.VMEM((seq, model), BF16),
            pltpu.VMEM((seq, model), F32),
            pltpu.VMEM((ROWS, ROWS + LANES), F32),
            pltpu.VMEM((seq, LANES), F32),
            pltpu.VMEM((seq, LANES), F32),
            pltpu.VMEM((3, seq, width), BF16),
        ],
        compiler_params=pltpu.CompilerParams(vmem_limit_bytes=60 * 1024 * 1024),
        cost_estimate=pl.CostEstimate(
            flops=16 * seq * model * model + 8 * seq * seq * model,
            bytes_accessed=2 * H * seq * seq + 24 * seq * model,
            transcendentals=0,
        ),
        name="self_backward",
    )(x, gain, a1, g1, q, k, v, o, p, wo, wq, wk, wv)


def body(
    tokens, encoder_states, lengths, dealing, cotangent,
    w_query, w_key, w_value, w_out, c_query, c_key, c_value, c_out, w_in, w_down,
    gain_self, gain_cross, gain_ffn, bias_table,
):
    axes = ("dp", "fsdp")
    fsdp_size = lax.axis_size("fsdp")
    dp_size = lax.axis_size("dp")
    dev_count = dp_size * fsdp_size
    dp_index = lax.axis_index("dp")
    own = dp_index * fsdp_size + lax.axis_index("fsdp")
    seq_len, model = tokens.shape[1:]
    route = [(a, a ^ 1) for a in range(dp_size)]

    x = tokens[0]
    cot = cotangent[0]
    in_place = lax.dynamic_slice_in_dim(dealing, own, 1) == own
    enc_other = lax.ppermute(encoder_states[0], "dp", route)
    enc = jnp.where(in_place[:, None], encoder_states[0], enc_other)
    length = lax.dynamic_slice_in_dim(lengths, own, 1)

    part = w_query.shape[0]
    gain_part = gain_self.shape[0]
    small = jnp.concatenate([gain_self, gain_cross, gain_ffn, bias_table])
    small_row = jnp.pad(small, (0, model - small.shape[0]))[None, :]
    small_row = jnp.pad(small_row, ((0, 7), (0, 0)))
    first = lax.all_gather(
        jnp.concatenate([w_query, w_key, w_value, small_row], axis=0), axes, axis=0
    )
    second = lax.all_gather(
        jnp.concatenate([w_out, c_query, c_key, c_value, c_out, w_in.T, w_down], axis=0),
        axes, axis=0,
    )
    square = lambda pile, at: pile[:, at * part : (at + 1) * part].reshape(-1, model)
    wq, wk, wv = (square(first, i) for i in range(3))
    wo, cq, ck, cv, co = (square(second, i) for i in range(5))
    ff_part = w_down.shape[0]
    win_t = second[:, 5 * part : 5 * part + ff_part].reshape(-1, model)
    wdown = second[:, 5 * part + ff_part :].reshape(-1, model)
    small_all = first[:, 3 * part].astype(F32)
    gains = [
        small_all[:, i * gain_part : (i + 1) * gain_part].reshape(1, model) for i in range(3)
    ]
    table_part = bias_table.shape[0]
    table = small_all[:, 3 * gain_part : 3 * gain_part + table_part].reshape(NB, H)

    distance = jnp.arange(LANES + 1, dtype=jnp.int32)
    bucket_hot = (bucket_of(distance)[:, None] == jnp.arange(NB, dtype=jnp.int32)[None, :]).astype(
        F32
    )
    by_distance = jnp.dot(bucket_hot, table, precision=lax.Precision.HIGHEST)
    far = by_distance[LANES]
    near = (by_distance - far[None, :])[::-1].T
    near = jnp.pad(near, ((0, 16 - H), (0, 4 * LANES - near.shape[1])))

    q, k, v, o, p, a1 = self_forward(length, x, gains[0], wq, wk, wv, far, near)
    (
        out, g1, a2, mix, a3, r, du, g_low, g2_low, dcq, dck, dcv, egrad, mid_gain_grad,
    ) = middle(
        length, x, o, cot, enc, jnp.concatenate(gains[1:], axis=0),
        wo, cq, ck, cv, co, win_t, wdown,
    )
    split = lambda grad: grad.reshape(dev_count, -1, model)
    g_down = tn(r, g_low).astype(BF16)
    g_in = tn(du, a3).astype(BF16)
    g_cq = tn(a2, dcq).astype(BF16)
    g_co = tn(mix, g2_low).astype(BF16)
    g_ck = tn(enc, dck).astype(BF16)
    g_cv = tn(enc, dcv).astype(BF16)
    pile_one = jnp.concatenate(
        [split(g) for g in (g_cq, g_ck, g_cv, g_co, g_in, g_down)], axis=1
    )
    sum_one = lax.psum_scatter(pile_one, axes, scatter_dimension=0, tiled=False).astype(F32)

    in_grad, g_wq, g_wk, g_wv, g_wo, self_gain_grad, hist = self_backward(
        x, gains[0], a1, g1, q, k, v, o, p, wo, wq, wk, wv
    )
    by_dist = hist[:H, :LANES][:, ::-1]
    by_dist = jnp.concatenate([hist[:H, LANES : LANES + 1], by_dist[:, : LANES - 1]], axis=1)
    near_hot = bucket_hot[:LANES] * (jnp.arange(NB) < NB - 1).astype(F32)
    near_sums = jnp.dot(near_hot.T, by_dist.T, precision=lax.Precision.HIGHEST)
    grad_table = jnp.where(
        (jnp.arange(NB) < NB - 1)[:, None],
        near_sums, -jnp.sum(near_sums, axis=0, keepdims=True),
    )
    small_grads = jnp.concatenate(
        [
            self_gain_grad.reshape(dev_count, -1),
            mid_gain_grad[0].reshape(dev_count, -1),
            mid_gain_grad[1].reshape(dev_count, -1),
            grad_table.reshape(dev_count, -1),
        ],
        axis=1,
    )
    low = small_grads.astype(BF16)
    rest = (small_grads - low.astype(F32)).astype(BF16)
    both = jnp.concatenate([low, rest], axis=1)
    both = jnp.pad(both, ((0, 0), (0, model - both.shape[1])))[:, None, :]
    pile_two = jnp.concatenate(
        [split(g) for g in (g_wq, g_wk, g_wv, g_wo)] + [jnp.pad(both, ((0, 0), (0, 7), (0, 0)))],
        axis=1,
    )
    sum_two = lax.psum_scatter(pile_two, axes, scatter_dimension=0, tiled=False).astype(F32)

    egrad_other = lax.ppermute(egrad, "dp", route)
    encoder_grad = jnp.where(in_place[:, None], egrad, egrad_other)
    rows_of = lambda pile, at: pile[at * part : (at + 1) * part]
    ends = sum_two[4 * part]
    small_count = small_grads.shape[1]
    ends = ends[:small_count] + ends[small_count : 2 * small_count]
    return (
        out[None], in_grad[None], encoder_grad[None],
        rows_of(sum_two, 0), rows_of(sum_two, 1), rows_of(sum_two, 2), rows_of(sum_two, 3),
        rows_of(sum_one, 0), rows_of(sum_one, 1), rows_of(sum_one, 2), rows_of(sum_one, 3),
        sum_one[4 * part : 4 * part + ff_part].T,
        sum_one[4 * part + ff_part :],
        ends[:gain_part], ends[gain_part : 2 * gain_part], ends[2 * gain_part : 3 * gain_part],
        ends[3 * gain_part :],
    )


def solution(mesh):
    rows3 = P(("dp", "fsdp"), None, None)
    rows2 = P(("dp", "fsdp"), None)
    cols2 = P(None, ("dp", "fsdp"))
    line = P(("dp", "fsdp"))
    in_specs = (
        (rows3, rows3, P(), P(), rows3) + (rows2,) * 8 + (cols2, rows2) + (line,) * 4
    )
    out_specs = (rows3,) * 3 + (rows2,) * 8 + (cols2, rows2) + (line,) * 4
    return jax.shard_map(body, mesh=mesh, in_specs=in_specs, out_specs=out_specs, check_vma=False)
```

```python
import functools
import math

import jax
import jax.numpy as jnp
from jax import lax
from jax.experimental import pallas as pl
from jax.experimental.pallas import tpu as pltpu
from jax.sharding import PartitionSpec as P

H = 12
DH = 64
NB = 32
MAXDIST = 128
EPSILON = 1e-06
MASKED = -1e30
LANES = 128
ROWS = 256
F32 = jnp.float32
BF16 = jnp.bfloat16
GELU_C = math.sqrt(2.0 / math.pi)
GELU_A = 0.044715


def bucket_of(distance):
    exact_count = NB // 2
    bucket = jnp.minimum(distance, exact_count)
    for level_idx in range(1, exact_count):
        threshold = int(
            math.ceil(exact_count * (MAXDIST / exact_count) ** (level_idx / exact_count))
        )
        bucket = bucket + (distance >= threshold).astype(jnp.int32)
    return bucket


def nn(left_op, right_op):
    return lax.dot_general(
        left_op, right_op, (((1,), (0,)), ((), ())), preferred_element_type=F32
    )


def nt(left_op, right_op):
    return lax.dot_general(
        left_op, right_op, (((1,), (1,)), ((), ())), preferred_element_type=F32
    )


def tn(left_op, right_op):
    return lax.dot_general(
        left_op, right_op, (((0,), (0,)), ((), ())), preferred_element_type=F32
    )


def unit_rows(values_in):
    inv_rms = lax.rsqrt(jnp.mean(values_in * values_in, axis=-1, keepdims=True) + EPSILON)
    return values_in * inv_rms, inv_rms


def norm_back(grad_in, unit, inv_rms, gain_vec):
    scaled = grad_in * gain_vec
    through = inv_rms * (scaled - unit * jnp.mean(scaled * unit, axis=-1, keepdims=True))
    return through, jnp.sum(grad_in * unit, axis=0, keepdims=True)


def head_lane(shape, which):
    lane = lax.broadcasted_iota(jnp.int32, shape, len(shape) - 1)
    return (lane // DH) == which


def self_forward_kernel(
    length_ref, x_ref, gain_ref, wq_ref, wk_ref, wv_ref, far_ref, near_ref,
    q_ref, k_ref, v_ref, o_ref, p_ref, a_ref, tile_ref,
):
    step = pl.program_id(0)
    seq = x_ref.shape[0]
    width = wq_ref.shape[1]

    @pl.when(step == 0)
    def _():
        unit, _inv = unit_rows(x_ref[...].astype(F32))
        a_ref[...] = (unit * gain_ref[...]).astype(BF16)

    for w_ref, out_ref in ((wq_ref, q_ref), (wk_ref, k_ref), (wv_ref, v_ref)):
        out_ref[...] = nn(a_ref[...], w_ref[...]).astype(BF16)

    key_pos = lax.broadcasted_iota(jnp.int32, (seq, 1), 0)
    key_dead = key_pos >= length_ref[0]
    row = lax.broadcasted_iota(jnp.int32, (ROWS, ROWS + LANES), 0)
    col = lax.broadcasted_iota(jnp.int32, (ROWS, ROWS + LANES), 1)
    ahead = col - LANES > row
    for pair in range(width // LANES):
        cols = slice(pair * LANES, (pair + 1) * LANES)
        outs = [None] * (seq // ROWS)
        for which in range(2):
            local = pair * 2 + which
            head = step * (width // DH) + local
            spun = pltpu.roll(
                jnp.broadcast_to(near_ref[pl.ds(head, 1), :], (ROWS, 4 * LANES)),
                0, 1, stride=1, stride_axis=0,
            )
            tile_ref[...] = jnp.where(ahead, MASKED, spun[:, : ROWS + LANES])
            own = head_lane((seq, LANES), which)
            extra = lax.broadcasted_iota(jnp.int32, (seq, LANES), 1) == (DH if which == 0 else 0)
            far = jnp.where(key_dead, MASKED, far_ref[head]).astype(BF16)
            keys = jnp.where(own, k_ref[:, cols], jnp.where(extra, far, jnp.zeros((), BF16)))
            values = jnp.where(own, v_ref[:, cols], jnp.zeros((), BF16))
            queries = jnp.where(own, q_ref[:, cols], jnp.where(extra, 1.0, 0.0).astype(BF16))
            for blk in range(seq // ROWS):
                rows = slice(blk * ROWS, (blk + 1) * ROWS)
                span = (blk + 1) * ROWS
                cut = max(span - ROWS - LANES, 0)
                scores = nt(queries[rows], keys[:span])
                if cut:
                    near = scores[:, cut:] + tile_ref[...]
                    scores = jnp.concatenate([scores[:, :cut], near], axis=1)
                elif span == ROWS:
                    scores = scores + tile_ref[:, LANES:]
                else:
                    near = scores[:, ROWS - LANES :] + tile_ref[...]
                    scores = jnp.concatenate([scores[:, : ROWS - LANES], near], axis=1)
                top = jnp.max(scores, axis=1, keepdims=True)
                weights = jnp.exp(scores - top)
                total = jnp.sum(weights, axis=1, keepdims=True)
                probs = (weights * (1.0 / total)).astype(BF16)
                p_ref[local, rows, :span] = probs
                mixed = nn(probs, values[:span])
                outs[blk] = mixed if outs[blk] is None else outs[blk] + mixed
        for blk in range(seq // ROWS):
            o_ref[blk * ROWS : (blk + 1) * ROWS, cols] = outs[blk].astype(BF16)


def self_forward(length, x, gain, wq, wk, wv, far, near):
    seq, model = x.shape
    width = 256
    steps = model // width
    whole = lambda shape: pl.BlockSpec(shape, lambda i: (0,) * len(shape))
    smem = pl.BlockSpec(memory_space=pltpu.SMEM)
    columns = pl.BlockSpec((seq, width), lambda i: (0, i))
    weight = pl.BlockSpec((model, width), lambda i: (0, i))
    heads = width // DH
    return pl.pallas_call(
        self_forward_kernel,
        grid=(steps,),
        in_specs=[
            smem, whole((seq, model)), whole((1, model)), weight, weight, weight,
            smem, whole(near.shape),
        ],
        out_specs=[
            columns, columns, columns, columns,
            pl.BlockSpec((heads, seq, seq), lambda i: (i, 0, 0)),
            whole((seq, model)),
        ],
        out_shape=[jax.ShapeDtypeStruct((seq, model), BF16)] * 4
        + [
            jax.ShapeDtypeStruct((H, seq, seq), BF16),
            jax.ShapeDtypeStruct((seq, model), BF16),
        ],
        scratch_shapes=[pltpu.VMEM((ROWS, ROWS + LANES), F32)],
        compiler_params=pltpu.CompilerParams(vmem_limit_bytes=60 * 1024 * 1024),
        cost_estimate=pl.CostEstimate(
            flops=6 * seq * model * model + 4 * seq * seq * model,
            bytes_accessed=2 * H * seq * seq + 16 * seq * model,
            transcendentals=H * seq * seq,
        ),
        name="self_forward",
    )(length, x, gain, wq, wk, wv, far, near)


def middle_kernel(
    length_ref, x_ref, o_ref, cot_ref, enc_ref, gain_ref, wo_ref, cq_ref, ck_ref, cv_ref,
    co_ref, win_ref, wdown_ref,
    out_ref, g1_ref, a2_ref, mix_ref, a3_ref, r_ref, du_ref, g_ref, g2_ref, dcq_ref,
    dck_ref, dcv_ref, egrad_ref, gain_grad_ref,
    keys_ref, values_ref, dk_acc, dv_acc,
):
    step = pl.program_id(0)
    last = pl.num_programs(0) - 1
    rows = x_ref.shape[0]
    model = x_ref.shape[1]
    pairs = model // LANES

    @pl.when(step == 0)
    def _():
        keys_ref[...] = nn(enc_ref[...], ck_ref[...]).astype(BF16)
        values_ref[...] = nn(enc_ref[...], cv_ref[...]).astype(BF16)
        dk_acc[...] = jnp.zeros_like(dk_acc)
        dv_acc[...] = jnp.zeros_like(dv_acc)
        gain_grad_ref[...] = jnp.zeros_like(gain_grad_ref)

    gain_cross = gain_ref[0:1, :]
    gain_ffn = gain_ref[1:2, :]
    pos = step * rows + lax.broadcasted_iota(jnp.int32, (rows, 1), 0)
    valid = jnp.where(pos < length_ref[0], 1.0, 0.0).astype(F32)

    x1 = x_ref[...].astype(F32) + nn(o_ref[...], wo_ref[...])
    unit2, inv2 = unit_rows(x1)
    a2 = (unit2 * gain_cross).astype(BF16)
    a2_ref[...] = a2
    cq = nn(a2, cq_ref[...]).astype(BF16)
    probs = []
    mixed = []
    zero = jnp.zeros((), BF16)
    for pair in range(pairs):
        cols = slice(pair * LANES, (pair + 1) * LANES)
        total_out = None
        for which in range(2):
            own = head_lane((rows, LANES), which)
            own_key = head_lane((keys_ref.shape[0], LANES), which)
            scores = nt(jnp.where(own, cq[:, cols], zero), keys_ref[:, cols])
            top = jnp.max(scores, axis=1, keepdims=True)
            weights = jnp.exp(scores - top)
            prob = weights * (1.0 / jnp.sum(weights, axis=1, keepdims=True))
            probs.append(prob)
            part = nn(prob.astype(BF16), jnp.where(own_key, values_ref[:, cols], zero))
            total_out = part if total_out is None else total_out + part
        mixed.append(total_out.astype(BF16))
    mix = jnp.concatenate(mixed, axis=1)
    mix_ref[...] = mix
    x2 = x1 + nn(mix, co_ref[...])
    unit3, inv3 = unit_rows(x2)
    a3 = (unit3 * gain_ffn).astype(BF16)
    a3_ref[...] = a3
    grad = cot_ref[...].astype(F32) * valid
    grad_low = grad.astype(BF16)
    g_ref[...] = grad_low
    result = x2
    dy3 = None
    hidden_count = win_ref.shape[0]
    chunk = model
    for start in range(0, hidden_count, chunk):
        part = slice(start, start + chunk)
        z = nt(a3, win_ref[part, :])
        zz = z * z
        t = jnp.tanh(GELU_C * z * (1.0 + GELU_A * zz))
        half = 0.5 + 0.5 * t
        r = (z * half).astype(BF16)
        r_ref[:, part] = r
        slope = half + (0.5 * GELU_C) * z * (1.0 - t * t) * (1.0 + (3.0 * GELU_A) * zz)
        du = (nt(grad_low, wdown_ref[part, :]) * slope).astype(BF16)
        du_ref[:, part] = du
        result = result + nn(r, wdown_ref[part, :])
        back = nn(du, win_ref[part, :])
        dy3 = back if dy3 is None else dy3 + back
    out_ref[...] = result * valid
    through, gain_part = norm_back(dy3, unit3, inv3, gain_ffn)
    gain_grad_ref[1:2, :] += gain_part
    g2 = grad + through
    g2_low = g2.astype(BF16)
    g2_ref[...] = g2_low
    dmix = nt(g2_low, co_ref[...]).astype(BF16)
    dq_parts = []
    for pair in range(pairs):
        cols = slice(pair * LANES, (pair + 1) * LANES)
        dq = None
        for which in range(2):
            own = head_lane((rows, LANES), which)
            own_key = head_lane((keys_ref.shape[0], LANES), which)
            prob = probs[2 * pair + which]
            d_out = jnp.where(own, dmix[:, cols], zero)
            dp = nt(d_out, values_ref[:, cols])
            ds = prob * (dp - jnp.sum(prob * dp, axis=1, keepdims=True))
            ds_low = ds.astype(BF16)
            dv_acc[:, cols] += tn(prob.astype(BF16), d_out)
            dk_acc[:, cols] += tn(ds_low, jnp.where(own, cq[:, cols], zero))
            part = nn(ds_low, jnp.where(own_key, keys_ref[:, cols], zero))
            dq = part if dq is None else dq + part
        dq_parts.append(dq.astype(BF16))
    dcq = jnp.concatenate(dq_parts, axis=1)
    dcq_ref[...] = dcq
    through, gain_part = norm_back(nt(dcq, cq_ref[...]), unit2, inv2, gain_cross)
    gain_grad_ref[0:1, :] += gain_part
    g1_ref[...] = g2 + through

    @pl.when(step == last)
    def _():
        dk = dk_acc[...].astype(BF16)
        dv = dv_acc[...].astype(BF16)
        dck_ref[...] = dk
        dcv_ref[...] = dv
        egrad_ref[...] = nt(dk, ck_ref[...]) + nt(dv, cv_ref[...])


def middle(length, x, o, cot, enc, gains, wo, cq, ck, cv, co, win_t, wdown):
    seq, model = x.shape
    hidden = win_t.shape[0]
    enc_len = enc.shape[0]
    steps = seq // ROWS
    whole = lambda shape: pl.BlockSpec(shape, lambda i: (0,) * len(shape))
    held = lambda shape: pl.BlockSpec(
        shape, lambda i: (0,) * len(shape), pipeline_mode=pl.Buffered(1)
    )
    smem = pl.BlockSpec(memory_space=pltpu.SMEM)
    block = lambda width: pl.BlockSpec((ROWS, width), lambda i: (i, 0))
    square = held((model, model))
    wide = held((hidden, model))
    low = lambda width: jax.ShapeDtypeStruct((seq, width), BF16)
    return pl.pallas_call(
        middle_kernel,
        grid=(steps,),
        in_specs=[
            smem, block(model), block(model), block(model), held((enc_len, model)),
            held((2, model)), square, square, square, square, square, wide, wide,
        ],
        out_specs=[
            block(model), block(model), block(model), block(model), block(model),
            block(hidden), block(hidden), block(model), block(model), block(model),
            whole((enc_len, model)), whole((enc_len, model)), whole((enc_len, model)),
            whole((2, model)),
        ],
        out_shape=[
            jax.ShapeDtypeStruct((seq, model), F32),
            jax.ShapeDtypeStruct((seq, model), F32),
            low(model), low(model), low(model), low(hidden), low(hidden),
            low(model), low(model), low(model),
            jax.ShapeDtypeStruct((enc_len, model), BF16),
            jax.ShapeDtypeStruct((enc_len, model), BF16),
            jax.ShapeDtypeStruct((enc_len, model), F32),
            jax.ShapeDtypeStruct((2, model), F32),
        ],
        scratch_shapes=[
            pltpu.VMEM((enc_len, model), BF16),
            pltpu.VMEM((enc_len, model), BF16),
            pltpu.VMEM((enc_len, model), F32),
            pltpu.VMEM((enc_len, model), F32),
        ],
        compiler_params=pltpu.CompilerParams(vmem_limit_bytes=60 * 1024 * 1024),
        cost_estimate=pl.CostEstimate(
            flops=12 * seq * model * model + 8 * seq * model * hidden,
            bytes_accessed=40 * seq * model + 10 * model * model + 4 * hidden * model,
            transcendentals=seq * hidden,
        ),
        name="middle",
    )(length, x, o, cot, enc, gains, wo, cq, ck, cv, co, win_t, wdown)


def self_backward_kernel(
    x_ref, gain_ref, a_ref, g1_ref, q_ref, k_ref, v_ref, o_ref, p_ref,
    wo_ref, wq_ref, wk_ref, wv_ref,
    ingrad_ref, gwq_ref, gwk_ref, gwv_ref, gwo_ref, gain_grad_ref, hist_ref,
    low_ref, dy_acc, near_acc, dk_acc, dv_acc, dq_scr,
):
    step = pl.program_id(0)
    last = pl.num_programs(0) - 1
    seq = x_ref.shape[0]
    width = wq_ref.shape[1]

    @pl.when(step == 0)
    def _():
        low_ref[...] = g1_ref[...].astype(BF16)
        dy_acc[...] = jnp.zeros_like(dy_acc)

    d_all = nt(low_ref[...], wo_ref[...]).astype(BF16)
    gwo_ref[...] = tn(o_ref[...], low_ref[...]).astype(BF16)
    zero = jnp.zeros((), BF16)
    for pair in range(width // LANES):
        cols = slice(pair * LANES, (pair + 1) * LANES)
        dk_acc[...] = jnp.zeros_like(dk_acc)
        dv_acc[...] = jnp.zeros_like(dv_acc)
        dq_blocks = [None] * (seq // ROWS)
        for which in range(2):
            local = pair * 2 + which
            head = step * (width // DH) + local
            own = head_lane((seq, LANES), which)
            d_out = jnp.where(own, d_all[:, cols], zero)
            queries = jnp.where(own, q_ref[:, cols], zero)
            keys = jnp.where(own, k_ref[:, cols], zero)
            for blk in range(seq // ROWS):
                rows = slice(blk * ROWS, (blk + 1) * ROWS)
                span = (blk + 1) * ROWS
                prob_low = p_ref[local, rows, :span]
                prob = prob_low.astype(F32)
                dp = nt(d_out[rows], v_ref[:span, cols])
                ds = prob * (dp - jnp.sum(prob * dp, axis=1, keepdims=True))
                if blk == 0:
                    near_acc[:, :LANES] = jnp.zeros((ROWS, LANES), F32)
                    near_acc[:, LANES:] = ds
                else:
                    near_acc[...] += ds[:, span - ROWS - LANES :]
                ds_low = ds.astype(BF16)
                part = nn(ds_low, keys[:span])
                dq_blocks[blk] = part if which == 0 else dq_blocks[blk] + part
                dk_acc[:span, :] += tn(ds_low, queries[rows])
                dv_acc[:span, :] += tn(prob_low, d_out[rows])
            padded = jnp.concatenate(
                [near_acc[...], jnp.zeros((ROWS, LANES), F32)], axis=1
            )
            count = ROWS
            while count > 1:
                count //= 2
                padded = padded[:count] + pltpu.roll(padded[count:], 4 * LANES - count, 1)
            hist_ref[pl.ds(head, 1), :] = padded
        for blk in range(seq // ROWS):
            rows = slice(blk * ROWS, (blk + 1) * ROWS)
            dq_scr[0, rows, cols] = dq_blocks[blk].astype(BF16)
        dq_scr[1, :, cols] = dk_acc[...].astype(BF16)
        dq_scr[2, :, cols] = dv_acc[...].astype(BF16)
    dy_acc[...] += (
        nt(dq_scr[0], wq_ref[...]) + nt(dq_scr[1], wk_ref[...]) + nt(dq_scr[2], wv_ref[...])
    )
    gwq_ref[...] = tn(a_ref[...], dq_scr[0]).astype(BF16)
    gwk_ref[...] = tn(a_ref[...], dq_scr[1]).astype(BF16)
    gwv_ref[...] = tn(a_ref[...], dq_scr[2]).astype(BF16)

    @pl.when(step == last)
    def _():
        unit, inv = unit_rows(x_ref[...].astype(F32))
        through, gain_part = norm_back(dy_acc[...], unit, inv, gain_ref[...])
        ingrad_ref[...] = g1_ref[...] + through
        gain_grad_ref[...] = gain_part


def self_backward(x, gain, a1, g1, q, k, v, o, p, wo, wq, wk, wv):
    seq, model = x.shape
    width = 256
    heads = width // DH
    steps = model // width
    held = lambda shape: pl.BlockSpec(
        shape, lambda i: (0,) * len(shape), pipeline_mode=pl.Buffered(1)
    )
    whole = lambda shape: pl.BlockSpec(shape, lambda i: (0,) * len(shape))
    columns = pl.BlockSpec((seq, width), lambda i: (0, i))
    weight = pl.BlockSpec((model, width), lambda i: (0, i))
    weight_rows = pl.BlockSpec((width, model), lambda i: (i, 0))
    square = jax.ShapeDtypeStruct((model, model), BF16)
    return pl.pallas_call(
        self_backward_kernel,
        grid=(steps,),
        in_specs=[
            held((seq, model)), held((1, model)), held((seq, model)), held((seq, model)),
            columns, columns, columns, columns,
            pl.BlockSpec((heads, seq, seq), lambda i: (i, 0, 0)),
            weight_rows, weight, weight, weight,
        ],
        out_specs=[
            whole((seq, model)), weight, weight, weight, weight_rows, whole((1, model)),
            whole((16, 4 * LANES)),
        ],
        out_shape=[
            jax.ShapeDtypeStruct((seq, model), F32), square, square, square, square,
            jax.ShapeDtypeStruct((1, model), F32),
            jax.ShapeDtypeStruct((16, 4 * LANES), F32),
        ],
        scratch_shapes=[
            pltpu.VMEM((seq, model), BF16),
            pltpu.VMEM((seq, model), F32),
            pltpu.VMEM((ROWS, ROWS + LANES), F32),
            pltpu.VMEM((seq, LANES), F32),
            pltpu.VMEM((seq, LANES), F32),
            pltpu.VMEM((3, seq, width), BF16),
        ],
        compiler_params=pltpu.CompilerParams(vmem_limit_bytes=60 * 1024 * 1024),
        cost_estimate=pl.CostEstimate(
            flops=16 * seq * model * model + 8 * seq * seq * model,
            bytes_accessed=2 * H * seq * seq + 24 * seq * model,
            transcendentals=0,
        ),
        name="self_backward",
    )(x, gain, a1, g1, q, k, v, o, p, wo, wq, wk, wv)


SIDE_DP = 4
SIDE_FSDP = 8
MESH = pl.DeviceIdType.MESH


def coords():
    along = lax.axis_index("fsdp")
    return lax.axis_index("dp"), along // 4, lax.rem(along // 2, 2), lax.rem(along, 2)


def device(z, y, x, c):
    return (z, y * 4 + x * 2 + c)


def greet_peers():
    z, y, x, c = coords()
    peers = [device(lax.rem(z + k, SIDE_DP), y, x, c) for k in range(1, SIDE_DP)]
    peers += [device(z, y, 1 - x, c), device(z, 1 - y, x, c), device(z, y, x, 1 - c)]
    barrier = pltpu.get_barrier_semaphore()
    for peer in peers:
        pl.semaphore_signal(barrier, inc=1, device_id=peer, device_id_type=MESH)
    pl.semaphore_wait(barrier, len(peers))


class Link:
    def __init__(self, send, recv):
        self.send, self.recv, self.sent = send, recv, []

    def push(self, src, dst, peer):
        slot = len(self.sent)
        copy = pltpu.make_async_remote_copy(
            src_ref=src, dst_ref=dst, send_sem=self.send.at[slot], recv_sem=self.recv.at[slot],
            device_id=peer, device_id_type=MESH,
        )
        copy.start()
        self.sent.append(copy)
        return copy

    def drain(self):
        for copy in self.sent:
            copy.wait_send()


class Piece:
    def __init__(self, link, local, width):
        self.link, self.local = link, local
        self.cols_a, self.cols_b = slice(0, width // 2), slice(width // 2, width)
        z, y, x, c = self.at = coords()
        self.to_y = device(z, 1 - y, x, c)
        self.to_x = device(z, y, 1 - x, c)
        self.to_core = device(z, y, x, 1 - c)
        self.to_z = [device(lax.rem(z + k, SIDE_DP), y, x, c) for k in range(1, SIDE_DP)]


class Gather(Piece):
    SEMS = 13

    def __init__(self, src, out, link, local):
        super().__init__(link, local, src.shape[-1])
        self.src, self.out = src, out

    def same(self, ref, peer):
        return self.link.push(ref, ref, peer)

    def s0(self):
        here = self.out.at[self.at]
        self.one = [self.link.push(self.src, here, peer) for peer in self.to_z]
        self.own = pltpu.make_async_copy(self.src, here, self.local)
        self.own.start()

    def s1(self):
        z, y, x, c = self.at
        self.own.wait()
        for copy in self.one:
            copy.wait_recv()
        out, a, b = self.out, self.cols_a, self.cols_b
        self.two = [
            self.same(out.at[:, y, x, c, :, a], self.to_x),
            self.same(out.at[:, y, x, c, :, b], self.to_y),
        ]
        self.across = [self.same(out.at[:, y, x, c], self.to_core)]

    def s2(self):
        z, y, x, c = self.at
        for copy in self.two:
            copy.wait_recv()
        out, a, b = self.out, self.cols_a, self.cols_b
        self.three = [
            self.same(out.at[:, y, :, c, :, a], self.to_y),
            self.same(out.at[:, :, x, c, :, b], self.to_x),
        ]
        self.across += [
            self.same(out.at[:, y, 1 - x, c, :, a], self.to_core),
            self.same(out.at[:, 1 - y, x, c, :, b], self.to_core),
        ]

    def s3(self):
        z, y, x, c = self.at
        for copy in self.three:
            copy.wait_recv()
        out, a, b = self.out, self.cols_a, self.cols_b
        self.across += [
            self.same(out.at[:, 1 - y, :, c, :, a], self.to_core),
            self.same(out.at[:, :, 1 - x, c, :, b], self.to_core),
        ]

    def s4(self):
        for copy in self.across:
            copy.wait_recv()


class Reduce(Piece):
    SEMS = 8
    BUFFERS = 7

    def __init__(self, src, out, own, held, l1a, l1b, l2a, l2b, l3, link, local):
        super().__init__(link, local, src.shape[-1])
        self.src, self.out, self.own, self.held = src, out, own, held
        self.l1a, self.l1b, self.l2a, self.l2b, self.l3 = l1a, l1b, l2a, l2b, l3

    @staticmethod
    def scratch(rows, width):
        buffer = lambda *lead, cols=width: pltpu.VMEM(lead + (rows, cols), BF16)
        half = width // 2
        return [
            buffer(SIDE_DP, 2, 2), buffer(SIDE_DP, 2, 2),
            buffer(SIDE_DP, 2, cols=half), buffer(SIDE_DP, 2, cols=half),
            buffer(SIDE_DP, cols=half), buffer(SIDE_DP, cols=half), buffer(SIDE_DP - 1),
        ]

    def s0(self):
        z, y, x, c = self.at
        self.one = self.link.push(self.src.at[:, :, :, 1 - c], self.held, self.to_core)
        self.mine = pltpu.make_async_copy(self.src.at[:, :, :, c], self.own, self.local)
        self.mine.start()

    def s1(self):
        z, y, x, c = self.at
        self.mine.wait()
        self.one.wait_recv()
        held, a, b = self.held, self.cols_a, self.cols_b
        held[...] = held[...] + self.own[...]
        self.two = [
            self.link.push(held.at[:, 1 - y, :, :, a], self.l1a, self.to_y),
            self.link.push(held.at[:, :, 1 - x, :, b], self.l1b, self.to_x),
        ]

    def s2(self):
        z, y, x, c = self.at
        for copy in self.two:
            copy.wait_recv()
        held, a, b = self.held, self.cols_a, self.cols_b
        held[:, y, :, :, a] = held[:, y, :, :, a] + self.l1a[...]
        held[:, :, x, :, b] = held[:, :, x, :, b] + self.l1b[...]
        self.three = [
            self.link.push(held.at[:, y, 1 - x, :, a], self.l2a, self.to_x),
            self.link.push(held.at[:, 1 - y, x, :, b], self.l2b, self.to_y),
        ]

    def s3(self):
        z, y, x, c = self.at
        for copy in self.three:
            copy.wait_recv()
        held, a, b = self.held, self.cols_a, self.cols_b
        held[:, y, x, :, a] = held[:, y, x, :, a] + self.l2a[...]
        held[:, y, x, :, b] = held[:, y, x, :, b] + self.l2b[...]
        self.four = [
            self.link.push(held.at[lax.rem(z + k, SIDE_DP), y, x], self.l3.at[k - 1], peer)
            for k, peer in zip(range(1, SIDE_DP), self.to_z)
        ]

    def s4(self):
        z, y, x, c = self.at
        for copy in self.four:
            copy.wait_recv()
        total = self.held[z, y, x].astype(F32)
        for k in range(SIDE_DP - 1):
            total = total + self.l3[k].astype(F32)
        self.out[...] = total


def run_stages(pieces, lags):
    order = sorted(
        (i + lag, -k, i) for i in range(len(pieces)) for k, lag in enumerate(lags)
    )
    for _time, k, i in order:
        getattr(pieces[i], ("s0", "s1", "s2", "s3", "s4")[-k])()


def gather_kernel(cuts, lags, count, *refs):
    ins, outs = refs[:count], refs[count : 2 * count]
    send, recv, local = refs[2 * count :]
    greet_peers()
    link = Link(send, recv)
    pieces = [
        Gather(ins[w].at[lo:hi], outs[w].at[:, :, :, :, lo:hi], link, local.at[i])
        for i, (w, lo, hi) in enumerate(cuts)
    ]
    run_stages(pieces, lags)
    link.drain()


def gather_all(shards, cuts, lags):
    count = len(shards)
    sems = len(cuts) * Gather.SEMS
    outs = pl.pallas_call(
        functools.partial(gather_kernel, cuts, lags, count),
        out_shape=[
            jax.ShapeDtypeStruct((SIDE_DP, 2, 2, 2) + s.shape, s.dtype) for s in shards
        ],
        in_specs=[pl.BlockSpec(memory_space=pl.ANY)] * count,
        out_specs=[pl.BlockSpec(memory_space=pl.ANY)] * count,
        scratch_shapes=[
            pltpu.SemaphoreType.DMA((sems,)), pltpu.SemaphoreType.DMA((sems,)),
            pltpu.SemaphoreType.DMA((len(cuts),)),
        ],
        compiler_params=pltpu.CompilerParams(
            collective_id=1, has_side_effects=True, vmem_limit_bytes=56 * 1024 * 1024
        ),
        name="gather_all",
    )(*shards)
    return [o.reshape(-1, o.shape[-1]) for o in outs]


def reduce_kernel(cuts, lags, count, *refs):
    ins, outs, rest = refs[:count], refs[count : 2 * count], refs[2 * count :]
    send, recv, local = rest[Reduce.BUFFERS * len(cuts) :]
    greet_peers()
    link = Link(send, recv)
    pieces = [
        Reduce(
            ins[w].at[:, :, :, :, lo:hi], outs[w].at[lo:hi],
            *rest[Reduce.BUFFERS * i : Reduce.BUFFERS * (i + 1)], link, local.at[i],
        )
        for i, (w, lo, hi) in enumerate(cuts)
    ]
    run_stages(pieces, lags)
    link.drain()


def reduce_all(grads, cuts, lags):
    count = len(grads)
    width = grads[0].shape[-1]
    sems = len(cuts) * Reduce.SEMS
    grads = [g.reshape(SIDE_DP, 2, 2, 2, -1, width) for g in grads]
    scratch = []
    for _w, lo, hi in cuts:
        scratch += Reduce.scratch(hi - lo, width)
    return pl.pallas_call(
        functools.partial(reduce_kernel, cuts, lags, count),
        out_shape=[jax.ShapeDtypeStruct(g.shape[4:], F32) for g in grads],
        in_specs=[pl.BlockSpec(memory_space=pl.ANY)] * count,
        out_specs=[pl.BlockSpec(memory_space=pltpu.VMEM)] * count,
        scratch_shapes=scratch
        + [
            pltpu.SemaphoreType.DMA((sems,)), pltpu.SemaphoreType.DMA((sems,)),
            pltpu.SemaphoreType.DMA((len(cuts),)),
        ],
        compiler_params=pltpu.CompilerParams(
            collective_id=2, has_side_effects=True, vmem_limit_bytes=60 * 1024 * 1024
        ),
        name="reduce_all",
    )(*grads)


def gather_weights(shards, axes):
    if lax.axis_size("dp") == SIDE_DP and lax.axis_size("fsdp") == SIDE_FSDP:
        cuts = []
        for w, shard in enumerate(shards):
            step = min(shard.shape[0], 24)
            cuts += [(w, lo, lo + step) for lo in range(0, shard.shape[0], step)]
        return gather_all(shards, cuts, (0, 2, 4, 6, 8))
    pile = lax.all_gather(jnp.concatenate(shards, axis=0), axes, axis=0)
    full, at = [], 0
    for shard in shards:
        full.append(pile[:, at : at + shard.shape[0]].reshape(-1, pile.shape[-1]))
        at += shard.shape[0]
    return full


def reduce_grads(grads, axes):
    dev_count = lax.axis_size("dp") * lax.axis_size("fsdp")
    if lax.axis_size("dp") == SIDE_DP and lax.axis_size("fsdp") == SIDE_FSDP:
        cuts = []
        for w, grad in enumerate(grads):
            rows = grad.shape[0] // dev_count
            step = min(rows, 48)
            cuts += [(w, lo, lo + step) for lo in range(0, rows, step)]
        return reduce_all(grads, cuts, (0, 1, 3, 5, 7))
    split = [g.reshape(dev_count, -1, g.shape[-1]) for g in grads]
    pile = lax.psum_scatter(
        jnp.concatenate(split, axis=1), axes, scatter_dimension=0, tiled=False
    ).astype(F32)
    sums, at = [], 0
    for s in split:
        sums.append(pile[at : at + s.shape[1]])
        at += s.shape[1]
    return sums


def body(
    tokens, encoder_states, lengths, dealing, cotangent,
    w_query, w_key, w_value, w_out, c_query, c_key, c_value, c_out, w_in, w_down,
    gain_self, gain_cross, gain_ffn, bias_table,
):
    axes = ("dp", "fsdp")
    fsdp_size = lax.axis_size("fsdp")
    dp_size = lax.axis_size("dp")
    dev_count = dp_size * fsdp_size
    dp_index = lax.axis_index("dp")
    own = dp_index * fsdp_size + lax.axis_index("fsdp")
    seq_len, model = tokens.shape[1:]
    route = [(a, a ^ 1) for a in range(dp_size)]

    x = tokens[0]
    cot = cotangent[0]
    in_place = lax.dynamic_slice_in_dim(dealing, own, 1) == own
    enc_other = lax.ppermute(encoder_states[0], "dp", route)
    enc = jnp.where(in_place[:, None], encoder_states[0], enc_other)
    length = lax.dynamic_slice_in_dim(lengths, own, 1)

    gain_part = gain_self.shape[0]
    small = jnp.concatenate([gain_self, gain_cross, gain_ffn, bias_table])
    small_row = jnp.pad(small, (0, model - small.shape[0]))[None, :]
    small_row = jnp.pad(small_row, ((0, 7), (0, 0)))
    wq, wk, wv, small_all, wo, cq, ck, cv, co, win_t, wdown = gather_weights(
        [
            w_query, w_key, w_value, small_row, w_out, c_query, c_key, c_value, c_out,
            w_in.T, w_down,
        ],
        axes,
    )
    small_all = small_all.reshape(dev_count, 8, model)[:, 0].astype(F32)
    gains = [
        small_all[:, i * gain_part : (i + 1) * gain_part].reshape(1, model) for i in range(3)
    ]
    table_part = bias_table.shape[0]
    table = small_all[:, 3 * gain_part : 3 * gain_part + table_part].reshape(NB, H)

    distance = jnp.arange(LANES + 1, dtype=jnp.int32)
    bucket_hot = (bucket_of(distance)[:, None] == jnp.arange(NB, dtype=jnp.int32)[None, :]).astype(
        F32
    )
    by_distance = jnp.dot(bucket_hot, table, precision=lax.Precision.HIGHEST)
    far = by_distance[LANES]
    near = (by_distance - far[None, :])[::-1].T
    near = jnp.pad(near, ((0, 16 - H), (0, 4 * LANES - near.shape[1])))

    q, k, v, o, p, a1 = self_forward(length, x, gains[0], wq, wk, wv, far, near)
    (
        out, g1, a2, mix, a3, r, du, g_low, g2_low, dcq, dck, dcv, egrad, mid_gain_grad,
    ) = middle(
        length, x, o, cot, enc, jnp.concatenate(gains[1:], axis=0),
        wo, cq, ck, cv, co, win_t, wdown,
    )
    g_down = tn(r, g_low).astype(BF16)
    g_in = tn(du, a3).astype(BF16)
    g_cq = tn(a2, dcq).astype(BF16)
    g_co = tn(mix, g2_low).astype(BF16)
    g_ck = tn(enc, dck).astype(BF16)
    g_cv = tn(enc, dcv).astype(BF16)

    in_grad, g_wq, g_wk, g_wv, g_wo, self_gain_grad, hist = self_backward(
        x, gains[0], a1, g1, q, k, v, o, p, wo, wq, wk, wv
    )
    by_dist = hist[:H, :LANES][:, ::-1]
    by_dist = jnp.concatenate([hist[:H, LANES : LANES + 1], by_dist[:, : LANES - 1]], axis=1)
    near_hot = bucket_hot[:LANES] * (jnp.arange(NB) < NB - 1).astype(F32)
    near_sums = jnp.dot(near_hot.T, by_dist.T, precision=lax.Precision.HIGHEST)
    grad_table = jnp.where(
        (jnp.arange(NB) < NB - 1)[:, None],
        near_sums, -jnp.sum(near_sums, axis=0, keepdims=True),
    )
    small_grads = jnp.concatenate(
        [
            self_gain_grad.reshape(dev_count, -1),
            mid_gain_grad[0].reshape(dev_count, -1),
            mid_gain_grad[1].reshape(dev_count, -1),
            grad_table.reshape(dev_count, -1),
        ],
        axis=1,
    )
    small_count = small_grads.shape[1]
    small_low = jnp.pad(small_grads.astype(BF16), ((0, 0), (0, model - small_count)))
    small_low = jnp.pad(small_low[:, None, :], ((0, 0), (0, 7), (0, 0))).reshape(-1, model)
    (
        sum_in, sum_down, sum_cq, sum_ck, sum_cv, sum_co, sum_wq, sum_wk, sum_wv, sum_wo,
        sum_small,
    ) = reduce_grads(
        [g_in, g_down, g_cq, g_ck, g_cv, g_co, g_wq, g_wk, g_wv, g_wo, small_low], axes
    )

    egrad_other = lax.ppermute(egrad, "dp", route)
    encoder_grad = jnp.where(in_place[:, None], egrad, egrad_other)
    ends = sum_small[0]
    return (
        out[None], in_grad[None], encoder_grad[None],
        sum_wq, sum_wk, sum_wv, sum_wo, sum_cq, sum_ck, sum_cv, sum_co, sum_in.T, sum_down,
        ends[:gain_part], ends[gain_part : 2 * gain_part], ends[2 * gain_part : 3 * gain_part],
        ends[3 * gain_part : small_count],
    )


def solution(mesh):
    rows3 = P(("dp", "fsdp"), None, None)
    rows2 = P(("dp", "fsdp"), None)
    cols2 = P(None, ("dp", "fsdp"))
    line = P(("dp", "fsdp"))
    in_specs = (
        (rows3, rows3, P(), P(), rows3) + (rows2,) * 8 + (cols2, rows2) + (line,) * 4
    )
    out_specs = (rows3,) * 3 + (rows2,) * 8 + (cols2, rows2) + (line,) * 4
    return jax.shard_map(body, mesh=mesh, in_specs=in_specs, out_specs=out_specs, check_vma=False)
```

```python
import functools
import math

import jax
import jax.numpy as jnp
from jax import lax
from jax.experimental import pallas as pl
from jax.experimental.pallas import tpu as pltpu
from jax.sharding import PartitionSpec as P

H = 12
DH = 64
NB = 32
MAXDIST = 128
EPSILON = 1e-06
MASKED = -1e30
LANES = 128
ROWS = 256
F32 = jnp.float32
BF16 = jnp.bfloat16
GELU_C = math.sqrt(2.0 / math.pi)
GELU_A = 0.044715


def bucket_of(distance):
    exact_count = NB // 2
    bucket = jnp.minimum(distance, exact_count)
    for level_idx in range(1, exact_count):
        threshold = int(
            math.ceil(exact_count * (MAXDIST / exact_count) ** (level_idx / exact_count))
        )
        bucket = bucket + (distance >= threshold).astype(jnp.int32)
    return bucket


def nn(left_op, right_op):
    return lax.dot_general(
        left_op, right_op, (((1,), (0,)), ((), ())), preferred_element_type=F32
    )


def nt(left_op, right_op):
    return lax.dot_general(
        left_op, right_op, (((1,), (1,)), ((), ())), preferred_element_type=F32
    )


def tn(left_op, right_op):
    return lax.dot_general(
        left_op, right_op, (((0,), (0,)), ((), ())), preferred_element_type=F32
    )


def unit_rows(values_in):
    inv_rms = lax.rsqrt(jnp.mean(values_in * values_in, axis=-1, keepdims=True) + EPSILON)
    return values_in * inv_rms, inv_rms


def norm_back(grad_in, unit, inv_rms, gain_vec):
    scaled = grad_in * gain_vec
    through = inv_rms * (scaled - unit * jnp.mean(scaled * unit, axis=-1, keepdims=True))
    return through, jnp.sum(grad_in * unit, axis=0, keepdims=True)


def head_lane(shape, which):
    lane = lax.broadcasted_iota(jnp.int32, shape, len(shape) - 1)
    return (lane // DH) == which


def self_forward_kernel(
    length_ref, x_ref, gain_ref, wq_ref, wk_ref, wv_ref, far_ref, near_ref,
    q_ref, k_ref, v_ref, o_ref, p_ref, a_ref, tile_ref,
):
    step = pl.program_id(0)
    seq = x_ref.shape[0]
    width = wq_ref.shape[1]

    @pl.when(step == 0)
    def _():
        unit, _inv = unit_rows(x_ref[...].astype(F32))
        a_ref[...] = (unit * gain_ref[...]).astype(BF16)

    for w_ref, out_ref in ((wq_ref, q_ref), (wk_ref, k_ref), (wv_ref, v_ref)):
        out_ref[...] = nn(a_ref[...], w_ref[...]).astype(BF16)

    key_pos = lax.broadcasted_iota(jnp.int32, (seq, 1), 0)
    key_dead = key_pos >= length_ref[0]
    row = lax.broadcasted_iota(jnp.int32, (ROWS, ROWS + LANES), 0)
    col = lax.broadcasted_iota(jnp.int32, (ROWS, ROWS + LANES), 1)
    ahead = col - LANES > row
    for pair in range(width // LANES):
        cols = slice(pair * LANES, (pair + 1) * LANES)
        outs = [None] * (seq // ROWS)
        for which in range(2):
            local = pair * 2 + which
            head = step * (width // DH) + local
            spun = pltpu.roll(
                jnp.broadcast_to(near_ref[pl.ds(head, 1), :], (ROWS, 4 * LANES)),
                0, 1, stride=1, stride_axis=0,
            )
            tile_ref[...] = jnp.where(ahead, MASKED, spun[:, : ROWS + LANES])
            own = head_lane((seq, LANES), which)
            extra = lax.broadcasted_iota(jnp.int32, (seq, LANES), 1) == (DH if which == 0 else 0)
            far = jnp.where(key_dead, MASKED, far_ref[head]).astype(BF16)
            keys = jnp.where(own, k_ref[:, cols], jnp.where(extra, far, jnp.zeros((), BF16)))
            values = jnp.where(own, v_ref[:, cols], jnp.zeros((), BF16))
            queries = jnp.where(own, q_ref[:, cols], jnp.where(extra, 1.0, 0.0).astype(BF16))
            for blk in range(seq // ROWS):
                rows = slice(blk * ROWS, (blk + 1) * ROWS)
                span = (blk + 1) * ROWS
                cut = max(span - ROWS - LANES, 0)
                scores = nt(queries[rows], keys[:span])
                if cut:
                    near = scores[:, cut:] + tile_ref[...]
                    scores = jnp.concatenate([scores[:, :cut], near], axis=1)
                elif span == ROWS:
                    scores = scores + tile_ref[:, LANES:]
                else:
                    near = scores[:, ROWS - LANES :] + tile_ref[...]
                    scores = jnp.concatenate([scores[:, : ROWS - LANES], near], axis=1)
                top = jnp.max(scores, axis=1, keepdims=True)
                weights = jnp.exp(scores - top)
                total = jnp.sum(weights, axis=1, keepdims=True)
                probs = (weights * (1.0 / total)).astype(BF16)
                p_ref[local, rows, :span] = probs
                mixed = nn(probs, values[:span])
                outs[blk] = mixed if outs[blk] is None else outs[blk] + mixed
        for blk in range(seq // ROWS):
            o_ref[blk * ROWS : (blk + 1) * ROWS, cols] = outs[blk].astype(BF16)


def self_forward(length, x, gain, wq, wk, wv, far, near):
    seq, model = x.shape
    width = 256
    steps = model // width
    whole = lambda shape: pl.BlockSpec(shape, lambda i: (0,) * len(shape))
    smem = pl.BlockSpec(memory_space=pltpu.SMEM)
    columns = pl.BlockSpec((seq, width), lambda i: (0, i))
    weight = pl.BlockSpec((model, width), lambda i: (0, i))
    heads = width // DH
    return pl.pallas_call(
        self_forward_kernel,
        grid=(steps,),
        in_specs=[
            smem, whole((seq, model)), whole((1, model)), weight, weight, weight,
            smem, whole(near.shape),
        ],
        out_specs=[
            columns, columns, columns, columns,
            pl.BlockSpec((heads, seq, seq), lambda i: (i, 0, 0)),
            whole((seq, model)),
        ],
        out_shape=[jax.ShapeDtypeStruct((seq, model), BF16)] * 4
        + [
            jax.ShapeDtypeStruct((H, seq, seq), BF16),
            jax.ShapeDtypeStruct((seq, model), BF16),
        ],
        scratch_shapes=[pltpu.VMEM((ROWS, ROWS + LANES), F32)],
        compiler_params=pltpu.CompilerParams(vmem_limit_bytes=60 * 1024 * 1024),
        cost_estimate=pl.CostEstimate(
            flops=6 * seq * model * model + 4 * seq * seq * model,
            bytes_accessed=2 * H * seq * seq + 16 * seq * model,
            transcendentals=H * seq * seq,
        ),
        name="self_forward",
    )(length, x, gain, wq, wk, wv, far, near)


SIDE_DP = 4
SIDE_FSDP = 8
MESH = pl.DeviceIdType.MESH


def coords():
    along = lax.axis_index("fsdp")
    return lax.axis_index("dp"), along // 4, lax.rem(along // 2, 2), lax.rem(along, 2)


def device(z, y, x, c):
    return (z, y * 4 + x * 2 + c)


def greet_peers():
    z, y, x, c = coords()
    peers = [device(lax.rem(z + k, SIDE_DP), y, x, c) for k in range(1, SIDE_DP)]
    peers += [device(z, y, 1 - x, c), device(z, 1 - y, x, c), device(z, y, x, 1 - c)]
    barrier = pltpu.get_barrier_semaphore()
    for peer in peers:
        pl.semaphore_signal(barrier, inc=1, device_id=peer, device_id_type=MESH)
    pl.semaphore_wait(barrier, len(peers))


class Link:
    def __init__(self, send, recv):
        self.send, self.recv, self.used, self.pieces = send, recv, 0, []

    def take(self, piece):
        self.pieces.append(piece)
        self.used += piece.SEMS
        return self.used - piece.SEMS

    def drain(self):
        for piece in self.pieces:
            piece.drain()


class Place:
    def __init__(self):
        z, y, x, c = self.at = coords()
        self.to_y = device(z, 1 - y, x, c)
        self.to_x = device(z, y, 1 - x, c)
        self.to_core = device(z, y, x, 1 - c)
        self.other_z = [lax.rem(z + k, SIDE_DP) for k in range(1, SIDE_DP)]
        self.to_z = [device(other, y, x, c) for other in self.other_z]
        self.ny, self.nx, self.nc = 1 - y, 1 - x, 1 - c


class Piece:
    def __init__(self, link, local, place=None, first=None):
        self.link, self.local = link, local
        self.first = link.take(self) if first is None else first
        self.half_a, self.half_b = slice(0, SIDE_DP // 2), slice(SIDE_DP // 2, SIDE_DP)
        place = place or Place()
        self.at, self.to_y, self.to_x, self.to_core = (
            place.at, place.to_y, place.to_x, place.to_core
        )
        self.other_z, self.to_z = place.other_z, place.to_z
        self.ny, self.nx, self.nc = place.ny, place.nx, place.nc

    def copy(self, slot, src, dst, peer):
        return pltpu.make_async_remote_copy(
            src_ref=src, dst_ref=dst, send_sem=self.link.send.at[self.first + slot],
            recv_sem=self.link.recv.at[self.first + slot], device_id=peer, device_id_type=MESH,
        )

    def start(self, k):
        for copy in self.moves(k):
            copy.start()

    def arrive(self, k):
        for copy in self.moves(k):
            copy.wait_recv()

    def sent(self, k):
        for copy in self.moves(k):
            copy.wait_send()

    def drain(self):
        for k in self.UNSENT:
            self.sent(k)

    def stage(self, k):
        (self.s0, self.s1, self.s2, self.s3, self.s4)[k]()


class Gather(Piece):
    SEMS = 13
    UNSENT = (0, 1, 2, 3, 4, 5)

    def __init__(self, src, out, link, local, place=None, first=None):
        super().__init__(link, local, place, first)
        self.src, self.out = src, out

    def moves(self, k):
        z, y, x, c = self.at
        out, a, b = self.out, self.half_a, self.half_b
        if k == 0:
            here = out.at[z, y, x, c]
            return [self.copy(i, self.src, here, peer) for i, peer in enumerate(self.to_z)]
        same = lambda slot, ref, peer: self.copy(slot, ref, ref, peer)
        if k == 1:
            return [
                same(3, out.at[a, y, x, c], self.to_x),
                same(4, out.at[b, y, x, c], self.to_y),
            ]
        if k == 2:
            return [
                same(5, out.at[a, y, :, c], self.to_y),
                same(6, out.at[b, :, x, c], self.to_x),
            ]
        if k == 3:
            return [same(7, out.at[:, y, x, c], self.to_core)]
        if k == 4:
            return [
                same(8, out.at[a, y, self.nx, c], self.to_core),
                same(9, out.at[b, self.ny, x, c], self.to_core),
            ]
        return [
            same(10, out.at[a, self.ny, :, c], self.to_core),
            same(11, out.at[b, :, self.nx, c], self.to_core),
        ]

    def keep(self):
        return pltpu.make_async_copy(self.src, self.out.at[self.at], self.local)

    def s0(self):
        self.start(0)
        self.keep().start()

    def s1(self):
        self.keep().wait()
        self.arrive(0)
        self.start(1)
        self.start(3)

    def s2(self):
        self.arrive(1)
        self.start(2)
        self.start(4)

    def s3(self):
        self.arrive(2)
        self.start(5)

    def s4(self):
        for k in (3, 4, 5):
            self.arrive(k)


class Reduce(Piece):
    SEMS = 8
    BUFFERS = 6

    def __init__(
        self, src, out, own, held, l1a, l1b, l2a, l2b, l3, link, local, place=None, first=None,
        early=False,
    ):
        super().__init__(link, local, place, first)
        self.src, self.out, self.own, self.held = src, out, own, held
        self.l1a, self.l1b, self.l2a, self.l2b, self.l3 = l1a, l1b, l2a, l2b, l3
        self.UNSENT = (1, 2, 3) if early else (0, 1, 2, 3)

    @staticmethod
    def scratch(rows, width):
        buffer = lambda *lead: pltpu.VMEM(lead + (rows, width), BF16)
        half = SIDE_DP // 2
        return [
            buffer(SIDE_DP, 2, 2), buffer(half, 2), buffer(half, 2), buffer(half), buffer(half),
            buffer(SIDE_DP - 1),
        ]

    def moves(self, k):
        z, y, x, c = self.at
        held, a, b = self.held, self.half_a, self.half_b
        if k == 0:
            return [self.copy(0, self.src.at[:, :, :, self.nc], held, self.to_core)]
        if k == 1:
            return [
                self.copy(1, held.at[a, self.ny], self.l1a, self.to_y),
                self.copy(2, held.at[b, :, self.nx], self.l1b, self.to_x),
            ]
        if k == 2:
            return [
                self.copy(3, held.at[a, y, self.nx], self.l2a, self.to_x),
                self.copy(4, held.at[b, self.ny, x], self.l2b, self.to_y),
            ]
        return [
            self.copy(5 + i, held.at[other, y, x], self.l3.at[i], peer)
            for i, (other, peer) in enumerate(zip(self.other_z, self.to_z))
        ]

    def keep(self):
        return pltpu.make_async_copy(self.src.at[:, :, :, self.at[3]], self.own, self.local)

    def s0(self):
        self.start(0)
        if self.own is not None:
            self.keep().start()

    def s1(self):
        held = self.held
        if self.own is not None:
            self.keep().wait()
            self.arrive(0)
            held[...] = held[...] + self.own[...]
        else:
            self.arrive(0)
            held[...] = held[...] + self.src[:, :, :, self.at[3]]
        self.start(1)

    def s2(self):
        z, y, x, c = self.at
        self.arrive(1)
        held, a, b = self.held, self.half_a, self.half_b
        held[a, y] = held[a, y] + self.l1a[...]
        held[b, :, x] = held[b, :, x] + self.l1b[...]
        self.start(2)

    def s3(self):
        z, y, x, c = self.at
        self.arrive(2)
        held, a, b = self.held, self.half_a, self.half_b
        held[a, y, x] = held[a, y, x] + self.l2a[...]
        held[b, y, x] = held[b, y, x] + self.l2b[...]
        self.start(3)

    def s4(self):
        z, y, x, c = self.at
        self.arrive(3)
        total = self.held[z, y, x].astype(F32)
        for k in range(SIDE_DP - 1):
            total = total + self.l3[k].astype(F32)
        self.out[...] = total


class SumSmall(Piece):
    SEMS = 6
    UNSENT = ()

    def __init__(self, total, near, far, link):
        super().__init__(link, None)
        self.total, self.near, self.far = total, near, far

    def moves(self, k):
        if k < 3:
            peer = (self.to_core, self.to_y, self.to_x)[k]
            return [self.copy(k, self.total, self.near.at[k], peer)]
        return [
            self.copy(3 + i, self.total, self.far.at[i], peer) for i, peer in enumerate(self.to_z)
        ]

    def add(self, k):
        self.arrive(k)
        self.sent(k)
        if k < 3:
            self.total[...] = self.total[...] + self.near[k]
        else:
            total = self.total[...]
            for i in range(SIDE_DP - 1):
                total = total + self.far[i]
            self.total[...] = total

    def s0(self):
        self.start(0)

    def s1(self):
        self.add(0)
        self.start(1)

    def s2(self):
        self.add(1)
        self.start(2)

    def s3(self):
        self.add(2)
        self.start(3)

    def s4(self):
        self.add(3)


CHUNKS = 3


def middle_kernel(joined, length_ref, gain_ref, *refs):
    (x_hbm, o_hbm, cot_hbm, enc_hbm, wo_hbm, cq_hbm, ck_hbm, cv_hbm, co_hbm), refs = (
        refs[:9], refs[9:]
    )
    wide_hbm, refs = refs[0], refs[1:]
    (out_hbm, g1_hbm, egrad_ref, gain_grad_ref), refs = refs[:4], refs[4:]
    squares, refs = refs[:5], refs[5:]
    sum_ref, refs = refs[0], refs[1:]
    (
        xr_ref, o_ref, g_ref, a2_ref, cq_scr, mix_ref, a3_ref, r_ref, du_ref, prob_ref,
        x1_ref, x2_ref, acc_ref, dy_ref, enc_ref, keys_ref, values_ref, dk_acc, dv_acc,
        wo_ref, cq_ref, ck_ref, cv_ref, co_ref, wide_ref, src_ref, load_sem, wide_sem, out_sem,
    ), refs = refs[:29], refs[29:]
    seq, model = xr_ref.shape
    blocks = seq // ROWS
    pairs = model // LANES
    zero = jnp.zeros((), BF16)
    gain_cross = gain_ref[0:1, :]
    gain_ffn = gain_ref[1:2, :]

    loads = [
        pltpu.make_async_copy(src, dst, load_sem.at[i])
        for i, (src, dst) in enumerate(
            (
                (enc_hbm, enc_ref), (ck_hbm, ck_ref), (cv_hbm, cv_ref), (o_hbm, o_ref),
                (wo_hbm, wo_ref), (x_hbm, xr_ref), (cq_hbm, cq_ref), (cot_hbm, g_ref),
                (co_hbm, co_ref),
            )
        )
    ]
    for copy in loads:
        copy.start()

    chunk_rows = wide_ref.shape[2]

    def wide_loads(k):
        slot = lax.rem(k, 2)
        found = []
        for m in range(2):
            dst = wide_ref.at[slot, m]
            if joined:
                part = chunk_rows // (SIDE_DP * SIDE_FSDP)
                at = pl.multiple_of(m * part * CHUNKS + k * part, 8)
                src = wide_hbm.at[:, pl.ds(at, part), :]
                dst = dst.reshape(SIDE_DP * SIDE_FSDP, part, model)
            else:
                src = wide_hbm.at[m, k]
            found.append(pltpu.make_async_copy(src, dst, wide_sem.at[slot, m]))
        return found

    if joined:
        held, l1a, l1b, l2a, l2b, l3, rsend, rrecv = refs
        reduce_link = Link(rsend, rrecv)
        place = Place()
        part = chunk_rows // (SIDE_DP * SIDE_FSDP)

        def leaving(k):
            at = pl.multiple_of(k * part, 8)
            found = []
            for m in range(2):
                i = 2 * k + m
                found.append(
                    Reduce(
                        src_ref.at[m], sum_ref.at[m, pl.ds(at, part)], None, held.at[i],
                        l1a.at[i], l1b.at[i], l2a.at[i], l2b.at[i], l3.at[i], reduce_link, None,
                        place, i * Reduce.SEMS,
                    )
                )
            return found

    def reduce_stage(k, stage, when=None):
        if not joined:
            return

        def go():
            for piece in leaving(k):
                piece.stage(stage)

        go() if when is None else pl.when(when)(go)

    if joined:
        greet_peers()
    for copy in wide_loads(0):
        copy.start()

    for copy in loads[:3]:
        copy.wait()
    keys_ref[...] = nn(enc_ref[...], ck_ref[...]).astype(BF16)
    values_ref[...] = nn(enc_ref[...], cv_ref[...]).astype(BF16)
    dk_acc[...] = jnp.zeros_like(dk_acc)
    dv_acc[...] = jnp.zeros_like(dv_acc)
    gain_grad_ref[...] = jnp.zeros_like(gain_grad_ref)
    for copy in loads[3:]:
        copy.wait()

    def forward_rows(i, _):
        rows = pl.ds(pl.multiple_of(i * ROWS, ROWS), ROWS)
        pos = i * ROWS + lax.broadcasted_iota(jnp.int32, (ROWS, 1), 0)
        valid = jnp.where(pos < length_ref[0], 1.0, 0.0).astype(F32)
        x1 = xr_ref[rows, :].astype(F32) + nn(o_ref[rows, :], wo_ref[...])
        x1_ref[rows, :] = x1
        unit2, _inv2 = unit_rows(x1)
        a2 = (unit2 * gain_cross).astype(BF16)
        a2_ref[rows, :] = a2
        cq = nn(a2, cq_ref[...]).astype(BF16)
        cq_scr[rows, :] = cq
        mixed = []
        for pair in range(pairs):
            cols = slice(pair * LANES, (pair + 1) * LANES)
            total_out = None
            for which in range(2):
                own = head_lane((ROWS, LANES), which)
                own_key = head_lane((keys_ref.shape[0], LANES), which)
                scores = nt(jnp.where(own, cq[:, cols], zero), keys_ref[:, cols])
                top = jnp.max(scores, axis=1, keepdims=True)
                weights = jnp.exp(scores - top)
                prob = (weights * (1.0 / jnp.sum(weights, axis=1, keepdims=True))).astype(BF16)
                at = (2 * pair + which) * keys_ref.shape[0]
                prob_ref[rows, at : at + keys_ref.shape[0]] = prob
                piece = nn(prob, jnp.where(own_key, values_ref[:, cols], zero))
                total_out = piece if total_out is None else total_out + piece
            mixed.append(total_out.astype(BF16))
        mix = jnp.concatenate(mixed, axis=1)
        mix_ref[rows, :] = mix
        x2 = x1 + nn(mix, co_ref[...])
        x2_ref[rows, :] = x2
        acc_ref[rows, :] = x2
        unit3, _inv3 = unit_rows(x2)
        a3_ref[rows, :] = (unit3 * gain_ffn).astype(BF16)
        g_ref[rows, :] = (g_ref[rows, :].astype(F32) * valid).astype(BF16)
        return 0

    lax.fori_loop(0, blocks, forward_rows, 0)

    def chunk(k, _):
        slot = lax.rem(k, 2)
        for copy in wide_loads(k):
            copy.wait()
        for i in range(blocks):
            rows = slice(i * ROWS, (i + 1) * ROWS)
            z = nt(a3_ref[rows, :], wide_ref[slot, 0])
            zz = z * z
            t = jnp.tanh(GELU_C * z * (1.0 + GELU_A * zz))
            half = 0.5 + 0.5 * t
            r = (z * half).astype(BF16)
            r_ref[rows, :] = r
            slope = half + (0.5 * GELU_C) * z * (1.0 - t * t) * (1.0 + (3.0 * GELU_A) * zz)
            du = (nt(g_ref[rows, :], wide_ref[slot, 1]) * slope).astype(BF16)
            du_ref[rows, :] = du
            acc_ref[rows, :] += nn(r, wide_ref[slot, 1])
            dy_ref[rows, :] += nn(du, wide_ref[slot, 0])
        reduce_stage(k - 1, 1, k >= 1)
        reduce_stage(k - 2, 2, k >= 2)

        @pl.when(k >= 1)
        def _():
            if joined:
                for piece in leaving(k - 1):
                    piece.sent(0)
            else:
                for copy in grad_copies(k - 1):
                    copy.wait()

        @pl.when(k + 1 < CHUNKS)
        def _():
            for copy in wide_loads(k + 1):
                copy.start()

        shape = src_ref.shape[1:]
        src_ref[0] = tn(du_ref[...], a3_ref[...]).reshape(shape).astype(BF16)
        src_ref[1] = tn(r_ref[...], g_ref[...]).reshape(shape).astype(BF16)
        if joined:
            reduce_stage(k, 0)
        else:
            for copy in grad_copies(k):
                copy.start()
        return 0

    def grad_copies(k):
        return [
            pltpu.make_async_copy(src_ref.at[m], sum_ref.at[m, k], out_sem.at[m])
            for m in range(2)
        ]

    dy_ref[...] = jnp.zeros_like(dy_ref)
    lax.fori_loop(0, CHUNKS, chunk, 0)

    g1_low_ref = a3_ref
    g2_low_ref = g_ref
    dcq_ref = cq_scr
    final = CHUNKS - 1

    def out_copies(rows):
        return [
            pltpu.make_async_copy(acc_ref.at[rows, :], out_hbm.at[rows, :], out_sem.at[0]),
            pltpu.make_async_copy(dy_ref.at[rows, :], g1_hbm.at[rows, :], out_sem.at[1]),
        ]

    if not joined:
        for copy in grad_copies(final):
            copy.wait()

    def backward_rows(i, _):
        rows = pl.ds(pl.multiple_of(i * ROWS, ROWS), ROWS)
        for at, k, stage in ((0, 1, 2), (1, 0, 3), (1, 2, 1), (2, 1, 3), (3, 0, 4), (3, 2, 2)):
            reduce_stage(k, stage, i == at)
        pos = i * ROWS + lax.broadcasted_iota(jnp.int32, (ROWS, 1), 0)
        valid = jnp.where(pos < length_ref[0], 1.0, 0.0).astype(F32)
        acc_ref[rows, :] = acc_ref[rows, :] * valid
        unit3, inv3 = unit_rows(x2_ref[rows, :])
        through, gain_part = norm_back(dy_ref[rows, :], unit3, inv3, gain_ffn)
        gain_grad_ref[1:2, :] += gain_part
        g2 = g_ref[rows, :].astype(F32) + through
        g2_low = g2.astype(BF16)
        g2_low_ref[rows, :] = g2_low
        dmix = nt(g2_low, co_ref[...]).astype(BF16)
        cq = cq_scr[rows, :]
        dq_parts = []
        for pair in range(pairs):
            cols = slice(pair * LANES, (pair + 1) * LANES)
            dq = None
            for which in range(2):
                own = head_lane((ROWS, LANES), which)
                own_key = head_lane((keys_ref.shape[0], LANES), which)
                at = (2 * pair + which) * keys_ref.shape[0]
                prob_low = prob_ref[rows, at : at + keys_ref.shape[0]]
                prob = prob_low.astype(F32)
                d_out = jnp.where(own, dmix[:, cols], zero)
                dp = nt(d_out, values_ref[:, cols])
                ds = prob * (dp - jnp.sum(prob * dp, axis=1, keepdims=True))
                ds_low = ds.astype(BF16)
                dv_acc[:, cols] += tn(prob_low, d_out)
                dk_acc[:, cols] += tn(ds_low, jnp.where(own, cq[:, cols], zero))
                piece = nn(ds_low, jnp.where(own_key, keys_ref[:, cols], zero))
                dq = piece if dq is None else dq + piece
            dq_parts.append(dq.astype(BF16))
        dcq = jnp.concatenate(dq_parts, axis=1)
        dcq_ref[rows, :] = dcq
        unit2, inv2 = unit_rows(x1_ref[rows, :])
        through, gain_part = norm_back(nt(dcq, cq_ref[...]), unit2, inv2, gain_cross)
        gain_grad_ref[0:1, :] += gain_part
        g1 = g2 + through
        dy_ref[rows, :] = g1
        g1_low_ref[rows, :] = g1.astype(BF16)
        for copy in out_copies(rows):
            copy.start()
        return 0

    lax.fori_loop(0, blocks, backward_rows, 0)

    reduce_stage(final - 1, 4)
    reduce_stage(final, 3)
    dk = dk_acc[...].astype(BF16)
    dv = dv_acc[...].astype(BF16)
    egrad_ref[...] = nt(dk, ck_ref[...]) + nt(dv, cv_ref[...])
    made = (
        (cq_ref, lambda: tn(a2_ref[...], dcq_ref[...])),
        (ck_ref, lambda: tn(enc_ref[...], dk)),
        (cv_ref, lambda: tn(enc_ref[...], dv)),
        (co_ref, lambda: tn(mix_ref[...], g2_low_ref[...])),
        (wo_ref, lambda: tn(o_ref[...], g1_low_ref[...])),
    )
    writes = []
    for i, (buffer, make) in enumerate(made):
        buffer[...] = make().astype(BF16)
        writes.append(pltpu.make_async_copy(buffer, squares[i], load_sem.at[i]))
        writes[-1].start()
    reduce_stage(final, 4)
    for copy in writes:
        copy.wait()
    for i in range(blocks):
        for copy in out_copies(pl.ds(i * ROWS, ROWS)):
            copy.wait()
    if joined:
        for k in range(CHUNKS):
            for piece in leaving(k):
                for round_idx in (0, 1, 2, 3) if k == final else (1, 2, 3):
                    piece.sent(round_idx)


def middle(length, x, o, cot, enc, gains, wo, cq, ck, cv, co, wide, joined):
    seq, model = x.shape
    enc_len = enc.shape[0]
    anywhere = pl.BlockSpec(memory_space=pl.ANY)
    vmem = pl.BlockSpec(memory_space=pltpu.VMEM)
    smem = pl.BlockSpec(memory_space=pltpu.SMEM)
    low = lambda *shape: pltpu.VMEM(shape, BF16)
    full = lambda *shape: pltpu.VMEM(shape, F32)
    ins = [x, o, cot, enc, wo, cq, ck, cv, co, wide]
    square = jax.ShapeDtypeStruct((model, model), BF16)
    out_shape = [
        jax.ShapeDtypeStruct((seq, model), F32),
        jax.ShapeDtypeStruct((seq, model), F32),
        jax.ShapeDtypeStruct((enc_len, model), F32),
        jax.ShapeDtypeStruct((2, model), F32),
    ] + [square] * 5
    out_specs = [anywhere, anywhere, vmem, vmem] + [anywhere] * 5
    hidden = 4 * model
    chunk_rows = hidden // CHUNKS
    rows_low = [low(seq, model)] * 7 + [low(seq, chunk_rows)] * 2
    params = dict(vmem_limit_bytes=63 * 1024 * 1024)
    if joined:
        part = chunk_rows // (SIDE_DP * SIDE_FSDP)
        lead = (SIDE_DP, 2, 2, 2)
        out_shape += [
            jax.ShapeDtypeStruct((2, CHUNKS * part, model), F32),
        ]
        out_specs += [vmem]
        src = low(2, *lead, part, model)
        count = 2 * CHUNKS
        reduce_sems = count * Reduce.SEMS
        extra = [
            pltpu.VMEM((count,) + buffer.shape, BF16) for buffer in Reduce.scratch(part, model)
        ] + [
            pltpu.SemaphoreType.DMA((reduce_sems,)), pltpu.SemaphoreType.DMA((reduce_sems,)),
        ]
        params.update(collective_id=2, has_side_effects=True)
    else:
        out_shape += [jax.ShapeDtypeStruct((2, CHUNKS, chunk_rows, model), BF16)]
        out_specs += [anywhere]
        src = low(2, chunk_rows, model)
        extra = []
    return pl.pallas_call(
        functools.partial(middle_kernel, joined),
        in_specs=[smem, vmem] + [anywhere] * len(ins),
        out_specs=out_specs,
        out_shape=out_shape,
        scratch_shapes=rows_low
        + [
            low(seq, H * enc_len), full(seq, model), full(seq, model), full(seq, model),
            full(seq, model), low(enc_len, model), low(enc_len, model), low(enc_len, model),
            full(enc_len, model), full(enc_len, model),
        ]
        + [low(model, model)] * 5
        + [
            low(2, 2, chunk_rows, model), src,
            pltpu.SemaphoreType.DMA((9,)), pltpu.SemaphoreType.DMA((2, 2)),
            pltpu.SemaphoreType.DMA((2,)),
        ]
        + extra,
        compiler_params=pltpu.CompilerParams(**params),
        name="middle",
    )(length, gains, *ins)


def run_stages(pieces, lags):
    order = sorted(
        (i + lag, -k, i) for i in range(len(pieces)) for k, lag in enumerate(lags)
    )
    for _time, k, i in order:
        pieces[i].stage(-k)


def gather_kernel(cuts, lags, count, *refs):
    ins, outs = refs[:count], refs[count : 2 * count]
    send, recv, local = refs[2 * count :]
    greet_peers()
    link = Link(send, recv)
    pieces = [
        Gather(ins[w].at[lo:hi], outs[w].at[:, :, :, :, lo:hi], link, local.at[i])
        for i, (w, lo, hi) in enumerate(cuts)
    ]
    run_stages(pieces, lags)
    link.drain()


def gather_all(shards, cuts, lags):
    count = len(shards)
    sems = len(cuts) * Gather.SEMS
    outs = pl.pallas_call(
        functools.partial(gather_kernel, cuts, lags, count),
        out_shape=[
            jax.ShapeDtypeStruct((SIDE_DP, 2, 2, 2) + s.shape, s.dtype) for s in shards
        ],
        in_specs=[pl.BlockSpec(memory_space=pl.ANY)] * count,
        out_specs=[pl.BlockSpec(memory_space=pl.ANY)] * count,
        scratch_shapes=[
            pltpu.SemaphoreType.DMA((sems,)), pltpu.SemaphoreType.DMA((sems,)),
            pltpu.SemaphoreType.DMA((len(cuts),)),
        ],
        compiler_params=pltpu.CompilerParams(
            collective_id=1, has_side_effects=True, vmem_limit_bytes=56 * 1024 * 1024
        ),
        name="gather_all",
    )(*shards)
    return [o.reshape(-1, o.shape[-1]) for o in outs]


def reduce_kernel(cuts, lags, count, *refs):
    ins, outs, rest = refs[:count], refs[count : 2 * count], refs[2 * count :]
    send, recv, local = rest[(Reduce.BUFFERS + 1) * len(cuts) :]
    greet_peers()
    link = Link(send, recv)
    pieces = [
        Reduce(
            ins[w].at[:, :, :, :, lo:hi], outs[w].at[lo:hi],
            *rest[(Reduce.BUFFERS + 1) * i : (Reduce.BUFFERS + 1) * (i + 1)], link, local.at[i],
        )
        for i, (w, lo, hi) in enumerate(cuts)
    ]
    run_stages(pieces, lags)
    link.drain()


def reduce_all(grads, cuts, lags):
    count = len(grads)
    width = grads[0].shape[-1]
    sems = len(cuts) * Reduce.SEMS
    grads = [g.reshape(SIDE_DP, 2, 2, 2, -1, width) for g in grads]
    scratch = []
    for _w, lo, hi in cuts:
        scratch += [pltpu.VMEM((SIDE_DP, 2, 2, hi - lo, width), BF16)]
        scratch += Reduce.scratch(hi - lo, width)
    return pl.pallas_call(
        functools.partial(reduce_kernel, cuts, lags, count),
        out_shape=[jax.ShapeDtypeStruct(g.shape[4:], F32) for g in grads],
        in_specs=[pl.BlockSpec(memory_space=pl.ANY)] * count,
        out_specs=[pl.BlockSpec(memory_space=pltpu.VMEM)] * count,
        scratch_shapes=scratch
        + [
            pltpu.SemaphoreType.DMA((sems,)), pltpu.SemaphoreType.DMA((sems,)),
            pltpu.SemaphoreType.DMA((len(cuts),)),
        ],
        compiler_params=pltpu.CompilerParams(
            collective_id=2, has_side_effects=True, vmem_limit_bytes=60 * 1024 * 1024
        ),
        name="reduce_all",
    )(*grads)


def gather_weights(shards, axes):
    if lax.axis_size("dp") == SIDE_DP and lax.axis_size("fsdp") == SIDE_FSDP:
        cuts = []
        for w, shard in enumerate(shards):
            step = min(shard.shape[0], 24)
            cuts += [(w, lo, lo + step) for lo in range(0, shard.shape[0], step)]
        return gather_all(shards, cuts, (0, 2, 4, 6, 8))
    pile = lax.all_gather(jnp.concatenate(shards, axis=0), axes, axis=0)
    full, at = [], 0
    for shard in shards:
        full.append(pile[:, at : at + shard.shape[0]].reshape(-1, pile.shape[-1]))
        at += shard.shape[0]
    return full


def reduce_grads(grads, axes):
    dev_count = lax.axis_size("dp") * lax.axis_size("fsdp")
    if lax.axis_size("dp") == SIDE_DP and lax.axis_size("fsdp") == SIDE_FSDP:
        cuts = []
        for w, grad in enumerate(grads):
            rows = grad.shape[0] // dev_count
            step = min(rows, 48)
            cuts += [(w, lo, lo + step) for lo in range(0, rows, step)]
        return reduce_all(grads, cuts, (0, 1, 3, 5, 7))
    split = [g.reshape(dev_count, -1, g.shape[-1]) for g in grads]
    pile = lax.psum_scatter(
        jnp.concatenate(split, axis=1), axes, scatter_dimension=0, tiled=False
    ).astype(F32)
    sums, at = [], 0
    for s in split:
        sums.append(pile[at : at + s.shape[1]])
        at += s.shape[1]
    return sums


HIST = 2 * LANES


def self_backward_kernel(
    far_count, x_ref, gain_ref, mid_gain_ref, a_ref, g1_ref, q_ref, k_ref, v_ref, p_ref,
    wo_ref, wq_ref, wk_ref, wv_ref, *refs,
):
    joined = far_count is not None
    if joined:
        far_refs = refs[:far_count]
        ingrad_ref, sum_ref, near_sum_ref, small_ref, table_ref = refs[far_count : far_count + 5]
        rest = refs[far_count + 5 :]
    else:
        ingrad_ref, gw_ref, small_ref, hist_out = refs[:4]
        rest = refs[4:]
    low_ref, near_acc, dk_acc, dv_acc, dq_scr, hist_ref = rest[:6]
    rest = rest[6:]
    step = pl.program_id(0)
    last = pl.num_programs(0) - 1
    seq, model = x_ref.shape
    width = wq_ref.shape[1]
    heads = width // DH
    steps = model // width
    events = {}
    if joined:
        src_ref, own_ref, near_small, far_small, send, recv, local = rest[-7:]
        link = Link(send, recv)
        part = sum_ref.shape[0] // far_count
        pieces = []
        for i in range(far_count + steps):
            far = i < far_count
            pieces.append(
                Reduce(
                    far_refs[i] if far else src_ref.at[(i - far_count) % 2],
                    (sum_ref if far else near_sum_ref).at[
                        (i if far else i - far_count) * part
                        : (i + 1 if far else i + 1 - far_count) * part
                    ],
                    own_ref.at[i] if far else None,
                    *rest[Reduce.BUFFERS * i : Reduce.BUFFERS * (i + 1)], link,
                    local.at[i], early=far_count <= i < far_count + steps - 2,
                )
            )
        small = SumSmall(small_ref, near_small, far_small, link)
        far_times = [(0, 1, 3, 4, 6)] * 3 + [(0, 2, 4, 5, 7)] * (far_count - 3)
        near_times = [(2, 3, 5, 6), (3, 4, 6, 7), (4, 5, 6, 7), (5, 6, 7, 8)]
        near_times += [(6, 7, 8, 9)] * (steps - len(near_times))
        for i in range(far_count):
            for k, time in enumerate(far_times[i]):
                events.setdefault(time, []).append((-k, pieces[i]))
        for i in range(steps):
            for k, time in enumerate(near_times[i]):
                events.setdefault(time, []).append((-k - 1, pieces[far_count + i]))

    def tick(time):
        for k, piece in sorted(events.get(time, []), key=lambda event: event[0]):
            piece.stage(-k)

    @pl.when(step == 0)
    def _():
        if joined:
            greet_peers()
            tick(0)
        low_ref[...] = g1_ref[...].astype(BF16)
        ingrad_ref[...] = jnp.zeros_like(ingrad_ref)
        hist_ref[...] = jnp.zeros_like(hist_ref)

    for g in range(1, steps):
        if events.get(g):
            pl.when(step == g)(functools.partial(tick, g))

    d_all = nt(low_ref[...], wo_ref[...]).astype(BF16)
    zero = jnp.zeros((), BF16)
    for pair in range(width // LANES):
        cols = slice(pair * LANES, (pair + 1) * LANES)
        dk_acc[...] = jnp.zeros_like(dk_acc)
        dv_acc[...] = jnp.zeros_like(dv_acc)
        dq_blocks = [None] * (seq // ROWS)
        for which in range(2):
            local_head = pair * 2 + which
            head = step * heads + local_head
            own = head_lane((seq, LANES), which)
            d_out = jnp.where(own, d_all[:, cols], zero)
            queries = jnp.where(own, q_ref[:, cols], zero)
            keys = jnp.where(own, k_ref[:, cols], zero)
            for blk in range(seq // ROWS):
                rows = slice(blk * ROWS, (blk + 1) * ROWS)
                span = (blk + 1) * ROWS
                prob_low = p_ref[local_head, rows, :span]
                prob = prob_low.astype(F32)
                dp = nt(d_out[rows], v_ref[:span, cols])
                ds = prob * (dp - jnp.sum(prob * dp, axis=1, keepdims=True))
                if blk == 0:
                    near_acc[:, :LANES] = jnp.zeros((ROWS, LANES), F32)
                    near_acc[:, LANES:] = ds
                else:
                    near_acc[...] += ds[:, span - ROWS - LANES :]
                ds_low = ds.astype(BF16)
                part_q = nn(ds_low, keys[:span])
                dq_blocks[blk] = part_q if which == 0 else dq_blocks[blk] + part_q
                dk_acc[:span, :] += tn(ds_low, queries[rows])
                dv_acc[:span, :] += tn(prob_low, d_out[rows])
            padded = jnp.concatenate([near_acc[...], jnp.zeros((ROWS, LANES), F32)], axis=1)
            count = ROWS
            while count > 1:
                count //= 2
                padded = padded[:count] + pltpu.roll(padded[count:], 4 * LANES - count, 1)
            hist_ref[pl.ds(head, 1), :] = padded[:, :HIST]
        for blk in range(seq // ROWS):
            rows = slice(blk * ROWS, (blk + 1) * ROWS)
            dq_scr[rows, cols] = dq_blocks[blk].astype(BF16)
        dq_scr[:, width + pair * LANES : width + (pair + 1) * LANES] = dk_acc[...].astype(BF16)
        dq_scr[:, 2 * width + pair * LANES : 2 * width + (pair + 1) * LANES] = dv_acc[
            ...
        ].astype(BF16)

    grads = tn(a_ref[...], dq_scr[...])
    if joined:
        for g in range(steps):

            @pl.when(step == g)
            def _():
                if g >= 2:
                    pieces[far_count + g - 2].sent(0)
                src_ref[g % 2] = grads.reshape(src_ref.shape[1:]).astype(BF16)
                pieces[far_count + g].stage(0)
                if g == steps - 1:
                    tick(steps)
    else:
        gw_ref[0] = grads.astype(BF16)
    weights = jnp.concatenate([wq_ref[...], wk_ref[...], wv_ref[...]], axis=1)
    ingrad_ref[...] += nt(dq_scr[...], weights)

    @pl.when(step == last)
    def _():
        unit, inv = unit_rows(x_ref[...].astype(F32))
        through, gain_part = norm_back(ingrad_ref[...], unit, inv, gain_ref[...])
        small_ref[...] = jnp.zeros_like(small_ref)
        small_ref[0:1, :model] = gain_part
        small_ref[1:3, :model] = mid_gain_ref[...]
        small_ref[:, model : model + HIST] = hist_ref[0:8, :]
        small_ref[:, model + HIST :] = hist_ref[8:16, :]
        if joined:
            small.stage(0)
            tick(steps + 1)
            small.stage(1)
        ingrad_ref[...] = g1_ref[...] + through
        if joined:
            small.stage(2)
            tick(steps + 2)
            small.stage(3)
            small.stage(4)
            z, y, x, c = coords()
            mine = z * SIDE_FSDP + y * 4 + x * 2 + c
            lane = lax.broadcasted_iota(jnp.int32, (16, HIST), 1)
            distance = LANES - lane
            bucket = bucket_of(jnp.maximum(distance, 0))
            usable = (distance >= 0) & (bucket < NB - 1)
            picked = usable & ((bucket == mine) | (mine == NB - 1))
            sign = jnp.where(mine == NB - 1, -1.0, 1.0)
            hist = jnp.concatenate(
                [small_ref[:, model : model + HIST], small_ref[:, model + HIST :]], axis=0
            )
            column = sign * jnp.sum(jnp.where(picked, hist, 0.0), axis=1, keepdims=True)
            table_ref[...] = jnp.broadcast_to(column, table_ref.shape)
            tick(steps + 3)
            link.drain()
        else:
            hist_out[...] = hist_ref[...]


def self_backward(x, gain, mid_gain, a1, g1, q, k, v, p, wo, wq, wk, wv, far_grads):
    seq, model = x.shape
    width = 128
    heads = width // DH
    steps = model // width
    joined = far_grads is not None
    held = lambda shape: pl.BlockSpec(
        shape, lambda i: (0,) * len(shape), pipeline_mode=pl.Buffered(1)
    )
    whole = lambda shape: pl.BlockSpec(shape, lambda i: (0,) * len(shape))
    columns = pl.BlockSpec((seq, width), lambda i: (0, i))
    weight = pl.BlockSpec((model, width), lambda i: (0, i))
    weight_rows = pl.BlockSpec((width, model), lambda i: (i, 0))
    in_specs = [
        held((seq, model)), held((1, model)), held((2, model)), held((seq, model)),
        held((seq, model)), columns, columns, columns,
        pl.BlockSpec((heads, seq, seq), lambda i: (i, 0, 0)),
        weight_rows, weight, weight, weight,
    ]
    small = (8, model + 2 * HIST)
    out_specs = [whole((seq, model))]
    out_shape = [jax.ShapeDtypeStruct((seq, model), F32)]
    scratch = [
        pltpu.VMEM((seq, model), BF16),
        pltpu.VMEM((ROWS, ROWS + LANES), F32),
        pltpu.VMEM((seq, LANES), F32),
        pltpu.VMEM((seq, LANES), F32),
        pltpu.VMEM((seq, 3 * width), BF16),
        pltpu.VMEM((16, HIST), F32),
    ]
    extra = []
    params = dict(vmem_limit_bytes=63 * 1024 * 1024)
    if joined:
        count = len(far_grads)
        part = model // (SIDE_DP * SIDE_FSDP)
        across = 3 * width
        extra = [g.reshape(SIDE_DP, 2, 2, 2, part, model) for g in far_grads]
        in_specs += [pl.BlockSpec(memory_space=pl.ANY)] * count
        shapes = ((count * part, model), (steps * part, across), small, (16, LANES))
        out_specs += [whole(s) for s in shapes]
        out_shape += [jax.ShapeDtypeStruct(s, F32) for s in shapes]
        for i in range(count + steps):
            scratch += Reduce.scratch(part, model if i < count else across)
        sems = (count + steps) * Reduce.SEMS + SumSmall.SEMS
        scratch += [
            pltpu.VMEM((2, SIDE_DP, 2, 2, 2, part, across), BF16),
            pltpu.VMEM((count, SIDE_DP, 2, 2, part, model), BF16),
            pltpu.VMEM((3,) + small, F32),
            pltpu.VMEM((SIDE_DP - 1,) + small, F32),
            pltpu.SemaphoreType.DMA((sems,)), pltpu.SemaphoreType.DMA((sems,)),
            pltpu.SemaphoreType.DMA((count + steps,)),
        ]
        params.update(collective_id=3, has_side_effects=True)
    else:
        count = None
        out_specs += [
            pl.BlockSpec((1, model, 3 * width), lambda i: (i, 0, 0)), whole(small),
            whole((16, HIST)),
        ]
        out_shape += [
            jax.ShapeDtypeStruct((steps, model, 3 * width), BF16),
            jax.ShapeDtypeStruct(small, F32),
            jax.ShapeDtypeStruct((16, HIST), F32),
        ]
    return pl.pallas_call(
        functools.partial(self_backward_kernel, count),
        grid=(steps,),
        in_specs=in_specs,
        out_specs=out_specs,
        out_shape=out_shape,
        scratch_shapes=scratch,
        compiler_params=pltpu.CompilerParams(**params),
        cost_estimate=pl.CostEstimate(
            flops=14 * seq * model * model + 8 * seq * seq * model,
            bytes_accessed=2 * H * seq * seq + 24 * seq * model,
            transcendentals=0,
        ),
        name="self_backward",
    )(x, gain, mid_gain, a1, g1, q, k, v, p, wo, wq, wk, wv, *extra)


def body(
    tokens, encoder_states, lengths, dealing, cotangent,
    w_query, w_key, w_value, w_out, c_query, c_key, c_value, c_out, w_in, w_down,
    gain_self, gain_cross, gain_ffn, bias_table,
):
    axes = ("dp", "fsdp")
    fsdp_size = lax.axis_size("fsdp")
    dp_size = lax.axis_size("dp")
    dev_count = dp_size * fsdp_size
    dp_index = lax.axis_index("dp")
    own = dp_index * fsdp_size + lax.axis_index("fsdp")
    seq_len, model = tokens.shape[1:]
    route = [(a, a ^ 1) for a in range(dp_size)]

    x = tokens[0]
    cot = cotangent[0]
    in_place = lax.dynamic_slice_in_dim(dealing, own, 1) == own
    enc_other = lax.ppermute(encoder_states[0], "dp", route)
    enc = jnp.where(in_place[:, None], encoder_states[0], enc_other)
    length = lax.dynamic_slice_in_dim(lengths, own, 1)

    gain_part = gain_self.shape[0]
    small = jnp.concatenate([gain_self, gain_cross, gain_ffn, bias_table])
    small_row = jnp.pad(small, (0, model - small.shape[0]))[None, :]
    small_row = jnp.pad(small_row, ((0, 7), (0, 0)))
    joined = dp_size == SIDE_DP and fsdp_size == SIDE_FSDP
    pile = jnp.concatenate([w_in.T, w_down], axis=0)
    wide = lax.all_gather(pile, axes, axis=0)
    if not joined:
        wide = wide.reshape(dev_count, 2, -1, model).swapaxes(0, 1)
        wide = wide.reshape(2, CHUNKS, -1, model)
    wq, wk, wv, small_all, wo, cq, ck, cv, co = gather_weights(
        [w_query, w_key, w_value, small_row, w_out, c_query, c_key, c_value, c_out], axes
    )
    small_all = small_all.reshape(dev_count, 8, model)[:, 0].astype(F32)
    gains = [
        small_all[:, i * gain_part : (i + 1) * gain_part].reshape(1, model) for i in range(3)
    ]
    table_part = bias_table.shape[0]
    table = small_all[:, 3 * gain_part : 3 * gain_part + table_part].reshape(NB, H)

    distance = jnp.arange(LANES + 1, dtype=jnp.int32)
    bucket_hot = (bucket_of(distance)[:, None] == jnp.arange(NB, dtype=jnp.int32)[None, :]).astype(
        F32
    )
    by_distance = jnp.dot(bucket_hot, table, precision=lax.Precision.HIGHEST)
    far = by_distance[LANES]
    near = (by_distance - far[None, :])[::-1].T
    near = jnp.pad(near, ((0, 16 - H), (0, 4 * LANES - near.shape[1])))

    q, k, v, o, p, a1 = self_forward(length, x, gains[0], wq, wk, wv, far, near)
    done = middle(
        length, x, o, cot, enc, jnp.concatenate(gains[1:], axis=0), wo, cq, ck, cv, co, wide,
        joined,
    )
    out, g1, egrad, mid_gain_grad = done[:4]
    squares = list(done[4:9])
    if joined:
        sum_in, sum_down = done[9][0], done[9][1]
    else:
        sum_in, sum_down = reduce_grads([g.reshape(-1, model) for g in done[9]], axes)
    done = self_backward(
        x, gains[0], mid_gain_grad, a1, g1, q, k, v, p, wo, wq, wk, wv,
        squares if joined else None,
    )
    in_grad = done[0]
    if joined:
        sums, near_sums, small, table_column = done[1:]
        part = w_query.shape[0]
        sum_cq, sum_ck, sum_cv, sum_co, sum_wo = (
            sums[i * part : (i + 1) * part] for i in range(5)
        )
        steps = near_sums.shape[0] // part
        across = model // steps
        sum_wq, sum_wk, sum_wv = (
            jnp.concatenate(
                [
                    near_sums[g * part : (g + 1) * part, i * across : (i + 1) * across]
                    for g in range(steps)
                ],
                axis=1,
            )
            for i in range(3)
        )
        ends = lax.dynamic_slice(small, (0, own * gain_part), (3, gain_part))
        end_self, end_cross, end_ffn = ends[0], ends[1], ends[2]
        end_table = table_column[:H, 0]
    else:
        gw, small, hist = done[1:]
        g_wq, g_wk, g_wv = (
            jnp.concatenate(
                [g[:, i * LANES : (i + 1) * LANES] for g in gw], axis=1
            )
            for i in range(3)
        )
        near_hot = bucket_hot[:LANES] * (jnp.arange(NB) < NB - 1).astype(F32)
        by_dist = hist[:H, 1 : LANES + 1][:, ::-1]
        near_sums = jnp.dot(near_hot.T, by_dist.T, precision=lax.Precision.HIGHEST)
        grad_table = jnp.where(
            (jnp.arange(NB) < NB - 1)[:, None],
            near_sums, -jnp.sum(near_sums, axis=0, keepdims=True),
        )
        small_grads = jnp.concatenate(
            [small[i, :model].reshape(dev_count, -1) for i in range(3)]
            + [grad_table.reshape(dev_count, -1)],
            axis=1,
        )
        small_count = small_grads.shape[1]
        small_low = jnp.pad(small_grads.astype(BF16), ((0, 0), (0, model - small_count)))
        small_low = jnp.pad(small_low[:, None, :], ((0, 0), (0, 7), (0, 0))).reshape(-1, model)
        sum_cq, sum_ck, sum_cv, sum_co, sum_wo, sum_wq, sum_wk, sum_wv, sum_small = reduce_grads(
            squares + [g_wq, g_wk, g_wv, small_low], axes
        )
        ends = sum_small[0]
        end_self, end_cross, end_ffn = (
            ends[i * gain_part : (i + 1) * gain_part] for i in range(3)
        )
        end_table = ends[3 * gain_part : small_count]

    egrad_other = lax.ppermute(egrad, "dp", route)
    encoder_grad = jnp.where(in_place[:, None], egrad, egrad_other)
    return (
        out[None], in_grad[None], encoder_grad[None],
        sum_wq, sum_wk, sum_wv, sum_wo, sum_cq, sum_ck, sum_cv, sum_co, sum_in.T, sum_down,
        end_self, end_cross, end_ffn, end_table,
    )


def solution(mesh):
    rows3 = P(("dp", "fsdp"), None, None)
    rows2 = P(("dp", "fsdp"), None)
    cols2 = P(None, ("dp", "fsdp"))
    line = P(("dp", "fsdp"))
    in_specs = (
        (rows3, rows3, P(), P(), rows3) + (rows2,) * 8 + (cols2, rows2) + (line,) * 4
    )
    out_specs = (rows3,) * 3 + (rows2,) * 8 + (cols2, rows2) + (line,) * 4
    return jax.shard_map(body, mesh=mesh, in_specs=in_specs, out_specs=out_specs, check_vma=False)
```

```python
import functools
import math

import jax
import jax.numpy as jnp
from jax import lax
from jax.experimental import pallas as pl
from jax.experimental.pallas import tpu as pltpu
from jax.sharding import PartitionSpec as P

H = 12
DH = 64
NB = 32
MAXDIST = 128
EPSILON = 1e-06
MASKED = -1e30
LANES = 128
CHUNKS = 3
ROWS = 256
F32 = jnp.float32
BF16 = jnp.bfloat16
GELU_C = math.sqrt(2.0 / math.pi)
GELU_A = 0.044715


def bucket_of(distance):
    exact_count = NB // 2
    bucket = jnp.minimum(distance, exact_count)
    for level_idx in range(1, exact_count):
        threshold = int(
            math.ceil(exact_count * (MAXDIST / exact_count) ** (level_idx / exact_count))
        )
        bucket = bucket + (distance >= threshold).astype(jnp.int32)
    return bucket


def nn(left_op, right_op):
    return lax.dot_general(
        left_op, right_op, (((1,), (0,)), ((), ())), preferred_element_type=F32
    )


def nt(left_op, right_op):
    return lax.dot_general(
        left_op, right_op, (((1,), (1,)), ((), ())), preferred_element_type=F32
    )


def tn(left_op, right_op):
    return lax.dot_general(
        left_op, right_op, (((0,), (0,)), ((), ())), preferred_element_type=F32
    )


def unit_rows(values_in):
    inv_rms = lax.rsqrt(jnp.mean(values_in * values_in, axis=-1, keepdims=True) + EPSILON)
    return values_in * inv_rms, inv_rms


def norm_back(grad_in, unit, inv_rms, gain_vec):
    scaled = grad_in * gain_vec
    through = inv_rms * (scaled - unit * jnp.mean(scaled * unit, axis=-1, keepdims=True))
    return through, jnp.sum(grad_in * unit, axis=0, keepdims=True)


def head_lane(shape, which):
    lane = lax.broadcasted_iota(jnp.int32, shape, len(shape) - 1)
    return (lane // DH) == which


SIDE_DP = 4
SIDE_FSDP = 8
MESH = pl.DeviceIdType.MESH


def coords():
    along = lax.axis_index("fsdp")
    return lax.axis_index("dp"), along // 4, lax.rem(along // 2, 2), lax.rem(along, 2)


def device(z, y, x, c):
    return (z, y * 4 + x * 2 + c)


def greet_peers():
    z, y, x, c = coords()
    peers = [device(lax.rem(z + k, SIDE_DP), y, x, c) for k in range(1, SIDE_DP)]
    peers += [device(z, y, 1 - x, c), device(z, 1 - y, x, c), device(z, y, x, 1 - c)]
    barrier = pltpu.get_barrier_semaphore()
    for peer in peers:
        pl.semaphore_signal(barrier, inc=1, device_id=peer, device_id_type=MESH)
    pl.semaphore_wait(barrier, len(peers))


class Link:
    def __init__(self, send, recv):
        self.send, self.recv, self.used, self.pieces = send, recv, 0, []

    def take(self, piece):
        self.pieces.append(piece)
        self.used += piece.SEMS
        return self.used - piece.SEMS

    def drain(self):
        for piece in self.pieces:
            piece.drain()


class Place:
    def __init__(self):
        z, y, x, c = self.at = coords()
        self.to_y = device(z, 1 - y, x, c)
        self.to_x = device(z, y, 1 - x, c)
        self.to_core = device(z, y, x, 1 - c)
        self.other_z = [lax.rem(z + k, SIDE_DP) for k in range(1, SIDE_DP)]
        self.to_z = [device(other, y, x, c) for other in self.other_z]
        self.ny, self.nx, self.nc = 1 - y, 1 - x, 1 - c


class Piece:
    def __init__(self, link, local, place=None, first=None):
        self.link, self.local = link, local
        self.first = link.take(self) if first is None else first
        self.half_a, self.half_b = slice(0, SIDE_DP // 2), slice(SIDE_DP // 2, SIDE_DP)
        place = place or Place()
        self.at, self.to_y, self.to_x, self.to_core = (
            place.at, place.to_y, place.to_x, place.to_core
        )
        self.other_z, self.to_z = place.other_z, place.to_z
        self.ny, self.nx, self.nc = place.ny, place.nx, place.nc

    def copy(self, slot, src, dst, peer):
        return pltpu.make_async_remote_copy(
            src_ref=src, dst_ref=dst, send_sem=self.link.send.at[self.first + slot],
            recv_sem=self.link.recv.at[self.first + slot], device_id=peer, device_id_type=MESH,
        )

    def start(self, k):
        for copy in self.moves(k):
            copy.start()

    def arrive(self, k):
        for copy in self.moves(k):
            copy.wait_recv()

    def sent(self, k):
        for copy in self.moves(k):
            copy.wait_send()

    def drain(self):
        for k in self.UNSENT:
            self.sent(k)

    def stage(self, k):
        (self.s0, self.s1, self.s2, self.s3, self.s4)[k]()


class Gather(Piece):
    SEMS = 13
    UNSENT = (0, 1, 2, 3, 4, 5)

    def __init__(self, src, out, link, local, place=None, first=None):
        super().__init__(link, local, place, first)
        self.src, self.out = src, out

    def moves(self, k):
        z, y, x, c = self.at
        out, a, b = self.out, self.half_a, self.half_b
        if k == 0:
            here = out.at[z, y, x, c]
            return [self.copy(i, self.src, here, peer) for i, peer in enumerate(self.to_z)]
        same = lambda slot, ref, peer: self.copy(slot, ref, ref, peer)
        if k == 1:
            return [
                same(3, out.at[a, y, x, c], self.to_x),
                same(4, out.at[b, y, x, c], self.to_y),
            ]
        if k == 2:
            return [
                same(5, out.at[a, y, :, c], self.to_y),
                same(6, out.at[b, :, x, c], self.to_x),
            ]
        if k == 3:
            return [same(7, out.at[:, y, x, c], self.to_core)]
        if k == 4:
            return [
                same(8, out.at[a, y, self.nx, c], self.to_core),
                same(9, out.at[b, self.ny, x, c], self.to_core),
            ]
        return [
            same(10, out.at[a, self.ny, :, c], self.to_core),
            same(11, out.at[b, :, self.nx, c], self.to_core),
        ]

    def keep(self):
        return pltpu.make_async_copy(self.src, self.out.at[self.at], self.local)

    def s0(self):
        self.start(0)
        self.keep().start()

    def s1(self):
        self.keep().wait()
        self.arrive(0)
        self.start(1)
        self.start(3)

    def s2(self):
        self.arrive(1)
        self.start(2)
        self.start(4)

    def s3(self):
        self.arrive(2)
        self.start(5)

    def s4(self):
        for k in (3, 4, 5):
            self.arrive(k)


class Reduce(Piece):
    SEMS = 8
    BUFFERS = 6

    def __init__(
        self, src, out, own, held, l1a, l1b, l2a, l2b, l3, link, local, place=None, first=None,
        early=False,
    ):
        super().__init__(link, local, place, first)
        self.src, self.out, self.own, self.held = src, out, own, held
        self.l1a, self.l1b, self.l2a, self.l2b, self.l3 = l1a, l1b, l2a, l2b, l3
        self.UNSENT = (1, 2, 3) if early else (0, 1, 2, 3)

    @staticmethod
    def scratch(rows, width):
        buffer = lambda *lead: pltpu.VMEM(lead + (rows, width), BF16)
        half = SIDE_DP // 2
        return [
            buffer(SIDE_DP, 2, 2), buffer(half, 2), buffer(half, 2), buffer(half), buffer(half),
            buffer(SIDE_DP - 1),
        ]

    def moves(self, k):
        z, y, x, c = self.at
        held, a, b = self.held, self.half_a, self.half_b
        if k == 0:
            return [self.copy(0, self.src.at[:, :, :, self.nc], held, self.to_core)]
        if k == 1:
            return [
                self.copy(1, held.at[a, self.ny], self.l1a, self.to_y),
                self.copy(2, held.at[b, :, self.nx], self.l1b, self.to_x),
            ]
        if k == 2:
            return [
                self.copy(3, held.at[a, y, self.nx], self.l2a, self.to_x),
                self.copy(4, held.at[b, self.ny, x], self.l2b, self.to_y),
            ]
        return [
            self.copy(5 + i, held.at[other, y, x], self.l3.at[i], peer)
            for i, (other, peer) in enumerate(zip(self.other_z, self.to_z))
        ]

    def keep(self):
        return pltpu.make_async_copy(self.src.at[:, :, :, self.at[3]], self.own, self.local)

    def s0(self):
        self.start(0)
        if self.own is not None:
            self.keep().start()

    def s1(self):
        held = self.held
        if self.own is not None:
            self.keep().wait()
            self.arrive(0)
            held[...] = held[...] + self.own[...]
        else:
            self.arrive(0)
            held[...] = held[...] + self.src[:, :, :, self.at[3]]
        self.start(1)

    def s2(self):
        z, y, x, c = self.at
        self.arrive(1)
        held, a, b = self.held, self.half_a, self.half_b
        held[a, y] = held[a, y] + self.l1a[...]
        held[b, :, x] = held[b, :, x] + self.l1b[...]
        self.start(2)

    def s3(self):
        z, y, x, c = self.at
        self.arrive(2)
        held, a, b = self.held, self.half_a, self.half_b
        held[a, y, x] = held[a, y, x] + self.l2a[...]
        held[b, y, x] = held[b, y, x] + self.l2b[...]
        self.start(3)

    def s4(self):
        z, y, x, c = self.at
        self.arrive(3)
        total = self.held[z, y, x].astype(F32)
        for k in range(SIDE_DP - 1):
            total = total + self.l3[k].astype(F32)
        self.out[...] = total


class SumSmall(Piece):
    SEMS = 6
    UNSENT = ()

    def __init__(self, total, near, far, link):
        super().__init__(link, None)
        self.total, self.near, self.far = total, near, far

    def moves(self, k):
        if k < 3:
            peer = (self.to_core, self.to_y, self.to_x)[k]
            return [self.copy(k, self.total, self.near.at[k], peer)]
        return [
            self.copy(3 + i, self.total, self.far.at[i], peer) for i, peer in enumerate(self.to_z)
        ]

    def add(self, k):
        self.arrive(k)
        self.sent(k)
        if k < 3:
            self.total[...] = self.total[...] + self.near[k]
        else:
            total = self.total[...]
            for i in range(SIDE_DP - 1):
                total = total + self.far[i]
            self.total[...] = total

    def s0(self):
        self.start(0)

    def s1(self):
        self.add(0)
        self.start(1)

    def s2(self):
        self.add(1)
        self.start(2)

    def s3(self):
        self.add(2)
        self.start(3)

    def s4(self):
        self.add(3)


FORWARD_SQUARES = 5


def bias_tables(table):
    lane = lax.broadcasted_iota(jnp.int32, (NB, 4 * LANES), 1)
    bucket = bucket_of(jnp.maximum(LANES - lane, 0))
    bucket = jnp.where(lane <= LANES, bucket, NB - 1)
    row = lax.broadcasted_iota(jnp.int32, (NB, 4 * LANES), 0)
    last = jnp.where(row == NB - 1, 1.0, 0.0)
    hot = jnp.where(row == bucket, 1.0, 0.0) - last
    near = tn(table.astype(BF16), hot.astype(BF16))
    far = tn(table.astype(BF16), last[:, :LANES].astype(BF16))
    return near[:16], far[:16]


def self_forward_kernel(joined, length_ref, x_ref, *refs):
    step = pl.program_id(0)
    last = pl.num_programs(0) - 1
    if joined:
        shards, refs = refs[:11], refs[11:]
    else:
        (gain_in, wq_ref, wk_ref, wv_ref, table_in), refs = refs[:5], refs[5:]
    (q_ref, k_ref, v_ref, o_ref, p_ref, a_ref), refs = refs[:6], refs[6:]
    if joined:
        (wq_ref, wk_ref, wv_ref, gain_ref), refs = refs[:4], refs[4:]
        squares, wide_ref = refs[:FORWARD_SQUARES], refs[FORWARD_SQUARES]
        tile_ref, near_ref, far_ref, got_ref, got_small, send, recv, local = refs[
            FORWARD_SQUARES + 1 :
        ]
        link, place = Link(send, recv), Place()
        first = [Gather(shards[i], got_ref.at[i], link, local.at[i], place) for i in range(3)]
        first.append(Gather(shards[3], got_small, link, local.at[3], place))
        second = [
            Gather(shards[4 + i], squares[i], link, local.at[4 + i], place)
            for i in range(FORWARD_SQUARES)
        ]
        part = wide_ref.shape[-2]
        third = [
            Gather(
                shards[9 + m].at[k * part : (k + 1) * part], wide_ref.at[k, m], link,
                local.at[9 + 2 * k + m], place,
            )
            for k in range(CHUNKS)
            for m in range(2)
        ]
    else:
        tile_ref, near_ref, far_ref = refs
    seq, model = x_ref.shape
    width = q_ref.shape[1]

    def normed():
        return unit_rows(x_ref[...].astype(F32))[0]

    def set_tables(table):
        near, far = bias_tables(table)
        near_ref[...] = near
        far_ref[...] = far

    @pl.when(step == 0)
    def _():
        if not joined:
            a_ref[...] = (normed() * gain_in[0:1, :]).astype(BF16)
            set_tables(table_in[...])
            return
        greet_peers()
        for piece in first:
            piece.stage(0)
        unit = normed()
        for piece in first:
            piece.stage(1)
        for piece in second:
            piece.stage(0)
        for piece in first:
            piece.stage(2)
        first[3].stage(3)
        first[3].stage(4)
        small = got_small[...].astype(F32).reshape(NB, 8, model)
        gains = jnp.sum(small, axis=0)
        gain_ref[...] = gains
        which = lax.broadcasted_iota(jnp.int32, (NB, 8, LANES), 1)
        set_tables(jnp.sum(jnp.where(which == 3, small[:, :, :LANES], 0.0), axis=1))
        a_ref[...] = (unit * gains[0:1, :]).astype(BF16)
        for piece in first[:3]:
            piece.stage(3)
        for i, full_ref in enumerate((wq_ref, wk_ref, wv_ref)):
            first[i].stage(4)
            full_ref[...] = got_ref[i].astype(F32).reshape(model, model).astype(BF16)
        for piece in second:
            piece.stage(1)
        for piece in third[:2]:
            piece.stage(0)

    if joined:

        @pl.when(step == 1)
        def _():
            for piece in second:
                piece.stage(2)
            for piece in third[2:4]:
                piece.stage(0)

        @pl.when(step == 2)
        def _():
            for piece in third[:2]:
                piece.stage(1)
            for piece in third[4:]:
                piece.stage(0)

    for w_ref, out_ref in ((wq_ref, q_ref), (wk_ref, k_ref), (wv_ref, v_ref)):
        if joined:
            weights = w_ref[:, pl.ds(pl.multiple_of(step * width, LANES), width)]
        else:
            weights = w_ref[...]
        out_ref[...] = nn(a_ref[...], weights).astype(BF16)

    key_pos = lax.broadcasted_iota(jnp.int32, (seq, 1), 0)
    key_dead = key_pos >= length_ref[0]
    row = lax.broadcasted_iota(jnp.int32, (ROWS, ROWS + LANES), 0)
    col = lax.broadcasted_iota(jnp.int32, (ROWS, ROWS + LANES), 1)
    ahead = col - LANES > row
    for pair in range(width // LANES):
        cols = slice(pair * LANES, (pair + 1) * LANES)
        outs = [None] * (seq // ROWS)
        for which in range(2):
            local = pair * 2 + which
            head = step * (width // DH) + local
            spun = pltpu.roll(
                jnp.broadcast_to(near_ref[pl.ds(head, 1), :], (ROWS, 4 * LANES)),
                0, 1, stride=1, stride_axis=0,
            )
            tile_ref[...] = jnp.where(ahead, MASKED, spun[:, : ROWS + LANES])
            own = head_lane((seq, LANES), which)
            extra = lax.broadcasted_iota(jnp.int32, (seq, LANES), 1) == (DH if which == 0 else 0)
            far = jnp.where(key_dead, MASKED, far_ref[pl.ds(head, 1), 0:1]).astype(BF16)
            keys = jnp.where(own, k_ref[:, cols], jnp.where(extra, far, jnp.zeros((), BF16)))
            values = jnp.where(own, v_ref[:, cols], jnp.zeros((), BF16))
            queries = jnp.where(own, q_ref[:, cols], jnp.where(extra, 1.0, 0.0).astype(BF16))
            for blk in range(seq // ROWS):
                rows = slice(blk * ROWS, (blk + 1) * ROWS)
                span = (blk + 1) * ROWS
                cut = max(span - ROWS - LANES, 0)
                scores = nt(queries[rows], keys[:span])
                if cut:
                    near = scores[:, cut:] + tile_ref[...]
                    scores = jnp.concatenate([scores[:, :cut], near], axis=1)
                elif span == ROWS:
                    scores = scores + tile_ref[:, LANES:]
                else:
                    near = scores[:, ROWS - LANES :] + tile_ref[...]
                    scores = jnp.concatenate([scores[:, : ROWS - LANES], near], axis=1)
                top = jnp.max(scores, axis=1, keepdims=True)
                weights = jnp.exp(scores - top)
                total = jnp.sum(weights, axis=1, keepdims=True)
                probs = (weights * (1.0 / total)).astype(BF16)
                p_ref[local, rows, :span] = probs
                mixed = nn(probs, values[:span])
                outs[blk] = mixed if outs[blk] is None else outs[blk] + mixed
        for blk in range(seq // ROWS):
            o_ref[blk * ROWS : (blk + 1) * ROWS, cols] = outs[blk].astype(BF16)

    if joined:

        @pl.when(step == last)
        def _():
            for stage in (3, 4):
                for piece in second:
                    piece.stage(stage)
            for piece in third[:2]:
                piece.arrive(1)
                piece.arrive(3)
            for piece in third[2:]:
                piece.keep().wait()
                piece.arrive(0)
            for piece in first + second:
                piece.drain()
            for i, piece in enumerate(third):
                for k in (0, 1, 3) if i < 2 else (0,):
                    piece.sent(k)


def self_forward(length, x, shards, full):
    seq, model = x.shape
    width = 256
    heads = width // DH
    steps = model // width
    joined = full is None
    whole = lambda shape: pl.BlockSpec(shape, lambda i: (0,) * len(shape))
    held = lambda shape: pl.BlockSpec(
        shape, lambda i: (0,) * len(shape), pipeline_mode=pl.Buffered(1)
    )
    anywhere = pl.BlockSpec(memory_space=pl.ANY)
    smem = pl.BlockSpec(memory_space=pltpu.SMEM)
    columns = pl.BlockSpec((seq, width), lambda i: (0, i))
    weight = pl.BlockSpec((model, width), lambda i: (0, i))
    in_specs = [smem, held((seq, model))]
    out_specs = [
        columns, columns, columns, columns,
        pl.BlockSpec((heads, seq, seq), lambda i: (i, 0, 0)), whole((seq, model)),
    ]
    out_shape = [jax.ShapeDtypeStruct((seq, model), BF16)] * 4 + [
        jax.ShapeDtypeStruct((H, seq, seq), BF16), jax.ShapeDtypeStruct((seq, model), BF16),
    ]
    scratch = [
        pltpu.VMEM((ROWS, ROWS + LANES), F32), pltpu.VMEM((16, 4 * LANES), F32),
        pltpu.VMEM((16, LANES), F32),
    ]
    params = dict(vmem_limit_bytes=62 * 1024 * 1024)
    if joined:
        lead = (SIDE_DP, 2, 2, 2)
        part = shards[0].shape[0]
        wide = (CHUNKS, 2) + lead + (shards[9].shape[0] // CHUNKS, model)
        ins = list(shards)
        in_specs += [anywhere] * len(ins)
        square = jax.ShapeDtypeStruct((model, model), BF16)
        out_shape += [square] * 3 + [jax.ShapeDtypeStruct((8, model), F32)]
        out_specs += [whole((model, model))] * 3 + [whole((8, model))]
        out_shape += [jax.ShapeDtypeStruct(lead + (part, model), BF16)] * FORWARD_SQUARES
        out_shape += [jax.ShapeDtypeStruct(wide, BF16)]
        out_specs += [anywhere] * (FORWARD_SQUARES + 1)
        count = 4 + FORWARD_SQUARES + 2 * CHUNKS
        scratch += [
            pltpu.VMEM((3,) + lead + (part, model), BF16), pltpu.VMEM(lead + (8, model), BF16),
            pltpu.SemaphoreType.DMA((count * Gather.SEMS,)),
            pltpu.SemaphoreType.DMA((count * Gather.SEMS,)),
            pltpu.SemaphoreType.DMA((count,)),
        ]
        params.update(collective_id=1, has_side_effects=True)
    else:
        ins = list(full)
        in_specs += [whole((8, model)), weight, weight, weight, whole((NB, LANES))]
    return pl.pallas_call(
        functools.partial(self_forward_kernel, joined),
        grid=(steps,),
        in_specs=in_specs,
        out_specs=out_specs,
        out_shape=out_shape,
        scratch_shapes=scratch,
        compiler_params=pltpu.CompilerParams(**params),
        cost_estimate=pl.CostEstimate(
            flops=6 * seq * model * model + 4 * seq * seq * model,
            bytes_accessed=2 * H * seq * seq + 16 * seq * model,
            transcendentals=H * seq * seq,
        ),
        name="self_forward",
    )(length, x, *ins)


def middle_kernel(joined, length_ref, gain_ref, *refs):
    (x_hbm, o_hbm, cot_hbm, enc_hbm, wo_hbm, cq_hbm, ck_hbm, cv_hbm, co_hbm), refs = (
        refs[:9], refs[9:]
    )
    wide_hbm, refs = refs[0], refs[1:]
    (out_hbm, g1_hbm, egrad_ref, gain_grad_ref), refs = refs[:4], refs[4:]
    squares, refs = refs[:5], refs[5:]
    sum_ref, refs = refs[0], refs[1:]
    if joined:
        wide_hbm, refs = refs[0], refs[1:]
    (
        xr_ref, o_ref, g_ref, a2_ref, cq_scr, mix_ref, a3_ref, r_ref, du_ref, prob_ref,
        x1_ref, x2_ref, acc_ref, dy_ref, enc_ref, keys_ref, values_ref, dk_acc, dv_acc,
        wo_ref, cq_ref, ck_ref, cv_ref, co_ref, wide_ref, src_ref, load_sem, wide_sem, out_sem,
    ), refs = refs[:29], refs[29:]
    seq, model = xr_ref.shape
    blocks = seq // ROWS
    pairs = model // LANES
    zero = jnp.zeros((), BF16)
    gain_cross = gain_ref[1:2, :]
    gain_ffn = gain_ref[2:3, :]

    loads = [
        pltpu.make_async_copy(src, dst, load_sem.at[i])
        for i, (src, dst) in enumerate(
            (
                (enc_hbm, enc_ref), (ck_hbm, ck_ref), (cv_hbm, cv_ref), (o_hbm, o_ref),
                (wo_hbm, wo_ref), (x_hbm, xr_ref), (cq_hbm, cq_ref), (cot_hbm, g_ref),
                (co_hbm, co_ref),
            )
        )
    ]
    for copy in loads:
        copy.start()

    chunk_rows = wide_ref.shape[2]

    def wide_loads(k):
        slot = lax.rem(k, 2)
        found = []
        for m in range(2):
            dst = wide_ref.at[slot, m]
            if joined:
                src = wide_hbm.at[k, m].reshape(chunk_rows, model)
            else:
                src = wide_hbm.at[m, k]
            found.append(pltpu.make_async_copy(src, dst, wide_sem.at[slot, m]))
        return found

    if joined:
        held, l1a, l1b, l2a, l2b, l3, rsend, rrecv, gsend, grecv = refs
        gather_link = Link(gsend, grecv)
        reduce_link = Link(rsend, rrecv)
        place = Place()
        part = chunk_rows // (SIDE_DP * SIDE_FSDP)

        def incoming(k):
            return [
                Gather(
                    None, wide_hbm.at[k, m], gather_link, None, place,
                    (2 * k + m) * Gather.SEMS,
                )
                for m in range(2)
            ]

        def leaving(k):
            at = pl.multiple_of(k * part, 8)
            found = []
            for m in range(2):
                i = 2 * k + m
                found.append(
                    Reduce(
                        src_ref.at[m], sum_ref.at[m, pl.ds(at, part)], None, held.at[i],
                        l1a.at[i], l1b.at[i], l2a.at[i], l2b.at[i], l3.at[i], reduce_link, None,
                        place, i * Reduce.SEMS,
                    )
                )
            return found

    def arriving(k, wait=(), start=(), when=None):
        if not joined:
            return

        def go():
            for piece in incoming(k):
                for round_idx in wait:
                    piece.arrive(round_idx)
            for piece in incoming(k):
                for round_idx in start:
                    piece.start(round_idx)

        go() if when is None else pl.when(when)(go)

    def reduce_stage(k, stage, when=None):
        if not joined:
            return

        def go():
            for piece in leaving(k):
                piece.stage(stage)

        go() if when is None else pl.when(when)(go)

    if joined:
        greet_peers()
        arriving(0, start=(2, 4))
        arriving(1, start=(1, 3))
    else:
        for copy in wide_loads(0):
            copy.start()

    for copy in loads[:3]:
        copy.wait()
    keys_ref[...] = nn(enc_ref[...], ck_ref[...]).astype(BF16)
    values_ref[...] = nn(enc_ref[...], cv_ref[...]).astype(BF16)
    dk_acc[...] = jnp.zeros_like(dk_acc)
    dv_acc[...] = jnp.zeros_like(dv_acc)
    gain_grad_ref[...] = jnp.zeros_like(gain_grad_ref)
    for copy in loads[3:]:
        copy.wait()

    def forward_rows(i, _):
        rows = pl.ds(pl.multiple_of(i * ROWS, ROWS), ROWS)
        pos = i * ROWS + lax.broadcasted_iota(jnp.int32, (ROWS, 1), 0)
        valid = jnp.where(pos < length_ref[0], 1.0, 0.0).astype(F32)
        if joined:

            arriving(0, wait=(2,), start=(5,), when=i == 3)

        x1 = xr_ref[rows, :].astype(F32) + nn(o_ref[rows, :], wo_ref[...])
        x1_ref[rows, :] = x1
        unit2, _inv2 = unit_rows(x1)
        a2 = (unit2 * gain_cross).astype(BF16)
        a2_ref[rows, :] = a2
        cq = nn(a2, cq_ref[...]).astype(BF16)
        cq_scr[rows, :] = cq
        mixed = []
        for pair in range(pairs):
            cols = slice(pair * LANES, (pair + 1) * LANES)
            total_out = None
            for which in range(2):
                own = head_lane((ROWS, LANES), which)
                own_key = head_lane((keys_ref.shape[0], LANES), which)
                scores = nt(jnp.where(own, cq[:, cols], zero), keys_ref[:, cols])
                top = jnp.max(scores, axis=1, keepdims=True)
                weights = jnp.exp(scores - top)
                prob = (weights * (1.0 / jnp.sum(weights, axis=1, keepdims=True))).astype(BF16)
                at = (2 * pair + which) * keys_ref.shape[0]
                prob_ref[rows, at : at + keys_ref.shape[0]] = prob
                piece = nn(prob, jnp.where(own_key, values_ref[:, cols], zero))
                total_out = piece if total_out is None else total_out + piece
            mixed.append(total_out.astype(BF16))
        mix = jnp.concatenate(mixed, axis=1)
        mix_ref[rows, :] = mix
        x2 = x1 + nn(mix, co_ref[...])
        x2_ref[rows, :] = x2
        acc_ref[rows, :] = x2
        unit3, _inv3 = unit_rows(x2)
        a3_ref[rows, :] = (unit3 * gain_ffn).astype(BF16)
        g_ref[rows, :] = (g_ref[rows, :].astype(F32) * valid).astype(BF16)
        return 0

    lax.fori_loop(0, blocks, forward_rows, 0)

    def chunk(k, _):
        slot = lax.rem(k, 2)
        for copy in wide_loads(k):
            copy.wait()
        for i in range(blocks):
            rows = slice(i * ROWS, (i + 1) * ROWS)
            z = nt(a3_ref[rows, :], wide_ref[slot, 0])
            zz = z * z
            t = jnp.tanh(GELU_C * z * (1.0 + GELU_A * zz))
            half = 0.5 + 0.5 * t
            r = (z * half).astype(BF16)
            r_ref[rows, :] = r
            slope = half + (0.5 * GELU_C) * z * (1.0 - t * t) * (1.0 + (3.0 * GELU_A) * zz)
            du = (nt(g_ref[rows, :], wide_ref[slot, 1]) * slope).astype(BF16)
            du_ref[rows, :] = du
            acc_ref[rows, :] += nn(r, wide_ref[slot, 1])
            dy_ref[rows, :] += nn(du, wide_ref[slot, 0])
            if i == 1:
                arriving(2, wait=(2,), start=(5,), when=k == 1)
        arriving(1, wait=(2,), start=(5,), when=k == 0)
        arriving(2, wait=(1,), start=(2, 4), when=k == 0)
        reduce_stage(k - 1, 1, k >= 1)
        reduce_stage(k - 2, 2, k >= 2)

        @pl.when(k >= 1)
        def _():
            if joined:
                for piece in leaving(k - 1):
                    piece.sent(0)
            else:
                for copy in grad_copies(k - 1):
                    copy.wait()

        def next_loads():
            for copy in wide_loads(k + 1):
                copy.start()

        if not joined:
            pl.when(k + 1 < CHUNKS)(next_loads)
        shape = src_ref.shape[1:]
        src_ref[0] = tn(du_ref[...], a3_ref[...]).reshape(shape).astype(BF16)
        src_ref[1] = tn(r_ref[...], g_ref[...]).reshape(shape).astype(BF16)
        if joined:
            reduce_stage(k, 0)
            arriving(k + 1, wait=(3, 4, 5), when=k + 1 < CHUNKS)
            pl.when(k + 1 < CHUNKS)(next_loads)
        else:
            for copy in grad_copies(k):
                copy.start()
        return 0

    def grad_copies(k):
        return [
            pltpu.make_async_copy(src_ref.at[m], sum_ref.at[m, k], out_sem.at[m])
            for m in range(2)
        ]

    dy_ref[...] = jnp.zeros_like(dy_ref)
    if joined:
        arriving(0, wait=(4, 5))
        for copy in wide_loads(0):
            copy.start()
        arriving(1, wait=(1,), start=(2, 4))
        arriving(2, start=(1, 3))
    lax.fori_loop(0, CHUNKS, chunk, 0)

    g1_low_ref = a3_ref
    g2_low_ref = g_ref
    dcq_ref = cq_scr
    final = CHUNKS - 1

    def out_copies(rows):
        return [
            pltpu.make_async_copy(acc_ref.at[rows, :], out_hbm.at[rows, :], out_sem.at[0]),
            pltpu.make_async_copy(dy_ref.at[rows, :], g1_hbm.at[rows, :], out_sem.at[1]),
        ]

    if not joined:
        for copy in grad_copies(final):
            copy.wait()

    def backward_rows(i, _):
        rows = pl.ds(pl.multiple_of(i * ROWS, ROWS), ROWS)
        for at, k, stage in ((0, 1, 2), (1, 0, 3), (1, 2, 1), (2, 1, 3), (3, 0, 4), (3, 2, 2)):
            reduce_stage(k, stage, i == at)
        pos = i * ROWS + lax.broadcasted_iota(jnp.int32, (ROWS, 1), 0)
        valid = jnp.where(pos < length_ref[0], 1.0, 0.0).astype(F32)
        acc_ref[rows, :] = acc_ref[rows, :] * valid
        unit3, inv3 = unit_rows(x2_ref[rows, :])
        through, gain_part = norm_back(dy_ref[rows, :], unit3, inv3, gain_ffn)
        gain_grad_ref[1:2, :] += gain_part
        g2 = g_ref[rows, :].astype(F32) + through
        g2_low = g2.astype(BF16)
        g2_low_ref[rows, :] = g2_low
        dmix = nt(g2_low, co_ref[...]).astype(BF16)
        cq = cq_scr[rows, :]
        dq_parts = []
        for pair in range(pairs):
            cols = slice(pair * LANES, (pair + 1) * LANES)
            dq = None
            for which in range(2):
                own = head_lane((ROWS, LANES), which)
                own_key = head_lane((keys_ref.shape[0], LANES), which)
                at = (2 * pair + which) * keys_ref.shape[0]
                prob_low = prob_ref[rows, at : at + keys_ref.shape[0]]
                prob = prob_low.astype(F32)
                d_out = jnp.where(own, dmix[:, cols], zero)
                dp = nt(d_out, values_ref[:, cols])
                ds = prob * (dp - jnp.sum(prob * dp, axis=1, keepdims=True))
                ds_low = ds.astype(BF16)
                dv_acc[:, cols] += tn(prob_low, d_out)
                dk_acc[:, cols] += tn(ds_low, jnp.where(own, cq[:, cols], zero))
                piece = nn(ds_low, jnp.where(own_key, keys_ref[:, cols], zero))
                dq = piece if dq is None else dq + piece
            dq_parts.append(dq.astype(BF16))
        dcq = jnp.concatenate(dq_parts, axis=1)
        dcq_ref[rows, :] = dcq
        unit2, inv2 = unit_rows(x1_ref[rows, :])
        through, gain_part = norm_back(nt(dcq, cq_ref[...]), unit2, inv2, gain_cross)
        gain_grad_ref[0:1, :] += gain_part
        g1 = g2 + through
        dy_ref[rows, :] = g1
        g1_low_ref[rows, :] = g1.astype(BF16)
        for copy in out_copies(rows):
            copy.start()
        return 0

    lax.fori_loop(0, blocks, backward_rows, 0)

    reduce_stage(final - 1, 4)
    reduce_stage(final, 3)
    dk = dk_acc[...].astype(BF16)
    dv = dv_acc[...].astype(BF16)
    egrad_ref[...] = nt(dk, ck_ref[...]) + nt(dv, cv_ref[...])
    made = (
        (cq_ref, lambda: tn(a2_ref[...], dcq_ref[...])),
        (ck_ref, lambda: tn(enc_ref[...], dk)),
        (cv_ref, lambda: tn(enc_ref[...], dv)),
        (co_ref, lambda: tn(mix_ref[...], g2_low_ref[...])),
        (wo_ref, lambda: tn(o_ref[...], g1_low_ref[...])),
    )
    writes = []
    for i, (buffer, make) in enumerate(made):
        buffer[...] = make().astype(BF16)
        writes.append(pltpu.make_async_copy(buffer, squares[i], load_sem.at[i]))
        writes[-1].start()
    reduce_stage(final, 4)
    for copy in writes:
        copy.wait()
    for i in range(blocks):
        for copy in out_copies(pl.ds(i * ROWS, ROWS)):
            copy.wait()
    if joined:
        for k, rounds in enumerate(((2, 4, 5), (1, 2, 3, 4, 5), (1, 2, 3, 4, 5))):
            for piece in incoming(k):
                for round_idx in rounds:
                    piece.sent(round_idx)
        for k in range(CHUNKS):
            for piece in leaving(k):
                for round_idx in (0, 1, 2, 3) if k == final else (1, 2, 3):
                    piece.sent(round_idx)


def middle(length, x, o, cot, enc, gains, wo, cq, ck, cv, co, wide, joined):
    seq, model = x.shape
    enc_len = enc.shape[0]
    anywhere = pl.BlockSpec(memory_space=pl.ANY)
    vmem = pl.BlockSpec(memory_space=pltpu.VMEM)
    smem = pl.BlockSpec(memory_space=pltpu.SMEM)
    low = lambda *shape: pltpu.VMEM(shape, BF16)
    full = lambda *shape: pltpu.VMEM(shape, F32)
    ins = [x, o, cot, enc, wo, cq, ck, cv, co, wide]
    square = jax.ShapeDtypeStruct((model, model), BF16)
    out_shape = [
        jax.ShapeDtypeStruct((seq, model), F32),
        jax.ShapeDtypeStruct((seq, model), F32),
        jax.ShapeDtypeStruct((enc_len, model), F32),
        jax.ShapeDtypeStruct((2, model), F32),
    ] + [square] * 5
    out_specs = [anywhere, anywhere, vmem, vmem] + [anywhere] * 5
    hidden = 4 * model
    chunk_rows = hidden // CHUNKS
    rows_low = [low(seq, model)] * 7 + [low(seq, chunk_rows)] * 2
    params = dict(vmem_limit_bytes=63 * 1024 * 1024)
    if joined:
        part = chunk_rows // (SIDE_DP * SIDE_FSDP)
        lead = (SIDE_DP, 2, 2, 2)
        out_shape += [
            jax.ShapeDtypeStruct((2, CHUNKS * part, model), F32),
            jax.ShapeDtypeStruct(wide.shape, BF16),
        ]
        out_specs += [vmem, anywhere]
        gather_sems = 2 * CHUNKS * Gather.SEMS
        aliases = {2 + len(ins) - 1: len(out_shape) - 1}
        src = low(2, *lead, part, model)
        count = 2 * CHUNKS
        reduce_sems = count * Reduce.SEMS
        extra = [
            pltpu.VMEM((count,) + buffer.shape, BF16) for buffer in Reduce.scratch(part, model)
        ] + [
            pltpu.SemaphoreType.DMA((reduce_sems,)), pltpu.SemaphoreType.DMA((reduce_sems,)),
            pltpu.SemaphoreType.DMA((gather_sems,)), pltpu.SemaphoreType.DMA((gather_sems,)),
        ]
        params.update(collective_id=2, has_side_effects=True)
    else:
        out_shape += [jax.ShapeDtypeStruct((2, CHUNKS, chunk_rows, model), BF16)]
        out_specs += [anywhere]
        src = low(2, chunk_rows, model)
        extra = []
        aliases = {}
    return pl.pallas_call(
        functools.partial(middle_kernel, joined),
        in_specs=[smem, vmem] + [anywhere] * len(ins),
        out_specs=out_specs,
        out_shape=out_shape,
        scratch_shapes=rows_low
        + [
            low(seq, H * enc_len), full(seq, model), full(seq, model), full(seq, model),
            full(seq, model), low(enc_len, model), low(enc_len, model), low(enc_len, model),
            full(enc_len, model), full(enc_len, model),
        ]
        + [low(model, model)] * 5
        + [
            low(2, 2, chunk_rows, model), src,
            pltpu.SemaphoreType.DMA((9,)), pltpu.SemaphoreType.DMA((2, 2)),
            pltpu.SemaphoreType.DMA((2,)),
        ]
        + extra,
        input_output_aliases=aliases,
        compiler_params=pltpu.CompilerParams(**params),
        name="middle",
    )(length, gains, *ins)


def gather_weights(shards, axes):
    pile = lax.all_gather(jnp.concatenate(shards, axis=0), axes, axis=0)
    full, at = [], 0
    for shard in shards:
        full.append(pile[:, at : at + shard.shape[0]].reshape(-1, pile.shape[-1]))
        at += shard.shape[0]
    return full


def reduce_grads(grads, axes):
    dev_count = lax.axis_size("dp") * lax.axis_size("fsdp")
    split = [g.reshape(dev_count, -1, g.shape[-1]) for g in grads]
    pile = lax.psum_scatter(
        jnp.concatenate(split, axis=1), axes, scatter_dimension=0, tiled=False
    ).astype(F32)
    sums, at = [], 0
    for s in split:
        sums.append(pile[at : at + s.shape[1]])
        at += s.shape[1]
    return sums


HIST = 2 * LANES


def self_backward_kernel(
    far_count, x_ref, gain_ref, mid_gain_ref, a_ref, g1_ref, q_ref, k_ref, v_ref, p_ref,
    wo_ref, wq_ref, wk_ref, wv_ref, *refs,
):
    joined = far_count is not None
    if joined:
        far_refs = refs[:far_count]
        ingrad_ref, sum_ref, near_sum_ref, small_ref, table_ref = refs[far_count : far_count + 5]
        rest = refs[far_count + 5 :]
    else:
        ingrad_ref, gw_ref, small_ref, hist_out = refs[:4]
        rest = refs[4:]
    low_ref, near_acc, dk_acc, dv_acc, dq_scr, hist_ref = rest[:6]
    rest = rest[6:]
    step = pl.program_id(0)
    last = pl.num_programs(0) - 1
    seq, model = x_ref.shape
    width = wq_ref.shape[1]
    heads = width // DH
    steps = model // width
    events = {}
    if joined:
        src_ref, own_ref, near_small, far_small, send, recv, local = rest[-7:]
        link = Link(send, recv)
        part = sum_ref.shape[0] // far_count
        pieces = []
        for i in range(far_count + steps):
            far = i < far_count
            pieces.append(
                Reduce(
                    far_refs[i] if far else src_ref.at[(i - far_count) % 2],
                    (sum_ref if far else near_sum_ref).at[
                        (i if far else i - far_count) * part
                        : (i + 1 if far else i + 1 - far_count) * part
                    ],
                    own_ref.at[i] if far else None,
                    *rest[Reduce.BUFFERS * i : Reduce.BUFFERS * (i + 1)], link,
                    local.at[i], early=far_count <= i < far_count + steps - 2,
                )
            )
        small = SumSmall(small_ref, near_small, far_small, link)
        far_times = [(0, 1, 3, 4, 6)] * 3 + [(0, 2, 4, 5, 7)] * (far_count - 3)
        near_times = [(2, 3, 5, 6), (3, 4, 6, 7), (4, 5, 6, 7), (5, 6, 7, 8)]
        near_times += [(6, 7, 8, 9)] * (steps - len(near_times))
        for i in range(far_count):
            for k, time in enumerate(far_times[i]):
                events.setdefault(time, []).append((-k, pieces[i]))
        for i in range(steps):
            for k, time in enumerate(near_times[i]):
                events.setdefault(time, []).append((-k - 1, pieces[far_count + i]))

    def tick(time):
        for k, piece in sorted(events.get(time, []), key=lambda event: event[0]):
            piece.stage(-k)

    @pl.when(step == 0)
    def _():
        if joined:
            greet_peers()
            tick(0)
        low_ref[...] = g1_ref[...].astype(BF16)
        ingrad_ref[...] = jnp.zeros_like(ingrad_ref)
        hist_ref[...] = jnp.zeros_like(hist_ref)

    for g in range(1, steps):
        if events.get(g):
            pl.when(step == g)(functools.partial(tick, g))

    d_all = nt(low_ref[...], wo_ref[...]).astype(BF16)
    zero = jnp.zeros((), BF16)
    for pair in range(width // LANES):
        cols = slice(pair * LANES, (pair + 1) * LANES)
        dk_acc[...] = jnp.zeros_like(dk_acc)
        dv_acc[...] = jnp.zeros_like(dv_acc)
        dq_blocks = [None] * (seq // ROWS)
        for which in range(2):
            local_head = pair * 2 + which
            head = step * heads + local_head
            own = head_lane((seq, LANES), which)
            d_out = jnp.where(own, d_all[:, cols], zero)
            queries = jnp.where(own, q_ref[:, cols], zero)
            keys = jnp.where(own, k_ref[:, cols], zero)
            for blk in range(seq // ROWS):
                rows = slice(blk * ROWS, (blk + 1) * ROWS)
                span = (blk + 1) * ROWS
                prob_low = p_ref[local_head, rows, :span]
                prob = prob_low.astype(F32)
                dp = nt(d_out[rows], v_ref[:span, cols])
                ds = prob * (dp - jnp.sum(prob * dp, axis=1, keepdims=True))
                if blk == 0:
                    near_acc[:, :LANES] = jnp.zeros((ROWS, LANES), F32)
                    near_acc[:, LANES:] = ds
                else:
                    near_acc[...] += ds[:, span - ROWS - LANES :]
                ds_low = ds.astype(BF16)
                part_q = nn(ds_low, keys[:span])
                dq_blocks[blk] = part_q if which == 0 else dq_blocks[blk] + part_q
                dk_acc[:span, :] += tn(ds_low, queries[rows])
                dv_acc[:span, :] += tn(prob_low, d_out[rows])
            padded = jnp.concatenate([near_acc[...], jnp.zeros((ROWS, LANES), F32)], axis=1)
            count = ROWS
            while count > 1:
                count //= 2
                padded = padded[:count] + pltpu.roll(padded[count:], 4 * LANES - count, 1)
            hist_ref[pl.ds(head, 1), :] = padded[:, :HIST]
        for blk in range(seq // ROWS):
            rows = slice(blk * ROWS, (blk + 1) * ROWS)
            dq_scr[rows, cols] = dq_blocks[blk].astype(BF16)
        dq_scr[:, width + pair * LANES : width + (pair + 1) * LANES] = dk_acc[...].astype(BF16)
        dq_scr[:, 2 * width + pair * LANES : 2 * width + (pair + 1) * LANES] = dv_acc[
            ...
        ].astype(BF16)

    grads = tn(a_ref[...], dq_scr[...])
    if joined:
        for g in range(steps):

            @pl.when(step == g)
            def _():
                if g >= 2:
                    pieces[far_count + g - 2].sent(0)
                src_ref[g % 2] = grads.reshape(src_ref.shape[1:]).astype(BF16)
                pieces[far_count + g].stage(0)
                if g == steps - 1:
                    tick(steps)
    else:
        gw_ref[0] = grads.astype(BF16)
    weights = jnp.concatenate([wq_ref[...], wk_ref[...], wv_ref[...]], axis=1)
    ingrad_ref[...] += nt(dq_scr[...], weights)

    @pl.when(step == last)
    def _():
        unit, inv = unit_rows(x_ref[...].astype(F32))
        through, gain_part = norm_back(ingrad_ref[...], unit, inv, gain_ref[...])
        small_ref[...] = jnp.zeros_like(small_ref)
        small_ref[0:1, :model] = gain_part
        small_ref[1:3, :model] = mid_gain_ref[...]
        small_ref[:, model : model + HIST] = hist_ref[0:8, :]
        small_ref[:, model + HIST :] = hist_ref[8:16, :]
        if joined:
            small.stage(0)
            tick(steps + 1)
            small.stage(1)
        ingrad_ref[...] = g1_ref[...] + through
        if joined:
            small.stage(2)
            tick(steps + 2)
            small.stage(3)
            small.stage(4)
            z, y, x, c = coords()
            mine = z * SIDE_FSDP + y * 4 + x * 2 + c
            lane = lax.broadcasted_iota(jnp.int32, (16, HIST), 1)
            distance = LANES - lane
            bucket = bucket_of(jnp.maximum(distance, 0))
            usable = (distance >= 0) & (bucket < NB - 1)
            picked = usable & ((bucket == mine) | (mine == NB - 1))
            sign = jnp.where(mine == NB - 1, -1.0, 1.0)
            hist = jnp.concatenate(
                [small_ref[:, model : model + HIST], small_ref[:, model + HIST :]], axis=0
            )
            column = sign * jnp.sum(jnp.where(picked, hist, 0.0), axis=1, keepdims=True)
            table_ref[...] = jnp.broadcast_to(column, table_ref.shape)
            tick(steps + 3)
            link.drain()
        else:
            hist_out[...] = hist_ref[...]


def self_backward(x, gain, mid_gain, a1, g1, q, k, v, p, wo, wq, wk, wv, far_grads):
    seq, model = x.shape
    width = 128
    heads = width // DH
    steps = model // width
    joined = far_grads is not None
    held = lambda shape: pl.BlockSpec(
        shape, lambda i: (0,) * len(shape), pipeline_mode=pl.Buffered(1)
    )
    whole = lambda shape: pl.BlockSpec(shape, lambda i: (0,) * len(shape))
    columns = pl.BlockSpec((seq, width), lambda i: (0, i))
    weight = pl.BlockSpec((model, width), lambda i: (0, i))
    weight_rows = pl.BlockSpec((width, model), lambda i: (i, 0))
    in_specs = [
        held((seq, model)), held((1, model)), held((2, model)), held((seq, model)),
        held((seq, model)), columns, columns, columns,
        pl.BlockSpec((heads, seq, seq), lambda i: (i, 0, 0)),
        weight_rows, weight, weight, weight,
    ]
    small = (8, model + 2 * HIST)
    out_specs = [whole((seq, model))]
    out_shape = [jax.ShapeDtypeStruct((seq, model), F32)]
    scratch = [
        pltpu.VMEM((seq, model), BF16),
        pltpu.VMEM((ROWS, ROWS + LANES), F32),
        pltpu.VMEM((seq, LANES), F32),
        pltpu.VMEM((seq, LANES), F32),
        pltpu.VMEM((seq, 3 * width), BF16),
        pltpu.VMEM((16, HIST), F32),
    ]
    extra = []
    params = dict(vmem_limit_bytes=63 * 1024 * 1024)
    if joined:
        count = len(far_grads)
        part = model // (SIDE_DP * SIDE_FSDP)
        across = 3 * width
        extra = [g.reshape(SIDE_DP, 2, 2, 2, part, model) for g in far_grads]
        in_specs += [pl.BlockSpec(memory_space=pl.ANY)] * count
        shapes = ((count * part, model), (steps * part, across), small, (16, LANES))
        out_specs += [whole(s) for s in shapes]
        out_shape += [jax.ShapeDtypeStruct(s, F32) for s in shapes]
        for i in range(count + steps):
            scratch += Reduce.scratch(part, model if i < count else across)
        sems = (count + steps) * Reduce.SEMS + SumSmall.SEMS
        scratch += [
            pltpu.VMEM((2, SIDE_DP, 2, 2, 2, part, across), BF16),
            pltpu.VMEM((count, SIDE_DP, 2, 2, part, model), BF16),
            pltpu.VMEM((3,) + small, F32),
            pltpu.VMEM((SIDE_DP - 1,) + small, F32),
            pltpu.SemaphoreType.DMA((sems,)), pltpu.SemaphoreType.DMA((sems,)),
            pltpu.SemaphoreType.DMA((count + steps,)),
        ]
        params.update(collective_id=3, has_side_effects=True)
    else:
        count = None
        out_specs += [
            pl.BlockSpec((1, model, 3 * width), lambda i: (i, 0, 0)), whole(small),
            whole((16, HIST)),
        ]
        out_shape += [
            jax.ShapeDtypeStruct((steps, model, 3 * width), BF16),
            jax.ShapeDtypeStruct(small, F32),
            jax.ShapeDtypeStruct((16, HIST), F32),
        ]
    return pl.pallas_call(
        functools.partial(self_backward_kernel, count),
        grid=(steps,),
        in_specs=in_specs,
        out_specs=out_specs,
        out_shape=out_shape,
        scratch_shapes=scratch,
        compiler_params=pltpu.CompilerParams(**params),
        cost_estimate=pl.CostEstimate(
            flops=14 * seq * model * model + 8 * seq * seq * model,
            bytes_accessed=2 * H * seq * seq + 24 * seq * model,
            transcendentals=0,
        ),
        name="self_backward",
    )(x, gain, mid_gain, a1, g1, q, k, v, p, wo, wq, wk, wv, *extra)


def body(
    tokens, encoder_states, lengths, dealing, cotangent,
    w_query, w_key, w_value, w_out, c_query, c_key, c_value, c_out, w_in, w_down,
    gain_self, gain_cross, gain_ffn, bias_table,
):
    axes = ("dp", "fsdp")
    fsdp_size = lax.axis_size("fsdp")
    dp_size = lax.axis_size("dp")
    dev_count = dp_size * fsdp_size
    dp_index = lax.axis_index("dp")
    own = dp_index * fsdp_size + lax.axis_index("fsdp")
    seq_len, model = tokens.shape[1:]
    route = [(a, a ^ 1) for a in range(dp_size)]

    x = tokens[0]
    cot = cotangent[0]
    in_place = lax.dynamic_slice_in_dim(dealing, own, 1) == own
    enc_other = lax.ppermute(encoder_states[0], "dp", route)
    enc = jnp.where(in_place[:, None], encoder_states[0], enc_other)
    length = lax.dynamic_slice_in_dim(lengths, own, 1)

    gain_part = gain_self.shape[0]
    joined = dp_size == SIDE_DP and fsdp_size == SIDE_FSDP
    in_rows = w_in.T
    column = jnp.arange(model, dtype=jnp.int32)[None, :]
    gain_rows = jnp.stack(
        [jnp.tile(g, model // gain_part) for g in (gain_self, gain_cross, gain_ffn)]
    )
    gain_rows = jnp.where(column // gain_part == own, gain_rows, jnp.zeros((), BF16))
    table_row = jnp.pad(bias_table, (0, model - bias_table.shape[0]))[None, :]
    small = jnp.pad(jnp.concatenate([gain_rows, table_row], axis=0), ((0, 4), (0, 0)))
    if joined:
        done = self_forward(
            length, x,
            [
                w_query, w_key, w_value, small, w_out, c_query, c_key, c_value, c_out, in_rows,
                w_down,
            ],
            None,
        )
        q, k, v, o, p, a1, wq, wk, wv, gains = done[:10]
        wo, cq, ck, cv, co = (w.reshape(model, model) for w in done[10:15])
        wide = done[15]
    else:
        wq, wk, wv, small_all, wo, cq, ck, cv, co, win_t, wdown = gather_weights(
            [
                w_query, w_key, w_value, small, w_out, c_query, c_key, c_value, c_out, in_rows,
                w_down,
            ],
            axes,
        )
        wide = jnp.stack([w.reshape(CHUNKS, -1, model) for w in (win_t, wdown)])
        small_all = small_all.reshape(dev_count, 8, model).astype(F32)
        gains = jnp.sum(small_all, axis=0)
        table = small_all[:, 3, : bias_table.shape[0]].reshape(NB, H)
        table = jnp.pad(table, ((0, 0), (0, LANES - H)))
        q, k, v, o, p, a1 = self_forward(length, x, None, [gains, wq, wk, wv, table])
    done = middle(length, x, o, cot, enc, gains, wo, cq, ck, cv, co, wide, joined)
    out, g1, egrad, mid_gain_grad = done[:4]
    squares = list(done[4:9])
    if joined:
        sum_in, sum_down = done[9][0], done[9][1]
    else:
        sum_in, sum_down = reduce_grads([g.reshape(-1, model) for g in done[9]], axes)
    done = self_backward(
        x, gains[0:1], mid_gain_grad, a1, g1, q, k, v, p, wo, wq, wk, wv,
        squares if joined else None,
    )
    in_grad = done[0]
    if joined:
        sums, near_sums, small, table_column = done[1:]
        part = w_query.shape[0]
        sum_cq, sum_ck, sum_cv, sum_co, sum_wo = (
            sums[i * part : (i + 1) * part] for i in range(5)
        )
        steps = near_sums.shape[0] // part
        across = model // steps
        sum_wq, sum_wk, sum_wv = (
            jnp.concatenate(
                [
                    near_sums[g * part : (g + 1) * part, i * across : (i + 1) * across]
                    for g in range(steps)
                ],
                axis=1,
            )
            for i in range(3)
        )
        ends = lax.dynamic_slice(small, (0, own * gain_part), (3, gain_part))
        end_self, end_cross, end_ffn = ends[0], ends[1], ends[2]
        end_table = table_column[:H, 0]
    else:
        gw, small, hist = done[1:]
        g_wq, g_wk, g_wv = (
            jnp.concatenate(
                [g[:, i * LANES : (i + 1) * LANES] for g in gw], axis=1
            )
            for i in range(3)
        )
        distance = jnp.arange(LANES, dtype=jnp.int32)
        bucket_hot = bucket_of(distance)[:, None] == jnp.arange(NB, dtype=jnp.int32)[None, :]
        near_hot = bucket_hot.astype(F32) * (jnp.arange(NB) < NB - 1).astype(F32)
        by_dist = hist[:H, 1 : LANES + 1][:, ::-1]
        near_sums = jnp.dot(near_hot.T, by_dist.T, precision=lax.Precision.HIGHEST)
        grad_table = jnp.where(
            (jnp.arange(NB) < NB - 1)[:, None],
            near_sums, -jnp.sum(near_sums, axis=0, keepdims=True),
        )
        small_grads = jnp.concatenate(
            [small[i, :model].reshape(dev_count, -1) for i in range(3)]
            + [grad_table.reshape(dev_count, -1)],
            axis=1,
        )
        small_count = small_grads.shape[1]
        small_low = jnp.pad(small_grads.astype(BF16), ((0, 0), (0, model - small_count)))
        small_low = jnp.pad(small_low[:, None, :], ((0, 0), (0, 7), (0, 0))).reshape(-1, model)
        sum_cq, sum_ck, sum_cv, sum_co, sum_wo, sum_wq, sum_wk, sum_wv, sum_small = reduce_grads(
            squares + [g_wq, g_wk, g_wv, small_low], axes
        )
        ends = sum_small[0]
        end_self, end_cross, end_ffn = (
            ends[i * gain_part : (i + 1) * gain_part] for i in range(3)
        )
        end_table = ends[3 * gain_part : small_count]

    egrad_other = lax.ppermute(egrad, "dp", route)
    encoder_grad = jnp.where(in_place[:, None], egrad, egrad_other)
    return (
        out[None], in_grad[None], encoder_grad[None],
        sum_wq, sum_wk, sum_wv, sum_wo, sum_cq, sum_ck, sum_cv, sum_co, sum_in.T, sum_down,
        end_self, end_cross, end_ffn, end_table,
    )


def solution(mesh):
    rows3 = P(("dp", "fsdp"), None, None)
    rows2 = P(("dp", "fsdp"), None)
    cols2 = P(None, ("dp", "fsdp"))
    line = P(("dp", "fsdp"))
    in_specs = (
        (rows3, rows3, P(), P(), rows3) + (rows2,) * 8 + (cols2, rows2) + (line,) * 4
    )
    out_specs = (rows3,) * 3 + (rows2,) * 8 + (cols2, rows2) + (line,) * 4
    return jax.shard_map(body, mesh=mesh, in_specs=in_specs, out_specs=out_specs, check_vma=False)
```

```python
import functools
import math

import jax
import jax.numpy as jnp
from jax import lax
from jax.experimental import pallas as pl
from jax.experimental.pallas import tpu as pltpu
from jax.sharding import PartitionSpec as P

H = 12
DH = 64
NB = 32
MAXDIST = 128
EPSILON = 1e-06
MASKED = -1e30
LANES = 128
CHUNKS = 3
ROWS = 256
F32 = jnp.float32
BF16 = jnp.bfloat16
GELU_C = math.sqrt(2.0 / math.pi)
GELU_A = 0.044715


def bucket_of(distance):
    exact_count = NB // 2
    bucket = jnp.minimum(distance, exact_count)
    for level_idx in range(1, exact_count):
        threshold = int(
            math.ceil(exact_count * (MAXDIST / exact_count) ** (level_idx / exact_count))
        )
        bucket = bucket + (distance >= threshold).astype(jnp.int32)
    return bucket


def nn(left_op, right_op):
    return lax.dot_general(
        left_op, right_op, (((1,), (0,)), ((), ())), preferred_element_type=F32
    )


def nt(left_op, right_op):
    return lax.dot_general(
        left_op, right_op, (((1,), (1,)), ((), ())), preferred_element_type=F32
    )


def tn(left_op, right_op):
    return lax.dot_general(
        left_op, right_op, (((0,), (0,)), ((), ())), preferred_element_type=F32
    )


def unit_rows(values_in):
    inv_rms = lax.rsqrt(jnp.mean(values_in * values_in, axis=-1, keepdims=True) + EPSILON)
    return values_in * inv_rms, inv_rms


def norm_back(grad_in, unit, inv_rms, gain_vec):
    scaled = grad_in * gain_vec
    through = inv_rms * (scaled - unit * jnp.mean(scaled * unit, axis=-1, keepdims=True))
    return through, jnp.sum(grad_in * unit, axis=0, keepdims=True)


def head_lane(shape, which):
    lane = lax.broadcasted_iota(jnp.int32, shape, len(shape) - 1)
    return (lane // DH) == which


SIDE_DP = 4
SIDE_FSDP = 8
MESH = pl.DeviceIdType.MESH


def coords():
    along = lax.axis_index("fsdp")
    return lax.axis_index("dp"), along // 4, lax.rem(along // 2, 2), lax.rem(along, 2)


def device(z, y, x, c):
    return (z, y * 4 + x * 2 + c)


def greet_peers():
    z, y, x, c = coords()
    peers = [device(lax.rem(z + k, SIDE_DP), y, x, c) for k in range(1, SIDE_DP)]
    peers += [device(z, y, 1 - x, c), device(z, 1 - y, x, c), device(z, y, x, 1 - c)]
    barrier = pltpu.get_barrier_semaphore()
    for peer in peers:
        pl.semaphore_signal(barrier, inc=1, device_id=peer, device_id_type=MESH)
    pl.semaphore_wait(barrier, len(peers))


def own_index():
    return lax.axis_index("dp") * SIDE_FSDP + lax.axis_index("fsdp")


class Link:
    def __init__(self, send, recv):
        self.send, self.recv, self.used, self.pieces = send, recv, 0, []

    def take(self, piece):
        self.pieces.append(piece)
        self.used += piece.SEMS
        return self.used - piece.SEMS

    def drain(self):
        for piece in self.pieces:
            piece.drain()


class Place:
    def __init__(self):
        z, y, x, c = self.at = coords()
        self.to_y = device(z, 1 - y, x, c)
        self.to_x = device(z, y, 1 - x, c)
        self.to_core = device(z, y, x, 1 - c)
        self.other_z = [lax.rem(z + k, SIDE_DP) for k in range(1, SIDE_DP)]
        self.to_z = [device(other, y, x, c) for other in self.other_z]
        self.ny, self.nx, self.nc = 1 - y, 1 - x, 1 - c


class Piece:
    def __init__(self, link, local, place=None, first=None):
        self.link, self.local = link, local
        self.first = link.take(self) if first is None else first
        self.half_a, self.half_b = slice(0, SIDE_DP // 2), slice(SIDE_DP // 2, SIDE_DP)
        place = place or Place()
        self.at, self.to_y, self.to_x, self.to_core = (
            place.at, place.to_y, place.to_x, place.to_core
        )
        self.other_z, self.to_z = place.other_z, place.to_z
        self.ny, self.nx, self.nc = place.ny, place.nx, place.nc

    def copy(self, slot, src, dst, peer):
        return pltpu.make_async_remote_copy(
            src_ref=src, dst_ref=dst, send_sem=self.link.send.at[self.first + slot],
            recv_sem=self.link.recv.at[self.first + slot], device_id=peer, device_id_type=MESH,
        )

    def start(self, k):
        for copy in self.moves(k):
            copy.start()

    def arrive(self, k):
        for copy in self.moves(k):
            copy.wait_recv()

    def sent(self, k):
        for copy in self.moves(k):
            copy.wait_send()

    def drain(self):
        for k in self.UNSENT:
            self.sent(k)

    def stage(self, k):
        (self.s0, self.s1, self.s2, self.s3, self.s4)[k]()


class Gather(Piece):
    SEMS = 13
    UNSENT = (0, 1, 2, 3, 4, 5)

    def __init__(self, src, out, link, local, place=None, first=None):
        super().__init__(link, local, place, first)
        self.src, self.out = src, out

    def moves(self, k):
        z, y, x, c = self.at
        out, a, b = self.out, self.half_a, self.half_b
        if k == 0:
            here = out.at[z, y, x, c]
            return [self.copy(i, self.src, here, peer) for i, peer in enumerate(self.to_z)]
        same = lambda slot, ref, peer: self.copy(slot, ref, ref, peer)
        if k == 1:
            return [
                same(3, out.at[a, y, x, c], self.to_x),
                same(4, out.at[b, y, x, c], self.to_y),
            ]
        if k == 2:
            return [
                same(5, out.at[a, y, :, c], self.to_y),
                same(6, out.at[b, :, x, c], self.to_x),
            ]
        if k == 3:
            return [same(7, out.at[:, y, x, c], self.to_core)]
        if k == 4:
            return [
                same(8, out.at[a, y, self.nx, c], self.to_core),
                same(9, out.at[b, self.ny, x, c], self.to_core),
            ]
        return [
            same(10, out.at[a, self.ny, :, c], self.to_core),
            same(11, out.at[b, :, self.nx, c], self.to_core),
        ]

    def keep(self):
        return pltpu.make_async_copy(self.src, self.out.at[self.at], self.local)

    def s0(self):
        self.start(0)
        self.keep().start()

    def s1(self):
        self.keep().wait()
        self.arrive(0)
        self.start(1)
        self.start(3)

    def s2(self):
        self.arrive(1)
        self.start(2)
        self.start(4)

    def s3(self):
        self.arrive(2)
        self.start(5)

    def s4(self):
        for k in (3, 4, 5):
            self.arrive(k)


class Reduce(Piece):
    SEMS = 8
    BUFFERS = 6

    def __init__(
        self, src, out, own, held, l1a, l1b, l2a, l2b, l3, link, local, place=None, first=None,
        early=False,
    ):
        super().__init__(link, local, place, first)
        self.src, self.out, self.own, self.held = src, out, own, held
        self.l1a, self.l1b, self.l2a, self.l2b, self.l3 = l1a, l1b, l2a, l2b, l3
        self.UNSENT = (1, 2, 3) if early else (0, 1, 2, 3)

    @staticmethod
    def scratch(rows, width):
        buffer = lambda *lead: pltpu.VMEM(lead + (rows, width), BF16)
        half = SIDE_DP // 2
        return [
            buffer(SIDE_DP, 2, 2), buffer(half, 2), buffer(half, 2), buffer(half), buffer(half),
            buffer(SIDE_DP - 1),
        ]

    def moves(self, k):
        z, y, x, c = self.at
        held, a, b = self.held, self.half_a, self.half_b
        if k == 0:
            return [self.copy(0, self.src.at[:, :, :, self.nc], held, self.to_core)]
        if k == 1:
            return [
                self.copy(1, held.at[a, self.ny], self.l1a, self.to_y),
                self.copy(2, held.at[b, :, self.nx], self.l1b, self.to_x),
            ]
        if k == 2:
            return [
                self.copy(3, held.at[a, y, self.nx], self.l2a, self.to_x),
                self.copy(4, held.at[b, self.ny, x], self.l2b, self.to_y),
            ]
        return [
            self.copy(5 + i, held.at[other, y, x], self.l3.at[i], peer)
            for i, (other, peer) in enumerate(zip(self.other_z, self.to_z))
        ]

    def keep(self):
        return pltpu.make_async_copy(self.src.at[:, :, :, self.at[3]], self.own, self.local)

    def s0(self):
        self.start(0)
        if self.own is not None:
            self.keep().start()

    def s1(self):
        held = self.held
        if self.own is not None:
            self.keep().wait()
            self.arrive(0)
            held[...] = held[...] + self.own[...]
        else:
            self.arrive(0)
            held[...] = held[...] + self.src[:, :, :, self.at[3]]
        self.start(1)

    def s2(self):
        z, y, x, c = self.at
        self.arrive(1)
        held, a, b = self.held, self.half_a, self.half_b
        held[a, y] = held[a, y] + self.l1a[...]
        held[b, :, x] = held[b, :, x] + self.l1b[...]
        self.start(2)

    def s3(self):
        z, y, x, c = self.at
        self.arrive(2)
        held, a, b = self.held, self.half_a, self.half_b
        held[a, y, x] = held[a, y, x] + self.l2a[...]
        held[b, y, x] = held[b, y, x] + self.l2b[...]
        self.start(3)

    def s4(self):
        z, y, x, c = self.at
        self.arrive(3)
        total = self.held[z, y, x].astype(F32)
        for k in range(SIDE_DP - 1):
            total = total + self.l3[k].astype(F32)
        self.out[...] = total


class Swap(Piece):
    SEMS = 1
    UNSENT = (0,)

    def __init__(self, src, out, link, place):
        super().__init__(link, None, place)
        z, y, x, c = self.at
        self.src, self.out = src, out
        self.peer = device(z + 1 - 2 * lax.rem(z, 2), y, x, c)

    def moves(self, k):
        return [self.copy(0, self.src, self.out, self.peer)]


class SumSmall(Piece):
    SEMS = 6
    UNSENT = ()

    def __init__(self, total, near, far, link):
        super().__init__(link, None)
        self.total, self.near, self.far = total, near, far

    def moves(self, k):
        if k < 3:
            peer = (self.to_core, self.to_y, self.to_x)[k]
            return [self.copy(k, self.total, self.near.at[k], peer)]
        return [
            self.copy(3 + i, self.total, self.far.at[i], peer) for i, peer in enumerate(self.to_z)
        ]

    def add(self, k):
        self.arrive(k)
        self.sent(k)
        if k < 3:
            self.total[...] = self.total[...] + self.near[k]
        else:
            total = self.total[...]
            for i in range(SIDE_DP - 1):
                total = total + self.far[i]
            self.total[...] = total

    def s0(self):
        self.start(0)

    def s1(self):
        self.add(0)
        self.start(1)

    def s2(self):
        self.add(1)
        self.start(2)

    def s3(self):
        self.add(2)
        self.start(3)

    def s4(self):
        self.add(3)


FORWARD_SQUARES = 5


def bias_tables(table):
    lane = lax.broadcasted_iota(jnp.int32, (NB, 4 * LANES), 1)
    bucket = bucket_of(jnp.maximum(LANES - lane, 0))
    bucket = jnp.where(lane <= LANES, bucket, NB - 1)
    row = lax.broadcasted_iota(jnp.int32, (NB, 4 * LANES), 0)
    last = jnp.where(row == NB - 1, 1.0, 0.0)
    hot = jnp.where(row == bucket, 1.0, 0.0) - last
    near = tn(table.astype(BF16), hot.astype(BF16))
    far = tn(table.astype(BF16), last[:, :LANES].astype(BF16))
    return near[:16], far[:16]


def self_forward_kernel(joined, length_ref, x_ref, *refs):
    step = pl.program_id(0)
    last = pl.num_programs(0) - 1
    length = length_ref[own_index() if joined else 0]
    if joined:
        (raw_ref, enc_hbm), shards, refs = refs[:2], refs[2:12], refs[12:]
    else:
        (gain_in, wq_ref, wk_ref, wv_ref, table_in), refs = refs[:5], refs[5:]
    (q_ref, k_ref, v_ref, o_ref, p_ref, a_ref), refs = refs[:6], refs[6:]
    if joined:
        (wq_ref, wk_ref, wv_ref, gain_ref), refs = refs[:4], refs[4:]
        squares, (wide_ref, enc_other) = (
            refs[:FORWARD_SQUARES], refs[FORWARD_SQUARES : FORWARD_SQUARES + 2]
        )
        tile_ref, near_ref, far_ref, got_ref, small_src, got_small, send, recv, local = refs[
            FORWARD_SQUARES + 2 :
        ]
        link, place = Link(send, recv), Place()
        first = [Gather(shards[i], got_ref.at[i], link, local.at[i], place) for i in range(3)]
        first.append(Gather(small_src, got_small, link, local.at[3], place))
        swap = Swap(enc_hbm, enc_other, link, place)
        second = [
            Gather(shards[3 + i], squares[i], link, local.at[4 + i], place)
            for i in range(FORWARD_SQUARES)
        ]
        part = wide_ref.shape[-2]
        third = [
            Gather(
                shards[8 + m].at[k * part : (k + 1) * part], wide_ref.at[k, m], link,
                local.at[9 + 2 * k + m], place,
            )
            for k in range(CHUNKS)
            for m in range(2)
        ]
    else:
        tile_ref, near_ref, far_ref = refs
    seq, model = x_ref.shape
    width = q_ref.shape[1]

    def normed():
        return unit_rows(x_ref[...].astype(F32))[0]

    def set_tables(table):
        near, far = bias_tables(table)
        near_ref[...] = near
        far_ref[...] = far

    @pl.when(step == 0)
    def _():
        if not joined:
            a_ref[...] = (normed() * gain_in[0:1, :]).astype(BF16)
            set_tables(table_in[...])
            return
        rows_in, model_cols = raw_ref.shape[1], model
        entry = lax.broadcasted_iota(jnp.int32, (rows_in, model_cols), 0)
        column = lax.broadcasted_iota(jnp.int32, (rows_in, model_cols), 1)
        spread = lambda at: nn(raw_ref[...], jnp.where(column == entry + at, 1.0, 0.0).astype(BF16))
        is_table = lax.broadcasted_iota(jnp.int32, (8, model_cols), 0) == 3
        small_src[...] = jnp.where(
            is_table, spread(0), spread(own_index() * rows_in)
        ).astype(BF16)
        greet_peers()
        for piece in first:
            piece.stage(0)
        swap.start(0)
        unit = normed()
        for piece in first:
            piece.stage(1)
        for piece in second:
            piece.stage(0)
        for piece in first:
            piece.stage(2)
        first[3].stage(3)
        first[3].stage(4)
        small = got_small[...].astype(F32).reshape(NB, 8, model)
        gains = jnp.sum(small, axis=0)
        gain_ref[...] = gains
        which = lax.broadcasted_iota(jnp.int32, (NB, 8, LANES), 1)
        set_tables(jnp.sum(jnp.where(which == 3, small[:, :, :LANES], 0.0), axis=1))
        a_ref[...] = (unit * gains[0:1, :]).astype(BF16)
        for piece in first[:3]:
            piece.stage(3)
        for i, full_ref in enumerate((wq_ref, wk_ref, wv_ref)):
            first[i].stage(4)
            full_ref[...] = got_ref[i].astype(F32).reshape(model, model).astype(BF16)
        for piece in second:
            piece.stage(1)
        for piece in third[:2]:
            piece.stage(0)

    if joined:

        @pl.when(step == 1)
        def _():
            for piece in second:
                piece.stage(2)
            for piece in third[2:4]:
                piece.stage(0)

        @pl.when(step == 2)
        def _():
            for piece in third[:2]:
                piece.stage(1)
            for piece in third[4:]:
                piece.stage(0)

    for w_ref, out_ref in ((wq_ref, q_ref), (wk_ref, k_ref), (wv_ref, v_ref)):
        if joined:
            weights = w_ref[:, pl.ds(pl.multiple_of(step * width, LANES), width)]
        else:
            weights = w_ref[...]
        out_ref[...] = nn(a_ref[...], weights).astype(BF16)

    key_pos = lax.broadcasted_iota(jnp.int32, (seq, 1), 0)
    key_dead = key_pos >= length
    row = lax.broadcasted_iota(jnp.int32, (ROWS, ROWS + LANES), 0)
    col = lax.broadcasted_iota(jnp.int32, (ROWS, ROWS + LANES), 1)
    ahead = col - LANES > row
    for pair in range(width // LANES):
        cols = slice(pair * LANES, (pair + 1) * LANES)
        outs = [None] * (seq // ROWS)
        for which in range(2):
            local = pair * 2 + which
            head = step * (width // DH) + local
            spun = pltpu.roll(
                jnp.broadcast_to(near_ref[pl.ds(head, 1), :], (ROWS, 4 * LANES)),
                0, 1, stride=1, stride_axis=0,
            )
            tile_ref[...] = jnp.where(ahead, MASKED, spun[:, : ROWS + LANES])
            own = head_lane((seq, LANES), which)
            extra = lax.broadcasted_iota(jnp.int32, (seq, LANES), 1) == (DH if which == 0 else 0)
            far = jnp.where(key_dead, MASKED, far_ref[pl.ds(head, 1), 0:1]).astype(BF16)
            keys = jnp.where(own, k_ref[:, cols], jnp.where(extra, far, jnp.zeros((), BF16)))
            values = jnp.where(own, v_ref[:, cols], jnp.zeros((), BF16))
            queries = jnp.where(own, q_ref[:, cols], jnp.where(extra, 1.0, 0.0).astype(BF16))
            for blk in range(seq // ROWS):
                rows = slice(blk * ROWS, (blk + 1) * ROWS)
                span = (blk + 1) * ROWS
                cut = max(span - ROWS - LANES, 0)
                scores = nt(queries[rows], keys[:span])
                if cut:
                    near = scores[:, cut:] + tile_ref[...]
                    scores = jnp.concatenate([scores[:, :cut], near], axis=1)
                elif span == ROWS:
                    scores = scores + tile_ref[:, LANES:]
                else:
                    near = scores[:, ROWS - LANES :] + tile_ref[...]
                    scores = jnp.concatenate([scores[:, : ROWS - LANES], near], axis=1)
                top = jnp.max(scores, axis=1, keepdims=True)
                weights = jnp.exp(scores - top)
                total = jnp.sum(weights, axis=1, keepdims=True)
                probs = (weights * (1.0 / total)).astype(BF16)
                p_ref[local, rows, :span] = probs
                mixed = nn(probs, values[:span])
                outs[blk] = mixed if outs[blk] is None else outs[blk] + mixed
        for blk in range(seq // ROWS):
            o_ref[blk * ROWS : (blk + 1) * ROWS, cols] = outs[blk].astype(BF16)

    if joined:

        @pl.when(step == last)
        def _():
            for stage in (3, 4):
                for piece in second:
                    piece.stage(stage)
            for piece in third[:2]:
                piece.arrive(1)
                piece.arrive(3)
            for piece in third[2:]:
                piece.keep().wait()
                piece.arrive(0)
            swap.arrive(0)
            for piece in first + second + [swap]:
                piece.drain()
            for i, piece in enumerate(third):
                for k in (0, 1, 3) if i < 2 else (0,):
                    piece.sent(k)


def self_forward(length, x, shards, full, raw=None, enc=None):
    seq, model = x.shape
    width = 256
    heads = width // DH
    steps = model // width
    joined = full is None
    whole = lambda shape: pl.BlockSpec(shape, lambda i: (0,) * len(shape))
    held = lambda shape: pl.BlockSpec(
        shape, lambda i: (0,) * len(shape), pipeline_mode=pl.Buffered(1)
    )
    anywhere = pl.BlockSpec(memory_space=pl.ANY)
    smem = pl.BlockSpec(memory_space=pltpu.SMEM)
    columns = pl.BlockSpec((seq, width), lambda i: (0, i))
    weight = pl.BlockSpec((model, width), lambda i: (0, i))
    in_specs = [smem, held((seq, model))]
    out_specs = [
        columns, columns, columns, columns,
        pl.BlockSpec((heads, seq, seq), lambda i: (i, 0, 0)), whole((seq, model)),
    ]
    out_shape = [jax.ShapeDtypeStruct((seq, model), BF16)] * 4 + [
        jax.ShapeDtypeStruct((H, seq, seq), BF16), jax.ShapeDtypeStruct((seq, model), BF16),
    ]
    scratch = [
        pltpu.VMEM((ROWS, ROWS + LANES), F32), pltpu.VMEM((16, 4 * LANES), F32),
        pltpu.VMEM((16, LANES), F32),
    ]
    params = dict(vmem_limit_bytes=62 * 1024 * 1024)
    if joined:
        lead = (SIDE_DP, 2, 2, 2)
        part = shards[0].shape[0]
        wide = (CHUNKS, 2) + lead + (shards[8].shape[0] // CHUNKS, model)
        ins = [raw, enc] + list(shards)
        in_specs += [whole(raw.shape)] + [anywhere] * (len(ins) - 1)
        square = jax.ShapeDtypeStruct((model, model), BF16)
        out_shape += [square] * 3 + [jax.ShapeDtypeStruct((8, model), F32)]
        out_specs += [whole((model, model))] * 3 + [whole((8, model))]
        out_shape += [jax.ShapeDtypeStruct(lead + (part, model), BF16)] * FORWARD_SQUARES
        out_shape += [jax.ShapeDtypeStruct(wide, BF16), jax.ShapeDtypeStruct(enc.shape, BF16)]
        out_specs += [anywhere] * (FORWARD_SQUARES + 2)
        count = 4 + FORWARD_SQUARES + 2 * CHUNKS
        scratch += [
            pltpu.VMEM((3,) + lead + (part, model), BF16), pltpu.VMEM((8, model), BF16),
            pltpu.VMEM(lead + (8, model), BF16),
            pltpu.SemaphoreType.DMA((count * Gather.SEMS + 1,)),
            pltpu.SemaphoreType.DMA((count * Gather.SEMS + 1,)),
            pltpu.SemaphoreType.DMA((count,)),
        ]
        params.update(collective_id=1, has_side_effects=True)
    else:
        ins = list(full)
        in_specs += [whole((8, model)), weight, weight, weight, whole((NB, LANES))]
    return pl.pallas_call(
        functools.partial(self_forward_kernel, joined),
        grid=(steps,),
        in_specs=in_specs,
        out_specs=out_specs,
        out_shape=out_shape,
        scratch_shapes=scratch,
        compiler_params=pltpu.CompilerParams(**params),
        cost_estimate=pl.CostEstimate(
            flops=6 * seq * model * model + 4 * seq * seq * model,
            bytes_accessed=2 * H * seq * seq + 16 * seq * model,
            transcendentals=H * seq * seq,
        ),
        name="self_forward",
    )(length, x, *ins)


def middle_kernel(joined, length_ref, gain_ref, *refs):
    if joined:
        (dealing_ref, other_hbm), refs = refs[:2], refs[2:]
    length = length_ref[own_index() if joined else 0]
    (x_hbm, o_hbm, cot_hbm, enc_hbm, wo_hbm, cq_hbm, ck_hbm, cv_hbm, co_hbm), refs = (
        refs[:9], refs[9:]
    )
    wide_hbm, refs = refs[0], refs[1:]
    (out_hbm, g1_hbm, egrad_ref, gain_grad_ref), refs = refs[:4], refs[4:]
    squares, refs = refs[:5], refs[5:]
    sum_ref, refs = refs[0], refs[1:]
    if joined:
        wide_hbm, refs = refs[0], refs[1:]
    (
        xr_ref, o_ref, g_ref, a2_ref, cq_scr, mix_ref, a3_ref, r_ref, du_ref, prob_ref,
        x1_ref, x2_ref, acc_ref, dy_ref, enc_ref, keys_ref, values_ref, dk_acc, dv_acc,
        wo_ref, cq_ref, ck_ref, cv_ref, co_ref, wide_ref, src_ref, load_sem, wide_sem, out_sem,
    ), refs = refs[:29], refs[29:]
    seq, model = xr_ref.shape
    blocks = seq // ROWS
    pairs = model // LANES
    zero = jnp.zeros((), BF16)
    gain_cross = gain_ref[1:2, :]
    gain_ffn = gain_ref[2:3, :]

    loads = [
        pltpu.make_async_copy(src, dst, load_sem.at[i])
        for i, (src, dst) in enumerate(
            (
                (enc_hbm, enc_ref), (ck_hbm, ck_ref), (cv_hbm, cv_ref), (o_hbm, o_ref),
                (wo_hbm, wo_ref), (x_hbm, xr_ref), (cq_hbm, cq_ref), (cot_hbm, g_ref),
                (co_hbm, co_ref),
            )
            + (((other_hbm, keys_ref),) if joined else ())
        )
    ]
    for copy in loads:
        copy.start()

    chunk_rows = wide_ref.shape[2]

    def wide_loads(k):
        slot = lax.rem(k, 2)
        found = []
        for m in range(2):
            dst = wide_ref.at[slot, m]
            if joined:
                src = wide_hbm.at[k, m].reshape(chunk_rows, model)
            else:
                src = wide_hbm.at[m, k]
            found.append(pltpu.make_async_copy(src, dst, wide_sem.at[slot, m]))
        return found

    if joined:
        held, l1a, l1b, l2a, l2b, l3, rsend, rrecv, gsend, grecv = refs
        gather_link = Link(gsend, grecv)
        reduce_link = Link(rsend, rrecv)
        place = Place()
        part = chunk_rows // (SIDE_DP * SIDE_FSDP)

        def incoming(k):
            return [
                Gather(
                    None, wide_hbm.at[k, m], gather_link, None, place,
                    (2 * k + m) * Gather.SEMS,
                )
                for m in range(2)
            ]

        def leaving(k):
            at = pl.multiple_of(k * part, 8)
            found = []
            for m in range(2):
                i = 2 * k + m
                found.append(
                    Reduce(
                        src_ref.at[m], sum_ref.at[m, pl.ds(at, part)], None, held.at[i],
                        l1a.at[i], l1b.at[i], l2a.at[i], l2b.at[i], l3.at[i], reduce_link, None,
                        place, i * Reduce.SEMS,
                    )
                )
            return found

    def arriving(k, wait=(), start=(), when=None):
        if not joined:
            return

        def go():
            for piece in incoming(k):
                for round_idx in wait:
                    piece.arrive(round_idx)
            for piece in incoming(k):
                for round_idx in start:
                    piece.start(round_idx)

        go() if when is None else pl.when(when)(go)

    def reduce_stage(k, stage, when=None):
        if not joined:
            return

        def go():
            for piece in leaving(k):
                piece.stage(stage)

        go() if when is None else pl.when(when)(go)

    if joined:
        greet_peers()
        arriving(0, start=(2, 4))
        arriving(1, start=(1, 3))
    else:
        for copy in wide_loads(0):
            copy.start()

    for copy in loads[:3] + loads[9:]:
        copy.wait()
    if joined:
        mine = own_index()
        enc_ref[...] = jnp.where(dealing_ref[mine] == mine, enc_ref[...], keys_ref[...])
    keys_ref[...] = nn(enc_ref[...], ck_ref[...]).astype(BF16)
    values_ref[...] = nn(enc_ref[...], cv_ref[...]).astype(BF16)
    dk_acc[...] = jnp.zeros_like(dk_acc)
    dv_acc[...] = jnp.zeros_like(dv_acc)
    gain_grad_ref[...] = jnp.zeros_like(gain_grad_ref)
    for copy in loads[3:9]:
        copy.wait()

    def forward_rows(i, _):
        rows = pl.ds(pl.multiple_of(i * ROWS, ROWS), ROWS)
        pos = i * ROWS + lax.broadcasted_iota(jnp.int32, (ROWS, 1), 0)
        valid = jnp.where(pos < length, 1.0, 0.0).astype(F32)
        if joined:

            arriving(0, wait=(2,), start=(5,), when=i == 3)

        x1 = xr_ref[rows, :].astype(F32) + nn(o_ref[rows, :], wo_ref[...])
        x1_ref[rows, :] = x1
        unit2, _inv2 = unit_rows(x1)
        a2 = (unit2 * gain_cross).astype(BF16)
        a2_ref[rows, :] = a2
        cq = nn(a2, cq_ref[...]).astype(BF16)
        cq_scr[rows, :] = cq
        mixed = []
        for pair in range(pairs):
            cols = slice(pair * LANES, (pair + 1) * LANES)
            total_out = None
            for which in range(2):
                own = head_lane((ROWS, LANES), which)
                own_key = head_lane((keys_ref.shape[0], LANES), which)
                scores = nt(jnp.where(own, cq[:, cols], zero), keys_ref[:, cols])
                top = jnp.max(scores, axis=1, keepdims=True)
                weights = jnp.exp(scores - top)
                prob = (weights * (1.0 / jnp.sum(weights, axis=1, keepdims=True))).astype(BF16)
                at = (2 * pair + which) * keys_ref.shape[0]
                prob_ref[rows, at : at + keys_ref.shape[0]] = prob
                piece = nn(prob, jnp.where(own_key, values_ref[:, cols], zero))
                total_out = piece if total_out is None else total_out + piece
            mixed.append(total_out.astype(BF16))
        mix = jnp.concatenate(mixed, axis=1)
        mix_ref[rows, :] = mix
        x2 = x1 + nn(mix, co_ref[...])
        x2_ref[rows, :] = x2
        acc_ref[rows, :] = x2
        unit3, _inv3 = unit_rows(x2)
        a3_ref[rows, :] = (unit3 * gain_ffn).astype(BF16)
        g_ref[rows, :] = (g_ref[rows, :].astype(F32) * valid).astype(BF16)
        return 0

    lax.fori_loop(0, blocks, forward_rows, 0)

    def chunk(k, _):
        slot = lax.rem(k, 2)
        for copy in wide_loads(k):
            copy.wait()
        for i in range(blocks):
            rows = slice(i * ROWS, (i + 1) * ROWS)
            z = nt(a3_ref[rows, :], wide_ref[slot, 0])
            zz = z * z
            t = jnp.tanh(GELU_C * z * (1.0 + GELU_A * zz))
            half = 0.5 + 0.5 * t
            r = (z * half).astype(BF16)
            r_ref[rows, :] = r
            slope = half + (0.5 * GELU_C) * z * (1.0 - t * t) * (1.0 + (3.0 * GELU_A) * zz)
            du = (nt(g_ref[rows, :], wide_ref[slot, 1]) * slope).astype(BF16)
            du_ref[rows, :] = du
            acc_ref[rows, :] += nn(r, wide_ref[slot, 1])
            dy_ref[rows, :] += nn(du, wide_ref[slot, 0])
            if i == 1:
                arriving(2, wait=(2,), start=(5,), when=k == 1)
        arriving(1, wait=(2,), start=(5,), when=k == 0)
        arriving(2, wait=(1,), start=(2, 4), when=k == 0)
        reduce_stage(k - 1, 1, k >= 1)
        reduce_stage(k - 2, 2, k >= 2)

        @pl.when(k >= 1)
        def _():
            if joined:
                for piece in leaving(k - 1):
                    piece.sent(0)
            else:
                for copy in grad_copies(k - 1):
                    copy.wait()

        def next_loads():
            for copy in wide_loads(k + 1):
                copy.start()

        if not joined:
            pl.when(k + 1 < CHUNKS)(next_loads)
        shape = src_ref.shape[1:]
        src_ref[0] = tn(du_ref[...], a3_ref[...]).reshape(shape).astype(BF16)
        src_ref[1] = tn(r_ref[...], g_ref[...]).reshape(shape).astype(BF16)
        if joined:
            reduce_stage(k, 0)
            arriving(k + 1, wait=(3, 4, 5), when=k + 1 < CHUNKS)
            pl.when(k + 1 < CHUNKS)(next_loads)
        else:
            for copy in grad_copies(k):
                copy.start()
        return 0

    def grad_copies(k):
        return [
            pltpu.make_async_copy(src_ref.at[m], sum_ref.at[m, k], out_sem.at[m])
            for m in range(2)
        ]

    dy_ref[...] = jnp.zeros_like(dy_ref)
    if joined:
        arriving(0, wait=(4, 5))
        for copy in wide_loads(0):
            copy.start()
        arriving(1, wait=(1,), start=(2, 4))
        arriving(2, start=(1, 3))
    lax.fori_loop(0, CHUNKS, chunk, 0)

    g1_low_ref = a3_ref
    g2_low_ref = g_ref
    dcq_ref = cq_scr
    final = CHUNKS - 1

    def out_copies(rows):
        return [
            pltpu.make_async_copy(acc_ref.at[rows, :], out_hbm.at[rows, :], out_sem.at[0]),
            pltpu.make_async_copy(dy_ref.at[rows, :], g1_hbm.at[rows, :], out_sem.at[1]),
        ]

    if not joined:
        for copy in grad_copies(final):
            copy.wait()

    def backward_rows(i, _):
        rows = pl.ds(pl.multiple_of(i * ROWS, ROWS), ROWS)
        for at, k, stage in ((0, 1, 2), (1, 0, 3), (1, 2, 1), (2, 1, 3), (3, 0, 4), (3, 2, 2)):
            reduce_stage(k, stage, i == at)
        pos = i * ROWS + lax.broadcasted_iota(jnp.int32, (ROWS, 1), 0)
        valid = jnp.where(pos < length, 1.0, 0.0).astype(F32)
        acc_ref[rows, :] = acc_ref[rows, :] * valid
        unit3, inv3 = unit_rows(x2_ref[rows, :])
        through, gain_part = norm_back(dy_ref[rows, :], unit3, inv3, gain_ffn)
        gain_grad_ref[1:2, :] += gain_part
        g2 = g_ref[rows, :].astype(F32) + through
        g2_low = g2.astype(BF16)
        g2_low_ref[rows, :] = g2_low
        dmix = nt(g2_low, co_ref[...]).astype(BF16)
        cq = cq_scr[rows, :]
        dq_parts = []
        for pair in range(pairs):
            cols = slice(pair * LANES, (pair + 1) * LANES)
            dq = None
            for which in range(2):
                own = head_lane((ROWS, LANES), which)
                own_key = head_lane((keys_ref.shape[0], LANES), which)
                at = (2 * pair + which) * keys_ref.shape[0]
                prob_low = prob_ref[rows, at : at + keys_ref.shape[0]]
                prob = prob_low.astype(F32)
                d_out = jnp.where(own, dmix[:, cols], zero)
                dp = nt(d_out, values_ref[:, cols])
                ds = prob * (dp - jnp.sum(prob * dp, axis=1, keepdims=True))
                ds_low = ds.astype(BF16)
                dv_acc[:, cols] += tn(prob_low, d_out)
                dk_acc[:, cols] += tn(ds_low, jnp.where(own, cq[:, cols], zero))
                piece = nn(ds_low, jnp.where(own_key, keys_ref[:, cols], zero))
                dq = piece if dq is None else dq + piece
            dq_parts.append(dq.astype(BF16))
        dcq = jnp.concatenate(dq_parts, axis=1)
        dcq_ref[rows, :] = dcq
        unit2, inv2 = unit_rows(x1_ref[rows, :])
        through, gain_part = norm_back(nt(dcq, cq_ref[...]), unit2, inv2, gain_cross)
        gain_grad_ref[0:1, :] += gain_part
        g1 = g2 + through
        dy_ref[rows, :] = g1
        g1_low_ref[rows, :] = g1.astype(BF16)
        for copy in out_copies(rows):
            copy.start()
        return 0

    lax.fori_loop(0, blocks, backward_rows, 0)

    reduce_stage(final - 1, 4)
    reduce_stage(final, 3)
    dk = dk_acc[...].astype(BF16)
    dv = dv_acc[...].astype(BF16)
    egrad_ref[...] = nt(dk, ck_ref[...]) + nt(dv, cv_ref[...])
    made = (
        (cq_ref, lambda: tn(a2_ref[...], dcq_ref[...])),
        (ck_ref, lambda: tn(enc_ref[...], dk)),
        (cv_ref, lambda: tn(enc_ref[...], dv)),
        (co_ref, lambda: tn(mix_ref[...], g2_low_ref[...])),
        (wo_ref, lambda: tn(o_ref[...], g1_low_ref[...])),
    )
    writes = []
    for i, (buffer, make) in enumerate(made):
        buffer[...] = make().astype(BF16)
        writes.append(pltpu.make_async_copy(buffer, squares[i], load_sem.at[i]))
        writes[-1].start()
    reduce_stage(final, 4)
    for copy in writes:
        copy.wait()
    for i in range(blocks):
        for copy in out_copies(pl.ds(i * ROWS, ROWS)):
            copy.wait()
    if joined:
        for k, rounds in enumerate(((2, 4, 5), (1, 2, 3, 4, 5), (1, 2, 3, 4, 5))):
            for piece in incoming(k):
                for round_idx in rounds:
                    piece.sent(round_idx)
        for k in range(CHUNKS):
            for piece in leaving(k):
                for round_idx in (0, 1, 2, 3) if k == final else (1, 2, 3):
                    piece.sent(round_idx)


def middle(
    length, x, o, cot, enc, gains, wo, cq, ck, cv, co, wide, joined, dealing=None, other=None
):
    seq, model = x.shape
    enc_len = enc.shape[0]
    anywhere = pl.BlockSpec(memory_space=pl.ANY)
    vmem = pl.BlockSpec(memory_space=pltpu.VMEM)
    smem = pl.BlockSpec(memory_space=pltpu.SMEM)
    low = lambda *shape: pltpu.VMEM(shape, BF16)
    full = lambda *shape: pltpu.VMEM(shape, F32)
    ins = [x, o, cot, enc, wo, cq, ck, cv, co, wide]
    square = jax.ShapeDtypeStruct((model, model), BF16)
    out_shape = [
        jax.ShapeDtypeStruct((seq, model), F32),
        jax.ShapeDtypeStruct((seq, model), F32),
        jax.ShapeDtypeStruct((enc_len, model), F32),
        jax.ShapeDtypeStruct((2, model), F32),
    ] + [square] * 5
    out_specs = [anywhere, anywhere, vmem, vmem] + [anywhere] * 5
    hidden = 4 * model
    chunk_rows = hidden // CHUNKS
    rows_low = [low(seq, model)] * 7 + [low(seq, chunk_rows)] * 2
    params = dict(vmem_limit_bytes=63 * 1024 * 1024)
    if joined:
        part = chunk_rows // (SIDE_DP * SIDE_FSDP)
        lead = (SIDE_DP, 2, 2, 2)
        out_shape += [
            jax.ShapeDtypeStruct((2, CHUNKS * part, model), F32),
            jax.ShapeDtypeStruct(wide.shape, BF16),
        ]
        out_specs += [vmem, anywhere]
        gather_sems = 2 * CHUNKS * Gather.SEMS
        aliases = {4 + len(ins) - 1: len(out_shape) - 1}
        src = low(2, *lead, part, model)
        count = 2 * CHUNKS
        reduce_sems = count * Reduce.SEMS
        extra = [
            pltpu.VMEM((count,) + buffer.shape, BF16) for buffer in Reduce.scratch(part, model)
        ] + [
            pltpu.SemaphoreType.DMA((reduce_sems,)), pltpu.SemaphoreType.DMA((reduce_sems,)),
            pltpu.SemaphoreType.DMA((gather_sems,)), pltpu.SemaphoreType.DMA((gather_sems,)),
        ]
        params.update(collective_id=2, has_side_effects=True)
    else:
        out_shape += [jax.ShapeDtypeStruct((2, CHUNKS, chunk_rows, model), BF16)]
        out_specs += [anywhere]
        src = low(2, chunk_rows, model)
        extra = []
        aliases = {}
    return pl.pallas_call(
        functools.partial(middle_kernel, joined),
        in_specs=[smem, vmem] + ([smem, anywhere] if joined else []) + [anywhere] * len(ins),
        out_specs=out_specs,
        out_shape=out_shape,
        scratch_shapes=rows_low
        + [
            low(seq, H * enc_len), full(seq, model), full(seq, model), full(seq, model),
            full(seq, model), low(enc_len, model), low(enc_len, model), low(enc_len, model),
            full(enc_len, model), full(enc_len, model),
        ]
        + [low(model, model)] * 5
        + [
            low(2, 2, chunk_rows, model), src,
            pltpu.SemaphoreType.DMA((10,)), pltpu.SemaphoreType.DMA((2, 2)),
            pltpu.SemaphoreType.DMA((2,)),
        ]
        + extra,
        input_output_aliases=aliases,
        compiler_params=pltpu.CompilerParams(**params),
        name="middle",
    )(length, gains, *([dealing, other] if joined else []), *ins)


def gather_weights(shards, axes):
    pile = lax.all_gather(jnp.concatenate(shards, axis=0), axes, axis=0)
    full, at = [], 0
    for shard in shards:
        full.append(pile[:, at : at + shard.shape[0]].reshape(-1, pile.shape[-1]))
        at += shard.shape[0]
    return full


def reduce_grads(grads, axes):
    dev_count = lax.axis_size("dp") * lax.axis_size("fsdp")
    split = [g.reshape(dev_count, -1, g.shape[-1]) for g in grads]
    pile = lax.psum_scatter(
        jnp.concatenate(split, axis=1), axes, scatter_dimension=0, tiled=False
    ).astype(F32)
    sums, at = [], 0
    for s in split:
        sums.append(pile[at : at + s.shape[1]])
        at += s.shape[1]
    return sums


HIST = 2 * LANES


def self_backward_kernel(
    far_count, x_ref, gain_ref, mid_gain_ref, a_ref, g1_ref, q_ref, k_ref, v_ref, p_ref,
    wo_ref, wq_ref, wk_ref, wv_ref, *refs,
):
    joined = far_count is not None
    if joined:
        egrad_ref, far_refs = refs[0], refs[1 : far_count + 1]
        ingrad_ref, sum_ref, near_sum_ref, small_ref, egrad_other = refs[
            far_count + 1 : far_count + 6
        ]
        rest = refs[far_count + 6 :]
    else:
        ingrad_ref, gw_ref, small_ref, hist_out = refs[:4]
        rest = refs[4:]
    low_ref, near_acc, dk_acc, dv_acc, dq_scr, hist_ref = rest[:6]
    rest = rest[6:]
    step = pl.program_id(0)
    last = pl.num_programs(0) - 1
    seq, model = x_ref.shape
    width = q_ref.shape[1]
    heads = width // DH
    steps = model // width
    events = {}
    if joined:
        src_ref, own_ref, near_small, far_small, send, recv, local = rest[-7:]
        link = Link(send, recv)
        part = sum_ref.shape[0] // far_count
        pieces = []
        for i in range(far_count + steps):
            far = i < far_count
            pieces.append(
                Reduce(
                    far_refs[i] if far else src_ref.at[(i - far_count) % 2],
                    (sum_ref if far else near_sum_ref).at[
                        (i if far else i - far_count) * part
                        : (i + 1 if far else i + 1 - far_count) * part
                    ],
                    own_ref.at[i] if far else None,
                    *rest[Reduce.BUFFERS * i : Reduce.BUFFERS * (i + 1)], link,
                    local.at[i], early=far_count <= i < far_count + steps - 2,
                )
            )
        small = SumSmall(small_ref, near_small, far_small, link)
        swap = Swap(egrad_ref, egrad_other, link, Place())
        far_times = [(0, 1, 3, 4, 7), (0, 1, 3, 5, 7), (0, 1, 4, 5, 8), (0, 2, 4, 5, 7)]
        far_times += [(0, 3, 5, 7, 9)] * (far_count - len(far_times))
        near_times = [(2, 3, 4, 8), (3, 5, 6, 9), (4, 5, 6, 8), (5, 6, 8, 10), (5, 6, 8, 10)]
        near_times += [(7, 8, 9, 10)] * (steps - len(near_times))
        for i in range(far_count):
            for k, time in enumerate(far_times[i]):
                events.setdefault(time, []).append((-k, pieces[i]))
        for i in range(steps):
            for k, time in enumerate(near_times[i]):
                events.setdefault(time, []).append((-k - 1, pieces[far_count + i]))

    def tick(time):
        for k, piece in sorted(events.get(time, []), key=lambda event: event[0]):
            piece.stage(-k)

    @pl.when(step == 0)
    def _():
        if joined:
            greet_peers()
            tick(0)
            swap.start(0)
        low_ref[...] = g1_ref[...].astype(BF16)
        hist_ref[...] = jnp.zeros_like(hist_ref)

    for g in range(1, steps):
        if events.get(g):
            pl.when(step == g)(functools.partial(tick, g))

    d_all = nt(low_ref[...], wo_ref[...]).astype(BF16)
    zero = jnp.zeros((), BF16)
    for pair in range(width // LANES):
        cols = slice(pair * LANES, (pair + 1) * LANES)
        dk_acc[...] = jnp.zeros_like(dk_acc)
        dv_acc[...] = jnp.zeros_like(dv_acc)
        dq_blocks = [None] * (seq // ROWS)
        for which in range(2):
            local_head = pair * 2 + which
            head = step * heads + local_head
            own = head_lane((seq, LANES), which)
            d_out = jnp.where(own, d_all[:, cols], zero)
            queries = jnp.where(own, q_ref[:, cols], zero)
            keys = jnp.where(own, k_ref[:, cols], zero)
            for blk in range(seq // ROWS):
                rows = slice(blk * ROWS, (blk + 1) * ROWS)
                span = (blk + 1) * ROWS
                prob_low = p_ref[local_head, rows, :span]
                prob = prob_low.astype(F32)
                dp = nt(d_out[rows], v_ref[:span, cols])
                ds = prob * (dp - jnp.sum(prob * dp, axis=1, keepdims=True))
                if blk == 0:
                    near_acc[:, :LANES] = jnp.zeros((ROWS, LANES), F32)
                    near_acc[:, LANES:] = ds
                else:
                    near_acc[...] += ds[:, span - ROWS - LANES :]
                ds_low = ds.astype(BF16)
                part_q = nn(ds_low, keys[:span])
                dq_blocks[blk] = part_q if which == 0 else dq_blocks[blk] + part_q
                dk_acc[:span, :] += tn(ds_low, queries[rows])
                dv_acc[:span, :] += tn(prob_low, d_out[rows])
            padded = jnp.concatenate([near_acc[...], jnp.zeros((ROWS, LANES), F32)], axis=1)
            count = ROWS
            while count > 1:
                count //= 2
                padded = padded[:count] + pltpu.roll(padded[count:], 4 * LANES - count, 1)
            hist_ref[pl.ds(head, 1), :] = padded[:, :HIST]
        dq = jnp.concatenate([block.astype(BF16) for block in dq_blocks], axis=0)
        dk = dk_acc[...].astype(BF16)
        dv = dv_acc[...].astype(BF16)
        at = pl.ds(pl.multiple_of(step * width + pair * LANES, LANES), LANES)
        for i, part_grad in enumerate((dq, dk, dv)):
            dq_scr[i, :, at] = part_grad

    @pl.when(step == last)
    def _():
        small_ref[...] = jnp.zeros_like(small_ref)
        small_ref[1:3, :model] = mid_gain_ref[...]
        small_ref[:, model : model + HIST] = hist_ref[0:8, :]
        small_ref[:, model + HIST :] = hist_ref[8:16, :]
        if joined:
            small.stage(0)

    grads = tn(a_ref[...], jnp.concatenate([dq, dk, dv], axis=1))
    if joined:
        for g in range(steps):

            @pl.when(step == g)
            def _():
                if g >= 2:
                    pieces[far_count + g - 2].sent(0)
                src_ref[g % 2] = grads.reshape(src_ref.shape[1:]).astype(BF16)
                pieces[far_count + g].stage(0)
                if g == steps - 1:
                    tick(steps)
    else:
        gw_ref[0] = grads.astype(BF16)

    @pl.when(step == last)
    def _():
        ingrad_ref[...] = nt(dq_scr[0], wq_ref[...])
        if joined:
            tick(steps + 1)
            small.stage(1)
        ingrad_ref[...] += nt(dq_scr[1], wk_ref[...])
        if joined:
            small.stage(2)
        ingrad_ref[...] += nt(dq_scr[2], wv_ref[...])
        if joined:
            tick(steps + 2)
            small.stage(3)
        unit, inv = unit_rows(x_ref[...].astype(F32))
        through, gain_part = norm_back(ingrad_ref[...], unit, inv, gain_ref[...])
        ingrad_ref[...] = g1_ref[...] + through
        if joined:
            tick(steps + 3)
            small.stage(4)
            swap.arrive(0)
            tick(steps + 4)
            link.drain()
        else:
            small_ref[0:1, :model] = gain_part
            hist_out[...] = hist_ref[...]


def self_backward(
    x, gain, mid_gain, a1, g1, q, k, v, p, wo, wq, wk, wv, far_grads, egrad=None
):
    seq, model = x.shape
    width = 128
    heads = width // DH
    steps = model // width
    joined = far_grads is not None
    held = lambda shape: pl.BlockSpec(
        shape, lambda i: (0,) * len(shape), pipeline_mode=pl.Buffered(1)
    )
    whole = lambda shape: pl.BlockSpec(shape, lambda i: (0,) * len(shape))
    columns = pl.BlockSpec((seq, width), lambda i: (0, i))
    weight_rows = pl.BlockSpec((width, model), lambda i: (i, 0))
    in_specs = [
        held((seq, model)), held((1, model)), held((2, model)), held((seq, model)),
        held((seq, model)), columns, columns, columns,
        pl.BlockSpec((heads, seq, seq), lambda i: (i, 0, 0)),
        weight_rows, held((model, model)), held((model, model)), held((model, model)),
    ]
    small = (8, model + 2 * HIST)
    out_specs = [whole((seq, model))]
    out_shape = [jax.ShapeDtypeStruct((seq, model), F32)]
    scratch = [
        pltpu.VMEM((seq, model), BF16),
        pltpu.VMEM((ROWS, ROWS + LANES), F32),
        pltpu.VMEM((seq, LANES), F32),
        pltpu.VMEM((seq, LANES), F32),
        pltpu.VMEM((3, seq, model), BF16),
        pltpu.VMEM((16, HIST), F32),
    ]
    extra = []
    params = dict(vmem_limit_bytes=63 * 1024 * 1024)
    if joined:
        count = len(far_grads)
        part = model // (SIDE_DP * SIDE_FSDP)
        across = 3 * width
        extra = [egrad] + [g.reshape(SIDE_DP, 2, 2, 2, part, model) for g in far_grads]
        in_specs += [pl.BlockSpec(memory_space=pl.ANY)] * (count + 1)
        shapes = ((count * part, model), (steps * part, across), small, egrad.shape)
        out_specs += [whole(s) for s in shapes[:3]] + [pl.BlockSpec(memory_space=pl.ANY)]
        out_shape += [jax.ShapeDtypeStruct(s, F32) for s in shapes]
        for i in range(count + steps):
            scratch += Reduce.scratch(part, model if i < count else across)
        sems = (count + steps) * Reduce.SEMS + SumSmall.SEMS + Swap.SEMS
        scratch += [
            pltpu.VMEM((2, SIDE_DP, 2, 2, 2, part, across), BF16),
            pltpu.VMEM((count, SIDE_DP, 2, 2, part, model), BF16),
            pltpu.VMEM((3,) + small, F32),
            pltpu.VMEM((SIDE_DP - 1,) + small, F32),
            pltpu.SemaphoreType.DMA((sems,)), pltpu.SemaphoreType.DMA((sems,)),
            pltpu.SemaphoreType.DMA((count + steps,)),
        ]
        params.update(collective_id=3, has_side_effects=True)
    else:
        count = None
        out_specs += [
            pl.BlockSpec((1, model, 3 * width), lambda i: (i, 0, 0)), whole(small),
            whole((16, HIST)),
        ]
        out_shape += [
            jax.ShapeDtypeStruct((steps, model, 3 * width), BF16),
            jax.ShapeDtypeStruct(small, F32),
            jax.ShapeDtypeStruct((16, HIST), F32),
        ]
    return pl.pallas_call(
        functools.partial(self_backward_kernel, count),
        grid=(steps,),
        in_specs=in_specs,
        out_specs=out_specs,
        out_shape=out_shape,
        scratch_shapes=scratch,
        compiler_params=pltpu.CompilerParams(**params),
        cost_estimate=pl.CostEstimate(
            flops=14 * seq * model * model + 8 * seq * seq * model,
            bytes_accessed=2 * H * seq * seq + 24 * seq * model,
            transcendentals=0,
        ),
        name="self_backward",
    )(x, gain, mid_gain, a1, g1, q, k, v, p, wo, wq, wk, wv, *extra)


def exact(left_op, right_op, dims):
    return lax.dot_general(
        left_op, right_op, (dims, ((), ())), preferred_element_type=F32,
        precision=lax.Precision.HIGHEST,
    )


def finish_kernel(
    dealing_ref, raw_ref, wq_ref, wk_ref, wv_ref, ccq_ref, sum_ref, near_ref, small_ref, wide_ref,
    egrad_ref, other_ref, out_in, ingrad_in, *refs,
):
    (
        out_ref, ingrad_ref, enc_ref, gq_ref, gk_ref, gv_ref, go_ref, gcq_ref, gck_ref, gcv_ref,
        gco_ref, gin_ref, gdown_ref, self_ref, cross_ref, ffn_ref, table_ref, through, sems,
    ) = refs
    pieces = []
    for i, (src, dst) in enumerate(((out_in, out_ref), (ingrad_in, ingrad_ref))):
        for j in range(src.shape[0] // ROWS):
            rows = slice(j * ROWS, (j + 1) * ROWS)
            pieces.append(
                (
                    pltpu.make_async_copy(src.at[rows], through.at[i, rows], sems.at[0, i, j]),
                    pltpu.make_async_copy(through.at[i, rows], dst.at[rows], sems.at[1, i, j]),
                )
            )
    for inward, _outward in pieces:
        inward.start()
    for inward, outward in pieces:
        inward.wait()
        outward.start()
    mine = own_index()
    part, model = gq_ref.shape
    steps = near_ref.shape[0] // part
    width = near_ref.shape[1] // 3
    for ref, i in ((gcq_ref, 0), (gck_ref, 1), (gcv_ref, 2), (gco_ref, 3), (go_ref, 4)):
        ref[...] = sum_ref[i * part : (i + 1) * part, :]
    for g in range(steps):
        for i, ref in enumerate((gq_ref, gk_ref, gv_ref)):
            ref[:, g * width : (g + 1) * width] = near_ref[
                g * part : (g + 1) * part, i * width : (i + 1) * width
            ]
    gin_ref[...] = wide_ref[0]
    gdown_ref[...] = wide_ref[1]
    enc_ref[...] = jnp.where(dealing_ref[mine] == mine, egrad_ref[...], other_ref[...])
    ones = jnp.ones((8, model), F32)
    gains = raw_ref[...].astype(F32)
    weighted = (
        gq_ref[...] * wq_ref[...].astype(F32) + gk_ref[...] * wk_ref[...].astype(F32)
        + gv_ref[...] * wv_ref[...].astype(F32)
    )
    self_ref[...] = exact(ones, weighted, ((1,), (1,)))[0:1, :] / gains[0:1, :part]
    weighted = gcq_ref[...] * ccq_ref[...].astype(F32)
    cross_ref[...] = exact(ones, weighted, ((1,), (1,)))[0:1, :] / gains[1:2, :part]
    entry = lax.broadcasted_iota(jnp.int32, (part, model), 0)
    column = lax.broadcasted_iota(jnp.int32, (part, model), 1)
    place = jnp.where(column == entry + mine * part, 1.0, 0.0)
    ffn_ref[...] = exact(small_ref[:, :model], place, ((1,), (1,)))[2:3, :]
    lane = lax.broadcasted_iota(jnp.int32, (16, HIST), 1)
    distance = LANES - lane
    bucket = bucket_of(jnp.maximum(distance, 0))
    usable = (distance >= 0) & (bucket < NB - 1)
    picked = usable & ((bucket == mine) | (mine == NB - 1))
    sign = jnp.where(mine == NB - 1, -1.0, 1.0)
    hist = jnp.concatenate(
        [small_ref[:, model : model + HIST], small_ref[:, model + HIST :]], axis=0
    )
    sums = exact(ones[:, :HIST], jnp.where(picked, hist, 0.0), ((1,), (1,)))
    table_ref[...] = sign * sums[0:1, : table_ref.shape[1]]
    for _inward, outward in pieces:
        outward.wait()


def finish(dealing, raw, shards, sums, near, small, wide, egrad, other, out, in_grad):
    part, model = shards[0].shape
    anywhere = pl.BlockSpec(memory_space=pl.ANY)
    vmem = pl.BlockSpec(memory_space=pltpu.VMEM)
    f32 = lambda *shape: jax.ShapeDtypeStruct(shape, F32)
    square = f32(part, model)
    hidden_part = wide.shape[1]
    return pl.pallas_call(
        finish_kernel,
        in_specs=[pl.BlockSpec(memory_space=pltpu.SMEM)] + [vmem] * 11 + [anywhere] * 2,
        out_specs=[anywhere] * 2 + [vmem] * 15,
        out_shape=[f32(*out.shape), f32(*in_grad.shape), f32(*egrad.shape)]
        + [square] * 8
        + [f32(hidden_part, model)] * 2
        + [f32(1, part)] * 3
        + [f32(1, NB * H // (SIDE_DP * SIDE_FSDP))],
        scratch_shapes=[
            pltpu.VMEM((2,) + out.shape, F32),
            pltpu.SemaphoreType.DMA((2, 2, out.shape[0] // ROWS)),
        ],
        compiler_params=pltpu.CompilerParams(vmem_limit_bytes=62 * 1024 * 1024),
        name="finish",
    )(dealing, raw, *shards, sums, near, small, wide, egrad, other, out, in_grad)


def body(
    tokens, encoder_states, lengths, dealing, cotangent,
    w_query, w_key, w_value, w_out, c_query, c_key, c_value, c_out, w_in, w_down,
    gain_self, gain_cross, gain_ffn, bias_table,
):
    axes = ("dp", "fsdp")
    fsdp_size = lax.axis_size("fsdp")
    dp_size = lax.axis_size("dp")
    dev_count = dp_size * fsdp_size
    dp_index = lax.axis_index("dp")
    own = dp_index * fsdp_size + lax.axis_index("fsdp")
    seq_len, model = tokens.shape[1:]
    route = [(a, a ^ 1) for a in range(dp_size)]

    x = tokens[0]
    cot = cotangent[0]
    gain_part = gain_self.shape[0]
    joined = dp_size == SIDE_DP and fsdp_size == SIDE_FSDP
    in_rows = w_in.T
    shards = [
        w_query, w_key, w_value, w_out, c_query, c_key, c_value, c_out, in_rows, w_down
    ]
    if joined:
        raw = jnp.stack(
            [gain_self, gain_cross, gain_ffn, jnp.pad(bias_table, (0, gain_part - bias_table.shape[0]))]
        )
        raw = jnp.pad(raw, ((0, 4), (0, 0)))
        done = self_forward(lengths, x, shards, None, raw, encoder_states[0])
        q, k, v, o, p, a1, wq, wk, wv, gains = done[:10]
        wo, cq, ck, cv, co = (w.reshape(model, model) for w in done[10:15])
        done = middle(
            lengths, x, o, cot, encoder_states[0], gains, wo, cq, ck, cv, co, done[15], True,
            dealing, done[16],
        )
        out, g1, egrad, mid_gain_grad = done[:4]
        wide_sums = done[9]
        done = self_backward(
            x, gains[0:1], mid_gain_grad, a1, g1, q, k, v, p, wo, wq, wk, wv,
            list(done[4:9]), egrad,
        )
        in_grad, sums, near_sums, small, egrad_other = done
        done = finish(
            dealing, raw, [w_query, w_key, w_value, c_query], sums, near_sums, small, wide_sums,
            egrad, egrad_other, out, in_grad,
        )
        return (
            tuple(d[None] for d in done[:3]) + tuple(done[3:11]) + (done[11].T, done[12])
            + tuple(d[0] for d in done[13:])
        )

    in_place = lax.dynamic_slice_in_dim(dealing, own, 1) == own
    enc_other = lax.ppermute(encoder_states[0], "dp", route)
    enc = jnp.where(in_place[:, None], encoder_states[0], enc_other)
    length = lax.dynamic_slice_in_dim(lengths, own, 1)
    column = jnp.arange(model, dtype=jnp.int32)[None, :]
    gain_rows = jnp.stack(
        [jnp.tile(g, model // gain_part) for g in (gain_self, gain_cross, gain_ffn)]
    )
    gain_rows = jnp.where(column // gain_part == own, gain_rows, jnp.zeros((), BF16))
    table_row = jnp.pad(bias_table, (0, model - bias_table.shape[0]))[None, :]
    small = jnp.pad(jnp.concatenate([gain_rows, table_row], axis=0), ((0, 4), (0, 0)))
    wq, wk, wv, wo, cq, ck, cv, co, win_t, wdown, small_all = gather_weights(
        shards + [small], axes
    )
    wide = jnp.stack([w.reshape(CHUNKS, -1, model) for w in (win_t, wdown)])
    small_all = small_all.reshape(dev_count, 8, model).astype(F32)
    gains = jnp.sum(small_all, axis=0)
    table = small_all[:, 3, : bias_table.shape[0]].reshape(NB, H)
    table = jnp.pad(table, ((0, 0), (0, LANES - H)))
    q, k, v, o, p, a1 = self_forward(length, x, None, [gains, wq, wk, wv, table])
    done = middle(length, x, o, cot, enc, gains, wo, cq, ck, cv, co, wide, False)
    out, g1, egrad, mid_gain_grad = done[:4]
    squares = list(done[4:9])
    sum_in, sum_down = reduce_grads([g.reshape(-1, model) for g in done[9]], axes)
    done = self_backward(
        x, gains[0:1], mid_gain_grad, a1, g1, q, k, v, p, wo, wq, wk, wv, None
    )
    in_grad = done[0]
    gw, small, hist = done[1:]
    g_wq, g_wk, g_wv = (
        jnp.concatenate(
            [g[:, i * LANES : (i + 1) * LANES] for g in gw], axis=1
        )
        for i in range(3)
    )
    distance = jnp.arange(LANES, dtype=jnp.int32)
    bucket_hot = bucket_of(distance)[:, None] == jnp.arange(NB, dtype=jnp.int32)[None, :]
    near_hot = bucket_hot.astype(F32) * (jnp.arange(NB) < NB - 1).astype(F32)
    by_dist = hist[:H, 1 : LANES + 1][:, ::-1]
    near_sums = jnp.dot(near_hot.T, by_dist.T, precision=lax.Precision.HIGHEST)
    grad_table = jnp.where(
        (jnp.arange(NB) < NB - 1)[:, None],
        near_sums, -jnp.sum(near_sums, axis=0, keepdims=True),
    )
    small_grads = jnp.concatenate(
        [small[i, :model].reshape(dev_count, -1) for i in range(3)]
        + [grad_table.reshape(dev_count, -1)],
        axis=1,
    )
    small_count = small_grads.shape[1]
    small_low = jnp.pad(small_grads.astype(BF16), ((0, 0), (0, model - small_count)))
    small_low = jnp.pad(small_low[:, None, :], ((0, 0), (0, 7), (0, 0))).reshape(-1, model)
    sum_cq, sum_ck, sum_cv, sum_co, sum_wo, sum_wq, sum_wk, sum_wv, sum_small = reduce_grads(
        squares + [g_wq, g_wk, g_wv, small_low], axes
    )
    ends = sum_small[0]
    end_self, end_cross, end_ffn = (
        ends[i * gain_part : (i + 1) * gain_part] for i in range(3)
    )
    end_table = ends[3 * gain_part : small_count]

    egrad_other = lax.ppermute(egrad, "dp", route)
    encoder_grad = jnp.where(in_place[:, None], egrad, egrad_other)
    return (
        out[None], in_grad[None], encoder_grad[None],
        sum_wq, sum_wk, sum_wv, sum_wo, sum_cq, sum_ck, sum_cv, sum_co, sum_in.T, sum_down,
        end_self, end_cross, end_ffn, end_table,
    )


def solution(mesh):
    rows3 = P(("dp", "fsdp"), None, None)
    rows2 = P(("dp", "fsdp"), None)
    cols2 = P(None, ("dp", "fsdp"))
    line = P(("dp", "fsdp"))
    in_specs = (
        (rows3, rows3, P(), P(), rows3) + (rows2,) * 8 + (cols2, rows2) + (line,) * 4
    )
    out_specs = (rows3,) * 3 + (rows2,) * 8 + (cols2, rows2) + (line,) * 4
    return jax.shard_map(body, mesh=mesh, in_specs=in_specs, out_specs=out_specs, check_vma=False)
```

```python
import functools
import math

import jax
import jax.numpy as jnp
from jax import lax
from jax.experimental import pallas as pl
from jax.experimental.pallas import tpu as pltpu
from jax.sharding import PartitionSpec as P

H = 12
DH = 64
NB = 32
MAXDIST = 128
EPSILON = 1e-06
MASKED = -1e30
LANES = 128
CHUNKS = 3
ROWS = 256
FORWARD_ROWS = 512
HIDDEN_ROWS = 256
BACK_ROWS = 512
CROSS_ROWS = 512
F32 = jnp.float32
BF16 = jnp.bfloat16
GELU_C = math.sqrt(2.0 / math.pi)
GELU_A = 0.044715


def bucket_of(distance):
    exact_count = NB // 2
    bucket = jnp.minimum(distance, exact_count)
    for level_idx in range(1, exact_count):
        threshold = int(
            math.ceil(exact_count * (MAXDIST / exact_count) ** (level_idx / exact_count))
        )
        bucket = bucket + (distance >= threshold).astype(jnp.int32)
    return bucket


def nn(left_op, right_op):
    return lax.dot_general(
        left_op, right_op, (((1,), (0,)), ((), ())), preferred_element_type=F32
    )


def nt(left_op, right_op):
    return lax.dot_general(
        left_op, right_op, (((1,), (1,)), ((), ())), preferred_element_type=F32
    )


def tn(left_op, right_op):
    return lax.dot_general(
        left_op, right_op, (((0,), (0,)), ((), ())), preferred_element_type=F32
    )


def unit_rows(values_in):
    inv_rms = lax.rsqrt(jnp.mean(values_in * values_in, axis=-1, keepdims=True) + EPSILON)
    return values_in * inv_rms, inv_rms


def norm_back(grad_in, unit, inv_rms, gain_vec):
    scaled = grad_in * gain_vec
    through = inv_rms * (scaled - unit * jnp.mean(scaled * unit, axis=-1, keepdims=True))
    return through, jnp.sum(grad_in * unit, axis=0, keepdims=True)


def head_lane(shape, which):
    lane = lax.broadcasted_iota(jnp.int32, shape, len(shape) - 1)
    return (lane // DH) == which


SIDE_DP = 4
SIDE_FSDP = 8
MESH = pl.DeviceIdType.MESH


def coords():
    along = lax.axis_index("fsdp")
    return lax.axis_index("dp"), along // 4, lax.rem(along // 2, 2), lax.rem(along, 2)


def device(z, y, x, c):
    return (z, y * 4 + x * 2 + c)


def greet_peers():
    z, y, x, c = coords()
    peers = [device(lax.rem(z + k, SIDE_DP), y, x, c) for k in range(1, SIDE_DP)]
    peers += [device(z, y, 1 - x, c), device(z, 1 - y, x, c), device(z, y, x, 1 - c)]
    barrier = pltpu.get_barrier_semaphore()
    for peer in peers:
        pl.semaphore_signal(barrier, inc=1, device_id=peer, device_id_type=MESH)
    pl.semaphore_wait(barrier, len(peers))


def own_index():
    return lax.axis_index("dp") * SIDE_FSDP + lax.axis_index("fsdp")


class Link:
    def __init__(self, send, recv):
        self.send, self.recv, self.used, self.pieces = send, recv, 0, []

    def take(self, piece):
        self.pieces.append(piece)
        self.used += piece.SEMS
        return self.used - piece.SEMS

    def drain(self):
        for piece in self.pieces:
            piece.drain()


class Place:
    def __init__(self):
        z, y, x, c = self.at = coords()
        self.to_y = device(z, 1 - y, x, c)
        self.to_x = device(z, y, 1 - x, c)
        self.to_core = device(z, y, x, 1 - c)
        self.other_z = [lax.rem(z + k, SIDE_DP) for k in range(1, SIDE_DP)]
        self.to_z = [device(other, y, x, c) for other in self.other_z]
        self.ny, self.nx, self.nc = 1 - y, 1 - x, 1 - c


class Piece:
    def __init__(self, link, local, place=None, first=None):
        self.link, self.local = link, local
        self.first = link.take(self) if first is None else first
        self.half_a, self.half_b = slice(0, SIDE_DP // 2), slice(SIDE_DP // 2, SIDE_DP)
        place = place or Place()
        self.at, self.to_y, self.to_x, self.to_core = (
            place.at, place.to_y, place.to_x, place.to_core
        )
        self.other_z, self.to_z = place.other_z, place.to_z
        self.ny, self.nx, self.nc = place.ny, place.nx, place.nc

    def copy(self, slot, src, dst, peer):
        return pltpu.make_async_remote_copy(
            src_ref=src, dst_ref=dst, send_sem=self.link.send.at[self.first + slot],
            recv_sem=self.link.recv.at[self.first + slot], device_id=peer, device_id_type=MESH,
        )

    def start(self, k):
        for copy in self.moves(k):
            copy.start()

    def arrive(self, k):
        for copy in self.moves(k):
            copy.wait_recv()

    def sent(self, k):
        for copy in self.moves(k):
            copy.wait_send()

    def drain(self):
        for k in self.UNSENT:
            self.sent(k)

    def stage(self, k):
        (self.s0, self.s1, self.s2, self.s3, self.s4)[k]()


class Gather(Piece):
    SEMS = 13
    UNSENT = (0, 1, 2, 3, 4, 5)

    def __init__(self, src, out, link, local, place=None, first=None):
        super().__init__(link, local, place, first)
        self.src, self.out = src, out

    def moves(self, k):
        z, y, x, c = self.at
        out, a, b = self.out, self.half_a, self.half_b
        if k == 0:
            here = out.at[z, y, x, c]
            return [self.copy(i, self.src, here, peer) for i, peer in enumerate(self.to_z)]
        same = lambda slot, ref, peer: self.copy(slot, ref, ref, peer)
        if k == 1:
            return [
                same(3, out.at[a, y, x, c], self.to_x),
                same(4, out.at[b, y, x, c], self.to_y),
            ]
        if k == 2:
            return [
                same(5, out.at[a, y, :, c], self.to_y),
                same(6, out.at[b, :, x, c], self.to_x),
            ]
        if k == 3:
            return [same(7, out.at[:, y, x, c], self.to_core)]
        if k == 4:
            return [
                same(8, out.at[a, y, self.nx, c], self.to_core),
                same(9, out.at[b, self.ny, x, c], self.to_core),
            ]
        return [
            same(10, out.at[a, self.ny, :, c], self.to_core),
            same(11, out.at[b, :, self.nx, c], self.to_core),
        ]

    def keep(self):
        return pltpu.make_async_copy(self.src, self.out.at[self.at], self.local)

    def s0(self):
        self.start(0)
        self.keep().start()

    def s1(self):
        self.keep().wait()
        self.arrive(0)
        self.start(1)
        self.start(3)

    def s2(self):
        self.arrive(1)
        self.start(2)
        self.start(4)

    def s3(self):
        self.arrive(2)
        self.start(5)

    def s4(self):
        for k in (3, 4, 5):
            self.arrive(k)


class Reduce(Piece):
    SEMS = 8
    BUFFERS = 6

    def __init__(
        self, src, out, own, held, l1a, l1b, l2a, l2b, l3, link, local, place=None, first=None,
        early=False,
    ):
        super().__init__(link, local, place, first)
        self.src, self.out, self.own, self.held = src, out, own, held
        self.l1a, self.l1b, self.l2a, self.l2b, self.l3 = l1a, l1b, l2a, l2b, l3
        self.UNSENT = (1, 2, 3) if early else (0, 1, 2, 3)

    @staticmethod
    def scratch(rows, width):
        buffer = lambda *lead: pltpu.VMEM(lead + (rows, width), BF16)
        half = SIDE_DP // 2
        return [
            buffer(SIDE_DP, 2, 2), buffer(half, 2), buffer(half, 2), buffer(half), buffer(half),
            buffer(SIDE_DP - 1),
        ]

    def moves(self, k):
        z, y, x, c = self.at
        held, a, b = self.held, self.half_a, self.half_b
        if k == 0:
            return [self.copy(0, self.src.at[:, :, :, self.nc], held, self.to_core)]
        if k == 1:
            return [
                self.copy(1, held.at[a, self.ny], self.l1a, self.to_y),
                self.copy(2, held.at[b, :, self.nx], self.l1b, self.to_x),
            ]
        if k == 2:
            return [
                self.copy(3, held.at[a, y, self.nx], self.l2a, self.to_x),
                self.copy(4, held.at[b, self.ny, x], self.l2b, self.to_y),
            ]
        return [
            self.copy(5 + i, held.at[other, y, x], self.l3.at[i], peer)
            for i, (other, peer) in enumerate(zip(self.other_z, self.to_z))
        ]

    def keep(self):
        return pltpu.make_async_copy(self.src.at[:, :, :, self.at[3]], self.own, self.local)

    def s0(self):
        self.start(0)
        if self.own is not None:
            self.keep().start()

    def s1(self):
        held = self.held
        if self.own is not None:
            self.keep().wait()
            self.arrive(0)
            held[...] = held[...] + self.own[...]
        else:
            self.arrive(0)
            held[...] = held[...] + self.src[:, :, :, self.at[3]]
        self.start(1)

    def s2(self):
        z, y, x, c = self.at
        self.arrive(1)
        held, a, b = self.held, self.half_a, self.half_b
        held[a, y] = held[a, y] + self.l1a[...]
        held[b, :, x] = held[b, :, x] + self.l1b[...]
        self.start(2)

    def s3(self):
        z, y, x, c = self.at
        self.arrive(2)
        held, a, b = self.held, self.half_a, self.half_b
        held[a, y, x] = held[a, y, x] + self.l2a[...]
        held[b, y, x] = held[b, y, x] + self.l2b[...]
        self.start(3)

    def s4(self):
        z, y, x, c = self.at
        self.arrive(3)
        total = self.held[z, y, x].astype(F32)
        for k in range(SIDE_DP - 1):
            total = total + self.l3[k].astype(F32)
        self.out[...] = total


class Swap(Piece):
    SEMS = 1
    UNSENT = (0,)

    def __init__(self, src, out, link, place):
        super().__init__(link, None, place)
        z, y, x, c = self.at
        self.src, self.out = src, out
        self.peer = device(z + 1 - 2 * lax.rem(z, 2), y, x, c)

    def moves(self, k):
        return [self.copy(0, self.src, self.out, self.peer)]


class SumSmall(Piece):
    SEMS = 6
    UNSENT = ()

    def __init__(self, total, near, far, link):
        super().__init__(link, None)
        self.total, self.near, self.far = total, near, far

    def moves(self, k):
        if k < 3:
            peer = (self.to_core, self.to_y, self.to_x)[k]
            return [self.copy(k, self.total, self.near.at[k], peer)]
        return [
            self.copy(3 + i, self.total, self.far.at[i], peer) for i, peer in enumerate(self.to_z)
        ]

    def add(self, k):
        self.arrive(k)
        self.sent(k)
        if k < 3:
            self.total[...] = self.total[...] + self.near[k]
        else:
            total = self.total[...]
            for i in range(SIDE_DP - 1):
                total = total + self.far[i]
            self.total[...] = total

    def s0(self):
        self.start(0)

    def s1(self):
        self.add(0)
        self.start(1)

    def s2(self):
        self.add(1)
        self.start(2)

    def s3(self):
        self.add(2)
        self.start(3)

    def s4(self):
        self.add(3)


FORWARD_SQUARES = 5


def bias_tables(table):
    lane = lax.broadcasted_iota(jnp.int32, (NB, 4 * LANES), 1)
    bucket = bucket_of(jnp.maximum(LANES - lane, 0))
    bucket = jnp.where(lane <= LANES, bucket, NB - 1)
    row = lax.broadcasted_iota(jnp.int32, (NB, 4 * LANES), 0)
    last = jnp.where(row == NB - 1, 1.0, 0.0)
    hot = jnp.where(row == bucket, 1.0, 0.0) - last
    near = tn(table.astype(BF16), hot.astype(BF16))
    far = tn(table.astype(BF16), last[:, :LANES].astype(BF16))
    return near[:16], far[:16]


def self_forward_kernel(joined, length_ref, x_ref, *refs):
    step = pl.program_id(0)
    last = pl.num_programs(0) - 1
    length = length_ref[own_index() if joined else 0]
    if joined:
        (raw_ref, enc_hbm), shards, refs = refs[:2], refs[2:12], refs[12:]
    else:
        (gain_in, wq_ref, wk_ref, wv_ref, table_in), refs = refs[:5], refs[5:]
    (q_ref, k_ref, v_ref, o_ref, p_ref, a_ref), refs = refs[:6], refs[6:]
    if joined:
        (wq_ref, wk_ref, wv_ref, gain_ref), refs = refs[:4], refs[4:]
        squares, (wide_ref, enc_other) = (
            refs[:FORWARD_SQUARES], refs[FORWARD_SQUARES : FORWARD_SQUARES + 2]
        )
        tile_ref, near_ref, far_ref, got_ref, small_src, got_small, send, recv, local = refs[
            FORWARD_SQUARES + 2 :
        ]
        link, place = Link(send, recv), Place()
        first = [Gather(shards[i], got_ref.at[i], link, local.at[i], place) for i in range(3)]
        first.append(Gather(small_src, got_small, link, local.at[3], place))
        swap = Swap(enc_hbm, enc_other, link, place)
        second = [
            Gather(shards[3 + i], squares[i], link, local.at[4 + i], place)
            for i in range(FORWARD_SQUARES)
        ]
        part = wide_ref.shape[-2]
        third = [
            Gather(
                shards[8 + m].at[k * part : (k + 1) * part], wide_ref.at[k, m], link,
                local.at[9 + 2 * k + m], place,
            )
            for k in range(CHUNKS)
            for m in range(2)
        ]
    else:
        tile_ref, near_ref, far_ref = refs
    seq, model = x_ref.shape
    width = q_ref.shape[1]

    def normed():
        return unit_rows(x_ref[...].astype(F32))[0]

    def set_tables(table):
        near, far = bias_tables(table)
        near_ref[...] = near
        far_ref[...] = far

    @pl.when(step == 0)
    def _():
        if not joined:
            a_ref[...] = (normed() * gain_in[0:1, :]).astype(BF16)
            set_tables(table_in[...])
            return
        rows_in, model_cols = raw_ref.shape[1], model
        entry = lax.broadcasted_iota(jnp.int32, (rows_in, model_cols), 0)
        column = lax.broadcasted_iota(jnp.int32, (rows_in, model_cols), 1)
        spread = lambda at: nn(raw_ref[...], jnp.where(column == entry + at, 1.0, 0.0).astype(BF16))
        is_table = lax.broadcasted_iota(jnp.int32, (8, model_cols), 0) == 3
        small_src[...] = jnp.where(
            is_table, spread(0), spread(own_index() * rows_in)
        ).astype(BF16)
        greet_peers()
        for piece in first:
            piece.stage(0)
        swap.start(0)
        unit = normed()
        for piece in first:
            piece.stage(1)
        for piece in second:
            piece.stage(0)
        for piece in first:
            piece.stage(2)
        first[3].stage(3)
        first[3].stage(4)
        small = got_small[...].astype(F32).reshape(NB, 8, model)
        gains = jnp.sum(small, axis=0)
        gain_ref[...] = gains
        which = lax.broadcasted_iota(jnp.int32, (NB, 8, LANES), 1)
        set_tables(jnp.sum(jnp.where(which == 3, small[:, :, :LANES], 0.0), axis=1))
        a_ref[...] = (unit * gains[0:1, :]).astype(BF16)
        for piece in first[:3]:
            piece.stage(3)
        for i, full_ref in enumerate((wq_ref, wk_ref, wv_ref)):
            first[i].stage(4)
            full_ref[...] = got_ref[i].astype(F32).reshape(model, model).astype(BF16)
        for piece in second:
            piece.stage(1)
        for piece in third[:2]:
            piece.stage(0)

    if joined:

        @pl.when(step == 1)
        def _():
            for piece in second:
                piece.stage(2)
            for piece in third[2:4]:
                piece.stage(0)

        @pl.when(step == 2)
        def _():
            for piece in third[:2]:
                piece.stage(1)
            for piece in third[4:]:
                piece.stage(0)

    for w_ref, out_ref in ((wq_ref, q_ref), (wk_ref, k_ref), (wv_ref, v_ref)):
        if joined:
            weights = w_ref[:, pl.ds(pl.multiple_of(step * width, LANES), width)]
        else:
            weights = w_ref[...]
        out_ref[...] = nn(a_ref[...], weights).astype(BF16)

    key_pos = lax.broadcasted_iota(jnp.int32, (seq, 1), 0)
    key_dead = key_pos >= length
    row = lax.broadcasted_iota(jnp.int32, (ROWS, ROWS + LANES), 0)
    col = lax.broadcasted_iota(jnp.int32, (ROWS, ROWS + LANES), 1)
    ahead = col - LANES > row
    for pair in range(width // LANES):
        cols = slice(pair * LANES, (pair + 1) * LANES)
        outs = [None] * (seq // ROWS)
        for which in range(2):
            local = pair * 2 + which
            head = step * (width // DH) + local
            spun = pltpu.roll(
                jnp.broadcast_to(near_ref[pl.ds(head, 1), :], (ROWS, 4 * LANES)),
                0, 1, stride=1, stride_axis=0,
            )
            tile_ref[...] = jnp.where(ahead, MASKED, spun[:, : ROWS + LANES])
            own = head_lane((seq, LANES), which)
            extra = lax.broadcasted_iota(jnp.int32, (seq, LANES), 1) == (DH if which == 0 else 0)
            far = jnp.where(key_dead, MASKED, far_ref[pl.ds(head, 1), 0:1]).astype(BF16)
            keys = jnp.where(own, k_ref[:, cols], jnp.where(extra, far, jnp.zeros((), BF16)))
            values = jnp.where(own, v_ref[:, cols], jnp.zeros((), BF16))
            queries = jnp.where(own, q_ref[:, cols], jnp.where(extra, 1.0, 0.0).astype(BF16))
            for blk in range(seq // ROWS):
                rows = slice(blk * ROWS, (blk + 1) * ROWS)
                span = (blk + 1) * ROWS
                cut = max(span - ROWS - LANES, 0)
                scores = nt(queries[rows], keys[:span])
                if cut:
                    near = scores[:, cut:] + tile_ref[...]
                    scores = jnp.concatenate([scores[:, :cut], near], axis=1)
                elif span == ROWS:
                    scores = scores + tile_ref[:, LANES:]
                else:
                    near = scores[:, ROWS - LANES :] + tile_ref[...]
                    scores = jnp.concatenate([scores[:, : ROWS - LANES], near], axis=1)
                top = jnp.max(scores, axis=1, keepdims=True)
                weights = jnp.exp(scores - top)
                total = jnp.sum(weights, axis=1, keepdims=True)
                probs = (weights * (1.0 / total)).astype(BF16)
                p_ref[local, rows, :span] = probs
                mixed = nn(probs, values[:span])
                outs[blk] = mixed if outs[blk] is None else outs[blk] + mixed
        for blk in range(seq // ROWS):
            o_ref[blk * ROWS : (blk + 1) * ROWS, cols] = outs[blk].astype(BF16)

    if joined:

        @pl.when(step == last)
        def _():
            for stage in (3, 4):
                for piece in second:
                    piece.stage(stage)
            for piece in third[:2]:
                piece.arrive(1)
                piece.arrive(3)
            for piece in third[2:]:
                piece.keep().wait()
                piece.arrive(0)
            swap.arrive(0)
            for piece in first + second + [swap]:
                piece.drain()
            for i, piece in enumerate(third):
                for k in (0, 1, 3) if i < 2 else (0,):
                    piece.sent(k)


def self_forward(length, x, shards, full, raw=None, enc=None):
    seq, model = x.shape
    width = 256
    heads = width // DH
    steps = model // width
    joined = full is None
    whole = lambda shape: pl.BlockSpec(shape, lambda i: (0,) * len(shape))
    held = lambda shape: pl.BlockSpec(
        shape, lambda i: (0,) * len(shape), pipeline_mode=pl.Buffered(1)
    )
    anywhere = pl.BlockSpec(memory_space=pl.ANY)
    smem = pl.BlockSpec(memory_space=pltpu.SMEM)
    columns = pl.BlockSpec((seq, width), lambda i: (0, i))
    weight = pl.BlockSpec((model, width), lambda i: (0, i))
    in_specs = [smem, held((seq, model))]
    out_specs = [
        columns, columns, columns, columns,
        pl.BlockSpec((heads, seq, seq), lambda i: (i, 0, 0)), whole((seq, model)),
    ]
    out_shape = [jax.ShapeDtypeStruct((seq, model), BF16)] * 4 + [
        jax.ShapeDtypeStruct((H, seq, seq), BF16), jax.ShapeDtypeStruct((seq, model), BF16),
    ]
    scratch = [
        pltpu.VMEM((ROWS, ROWS + LANES), F32), pltpu.VMEM((16, 4 * LANES), F32),
        pltpu.VMEM((16, LANES), F32),
    ]
    params = dict(vmem_limit_bytes=62 * 1024 * 1024)
    if joined:
        lead = (SIDE_DP, 2, 2, 2)
        part = shards[0].shape[0]
        wide = (CHUNKS, 2) + lead + (shards[8].shape[0] // CHUNKS, model)
        ins = [raw, enc] + list(shards)
        in_specs += [whole(raw.shape)] + [anywhere] * (len(ins) - 1)
        square = jax.ShapeDtypeStruct((model, model), BF16)
        out_shape += [square] * 3 + [jax.ShapeDtypeStruct((8, model), F32)]
        out_specs += [whole((model, model))] * 3 + [whole((8, model))]
        out_shape += [jax.ShapeDtypeStruct(lead + (part, model), BF16)] * FORWARD_SQUARES
        out_shape += [jax.ShapeDtypeStruct(wide, BF16), jax.ShapeDtypeStruct(enc.shape, BF16)]
        out_specs += [anywhere] * (FORWARD_SQUARES + 2)
        count = 4 + FORWARD_SQUARES + 2 * CHUNKS
        scratch += [
            pltpu.VMEM((3,) + lead + (part, model), BF16), pltpu.VMEM((8, model), BF16),
            pltpu.VMEM(lead + (8, model), BF16),
            pltpu.SemaphoreType.DMA((count * Gather.SEMS + 1,)),
            pltpu.SemaphoreType.DMA((count * Gather.SEMS + 1,)),
            pltpu.SemaphoreType.DMA((count,)),
        ]
        params.update(collective_id=1, has_side_effects=True)
    else:
        ins = list(full)
        in_specs += [whole((8, model)), weight, weight, weight, whole((NB, LANES))]
    return pl.pallas_call(
        functools.partial(self_forward_kernel, joined),
        grid=(steps,),
        in_specs=in_specs,
        out_specs=out_specs,
        out_shape=out_shape,
        scratch_shapes=scratch,
        compiler_params=pltpu.CompilerParams(**params),
        cost_estimate=pl.CostEstimate(
            flops=6 * seq * model * model + 4 * seq * seq * model,
            bytes_accessed=2 * H * seq * seq + 16 * seq * model,
            transcendentals=H * seq * seq,
        ),
        name="self_forward",
    )(length, x, *ins)


def middle_kernel(joined, length_ref, gain_ref, *refs):
    if joined:
        (dealing_ref, other_hbm), refs = refs[:2], refs[2:]
    length = length_ref[own_index() if joined else 0]
    (x_hbm, o_hbm, cot_hbm, enc_hbm, wo_hbm, cq_hbm, ck_hbm, cv_hbm, co_hbm), refs = (
        refs[:9], refs[9:]
    )
    wide_hbm, refs = refs[0], refs[1:]
    (out_hbm, g1_hbm, egrad_ref, gain_grad_ref), refs = refs[:4], refs[4:]
    squares, refs = refs[:5], refs[5:]
    sum_ref, refs = refs[0], refs[1:]
    if joined:
        wide_hbm, refs = refs[0], refs[1:]
    (
        o_ref, g_ref, a2_ref, cq_scr, mix_ref, a3_ref, r_ref, du_ref, prob_ref,
        x1_ref, x2_ref, acc_ref, dy_ref, enc_ref, keys_ref, values_ref, dk_acc, dv_acc,
        wo_ref, cq_ref, ck_ref, cv_ref, co_ref, wide_ref, src_ref, load_sem, wide_sem, out_sem,
    ), refs = refs[:28], refs[28:]
    seq, model = o_ref.shape
    xr_ref = du_ref.at[:, :model]
    blocks = seq // ROWS
    pairs = model // LANES
    zero = jnp.zeros((), BF16)
    gain_cross = gain_ref[1:2, :]
    gain_ffn = gain_ref[2:3, :]

    loads = [
        pltpu.make_async_copy(src, dst, load_sem.at[i])
        for i, (src, dst) in enumerate(
            (
                (enc_hbm, enc_ref), (ck_hbm, ck_ref), (cv_hbm, cv_ref), (o_hbm, o_ref),
                (wo_hbm, wo_ref), (x_hbm, xr_ref), (cq_hbm, cq_ref), (cot_hbm, g_ref),
                (co_hbm, co_ref),
            )
            + (((other_hbm, keys_ref),) if joined else ())
        )
    ]
    for copy in loads:
        copy.start()

    chunk_rows = wide_ref.shape[2]

    def wide_loads(k):
        slot = lax.rem(k, 2)
        found = []
        for m in range(2):
            dst = wide_ref.at[slot, m]
            if joined:
                src = wide_hbm.at[k, m].reshape(chunk_rows, model)
            else:
                src = wide_hbm.at[m, k]
            found.append(pltpu.make_async_copy(src, dst, wide_sem.at[slot, m]))
        return found

    if joined:
        held, l1a, l1b, l2a, l2b, l3, rsend, rrecv, gsend, grecv = refs
        gather_link = Link(gsend, grecv)
        reduce_link = Link(rsend, rrecv)
        place = Place()
        part = chunk_rows // (SIDE_DP * SIDE_FSDP)

        def incoming(k):
            return [
                Gather(
                    None, wide_hbm.at[k, m], gather_link, None, place,
                    (2 * k + m) * Gather.SEMS,
                )
                for m in range(2)
            ]

        def leaving(k):
            at = pl.multiple_of(k * part, 8)
            found = []
            for m in range(2):
                i = 2 * k + m
                found.append(
                    Reduce(
                        src_ref.at[m], sum_ref.at[m, pl.ds(at, part)], None, held.at[i],
                        l1a.at[i], l1b.at[i], l2a.at[i], l2b.at[i], l3.at[i], reduce_link, None,
                        place, i * Reduce.SEMS,
                    )
                )
            return found

    def arriving(k, wait=(), start=(), when=None):
        if not joined:
            return

        def go():
            for piece in incoming(k):
                for round_idx in wait:
                    piece.arrive(round_idx)
            for piece in incoming(k):
                for round_idx in start:
                    piece.start(round_idx)

        go() if when is None else pl.when(when)(go)

    def reduce_stage(k, stage, when=None):
        if not joined:
            return

        def go():
            for piece in leaving(k):
                piece.stage(stage)

        go() if when is None else pl.when(when)(go)

    if joined:
        greet_peers()
        arriving(0, start=(2, 4))
        arriving(1, start=(1, 3))
    else:
        for copy in wide_loads(0):
            copy.start()

    for copy in loads[:3] + loads[9:]:
        copy.wait()
    if joined:
        mine = own_index()
        enc_ref[...] = jnp.where(dealing_ref[mine] == mine, enc_ref[...], keys_ref[...])
    keys_ref[...] = nn(enc_ref[...], ck_ref[...]).astype(BF16)
    values_ref[...] = nn(enc_ref[...], cv_ref[...]).astype(BF16)
    gain_grad_ref[...] = jnp.zeros_like(gain_grad_ref)
    for copy in loads[3:9]:
        copy.wait()

    def forward_rows(i, _):
        rows = pl.ds(pl.multiple_of(i * FORWARD_ROWS, FORWARD_ROWS), FORWARD_ROWS)
        pos = i * FORWARD_ROWS + lax.broadcasted_iota(jnp.int32, (FORWARD_ROWS, 1), 0)
        valid = jnp.where(pos < length, 1.0, 0.0).astype(F32)
        x1 = xr_ref[rows, :].astype(F32) + nn(o_ref[rows, :], wo_ref[...])
        x1_ref[rows, :] = x1
        unit2, _inv2 = unit_rows(x1)
        a2 = (unit2 * gain_cross).astype(BF16)
        a2_ref[rows, :] = a2
        cq = nn(a2, cq_ref[...]).astype(BF16)
        cq_scr[rows, :] = cq
        mixed = []
        for pair in range(pairs):
            cols = slice(pair * LANES, (pair + 1) * LANES)
            total_out = None
            for which in range(2):
                own = head_lane((FORWARD_ROWS, LANES), which)
                own_key = head_lane((keys_ref.shape[0], LANES), which)
                scores = nt(jnp.where(own, cq[:, cols], zero), keys_ref[:, cols])
                top = jnp.max(scores, axis=1, keepdims=True)
                weights = jnp.exp(scores - top)
                prob = (weights * (1.0 / jnp.sum(weights, axis=1, keepdims=True))).astype(BF16)
                at = (2 * pair + which) * keys_ref.shape[0]
                prob_ref[rows, at : at + keys_ref.shape[0]] = prob
                piece = nn(prob, jnp.where(own_key, values_ref[:, cols], zero))
                total_out = piece if total_out is None else total_out + piece
            mixed.append(total_out.astype(BF16))
        mix = jnp.concatenate(mixed, axis=1)
        mix_ref[rows, :] = mix
        x2 = x1 + nn(mix, co_ref[...])
        x2_ref[rows, :] = x2
        acc_ref[rows, :] = x2
        unit3, _inv3 = unit_rows(x2)
        a3_ref[rows, :] = (unit3 * gain_ffn).astype(BF16)
        g_ref[rows, :] = (g_ref[rows, :].astype(F32) * valid).astype(BF16)
        return 0

    lax.fori_loop(0, seq // FORWARD_ROWS, forward_rows, 0)

    def chunk(k, _):
        slot = lax.rem(k, 2)
        for copy in wide_loads(k):
            copy.wait()
        for i in range(seq // HIDDEN_ROWS):
            rows = slice(i * HIDDEN_ROWS, (i + 1) * HIDDEN_ROWS)
            z = nt(a3_ref[rows, :], wide_ref[slot, 0])
            zz = z * z
            t = jnp.tanh(GELU_C * z * (1.0 + GELU_A * zz))
            half = 0.5 + 0.5 * t
            r = (z * half).astype(BF16)
            r_ref[rows, :] = r
            slope = half + (0.5 * GELU_C) * z * (1.0 - t * t) * (1.0 + (3.0 * GELU_A) * zz)
            du = (nt(g_ref[rows, :], wide_ref[slot, 1]) * slope).astype(BF16)
            du_ref[rows, :] = du
            acc_ref[rows, :] += nn(r, wide_ref[slot, 1])
            dy_ref[rows, :] += nn(du, wide_ref[slot, 0])
            if i == seq // HIDDEN_ROWS // 2 - 1:
                arriving(2, wait=(2,), start=(5,), when=k == 1)
                reduce_stage(k - 1, 1, k >= 1)
        arriving(1, wait=(2,), start=(5,), when=k == 0)
        arriving(2, wait=(1,), start=(2, 4), when=k == 0)
        reduce_stage(k - 2, 3, k >= 2)

        @pl.when(k >= 1)
        def _():
            if joined:
                for piece in leaving(k - 1):
                    piece.sent(0)
            else:
                for copy in grad_copies(k - 1):
                    copy.wait()

        def next_loads():
            for copy in wide_loads(k + 1):
                copy.start()

        if not joined:
            pl.when(k + 1 < CHUNKS)(next_loads)
        shape = src_ref.shape[1:]
        src_ref[0] = tn(du_ref[...], a3_ref[...]).reshape(shape).astype(BF16)
        src_ref[1] = tn(r_ref[...], g_ref[...]).reshape(shape).astype(BF16)
        if joined:
            reduce_stage(k, 0)
            arriving(k + 1, wait=(3, 4, 5), when=k + 1 < CHUNKS)
            pl.when(k + 1 < CHUNKS)(next_loads)
            reduce_stage(k - 1, 2, k >= 1)
        else:
            for copy in grad_copies(k):
                copy.start()
        return 0

    def grad_copies(k):
        return [
            pltpu.make_async_copy(src_ref.at[m], sum_ref.at[m, k], out_sem.at[m])
            for m in range(2)
        ]

    dy_ref[...] = jnp.zeros_like(dy_ref)
    if joined:
        arriving(0, wait=(2,), start=(5,))
        arriving(1, wait=(1,), start=(2, 4))
        arriving(2, start=(1, 3))
        arriving(0, wait=(4, 5))
        for copy in wide_loads(0):
            copy.start()
    lax.fori_loop(0, CHUNKS, chunk, 0)

    g1_low_ref = a3_ref
    g2_low_ref = g_ref
    dcq_ref = cq_scr
    final = CHUNKS - 1

    dmix_ref = du_ref.at[:, :model]

    def out_copies(rows):
        return [
            pltpu.make_async_copy(acc_ref.at[rows, :], out_hbm.at[rows, :], out_sem.at[0]),
            pltpu.make_async_copy(dy_ref.at[rows, :], g1_hbm.at[rows, :], out_sem.at[1]),
        ]

    everything = pl.ds(0, seq)
    if not joined:
        for copy in grad_copies(final):
            copy.wait()
    for i in range(seq // BACK_ROWS):
        rows = slice(i * BACK_ROWS, (i + 1) * BACK_ROWS)
        pos = i * BACK_ROWS + lax.broadcasted_iota(jnp.int32, (BACK_ROWS, 1), 0)
        valid = jnp.where(pos < length, 1.0, 0.0).astype(F32)
        acc_ref[rows, :] = acc_ref[rows, :] * valid
        unit3, inv3 = unit_rows(x2_ref[rows, :])
        through, gain_part = norm_back(dy_ref[rows, :], unit3, inv3, gain_ffn)
        gain_grad_ref[1:2, :] += gain_part
        g2 = g_ref[rows, :].astype(F32) + through
        dy_ref[rows, :] = g2
        g2_low = g2.astype(BF16)
        g2_low_ref[rows, :] = g2_low
        dmix_ref[rows, :] = nt(g2_low, co_ref[...]).astype(BF16)
    out_copies(everything)[0].start()
    reduce_stage(2, 1)
    reduce_stage(1, 3)
    reduce_stage(0, 4)
    def backward_pair(pair, _):
        cols = pl.ds(pl.multiple_of(pair * LANES, LANES), LANES)
        dk = dv = None
        for i in range(seq // CROSS_ROWS):
            rows = slice(i * CROSS_ROWS, (i + 1) * CROSS_ROWS)
            dq = None
            for which in range(2):
                own = head_lane((CROSS_ROWS, LANES), which)
                own_key = head_lane((keys_ref.shape[0], LANES), which)
                at = pl.multiple_of((2 * pair + which) * keys_ref.shape[0], LANES)
                prob_low = prob_ref[rows, pl.ds(at, keys_ref.shape[0])]
                prob = prob_low.astype(F32)
                d_out = jnp.where(own, dmix_ref[rows, cols], zero)
                dp = nt(d_out, values_ref[:, cols])
                ds = prob * (dp - jnp.sum(prob * dp, axis=1, keepdims=True))
                ds_low = ds.astype(BF16)
                dv_part = tn(prob_low, d_out)
                dk_part = tn(ds_low, jnp.where(own, cq_scr[rows, cols], zero))
                piece = nn(ds_low, jnp.where(own_key, keys_ref[:, cols], zero))
                dq = piece if dq is None else dq + piece
                dk = dk_part if dk is None else dk + dk_part
                dv = dv_part if dv is None else dv + dv_part
            dcq_ref[rows, cols] = dq.astype(BF16)
        dk_acc[:, cols] = dk
        dv_acc[:, cols] = dv
        return 0

    lax.fori_loop(0, pairs, backward_pair, 0)
    reduce_stage(2, 2)
    for i in range(seq // BACK_ROWS):
        rows = slice(i * BACK_ROWS, (i + 1) * BACK_ROWS)
        unit2, inv2 = unit_rows(x1_ref[rows, :])
        through, gain_part = norm_back(
            nt(dcq_ref[rows, :], cq_ref[...]), unit2, inv2, gain_cross
        )
        gain_grad_ref[0:1, :] += gain_part
        g1 = dy_ref[rows, :] + through
        dy_ref[rows, :] = g1
        g1_low_ref[rows, :] = g1.astype(BF16)
    out_copies(everything)[1].start()

    reduce_stage(1, 4)
    dk = dk_acc[...].astype(BF16)
    dv = dv_acc[...].astype(BF16)
    egrad_ref[...] = nt(dk, ck_ref[...]) + nt(dv, cv_ref[...])
    made = (
        (cq_ref, lambda: tn(a2_ref[...], dcq_ref[...])),
        (ck_ref, lambda: tn(enc_ref[...], dk)),
        (cv_ref, lambda: tn(enc_ref[...], dv)),
        (co_ref, lambda: tn(mix_ref[...], g2_low_ref[...])),
        (wo_ref, lambda: tn(o_ref[...], g1_low_ref[...])),
    )
    writes = []
    for i, (buffer, make) in enumerate(made):
        buffer[...] = make().astype(BF16)
        if i == 2:
            reduce_stage(final, 3)
        writes.append(pltpu.make_async_copy(buffer, squares[i], load_sem.at[i]))
        writes[-1].start()
    reduce_stage(final, 4)
    for copy in writes:
        copy.wait()
    for copy in out_copies(everything):
        copy.wait()
    if joined:
        for k, rounds in enumerate(((2, 4, 5), (1, 2, 3, 4, 5), (1, 2, 3, 4, 5))):
            for piece in incoming(k):
                for round_idx in rounds:
                    piece.sent(round_idx)
        for k in range(CHUNKS):
            for piece in leaving(k):
                for round_idx in (0, 1, 2, 3) if k == final else (1, 2, 3):
                    piece.sent(round_idx)


def middle(
    length, x, o, cot, enc, gains, wo, cq, ck, cv, co, wide, joined, dealing=None, other=None
):
    seq, model = x.shape
    enc_len = enc.shape[0]
    anywhere = pl.BlockSpec(memory_space=pl.ANY)
    vmem = pl.BlockSpec(memory_space=pltpu.VMEM)
    smem = pl.BlockSpec(memory_space=pltpu.SMEM)
    low = lambda *shape: pltpu.VMEM(shape, BF16)
    full = lambda *shape: pltpu.VMEM(shape, F32)
    ins = [x, o, cot, enc, wo, cq, ck, cv, co, wide]
    square = jax.ShapeDtypeStruct((model, model), BF16)
    out_shape = [
        jax.ShapeDtypeStruct((seq, model), F32),
        jax.ShapeDtypeStruct((seq, model), F32),
        jax.ShapeDtypeStruct((enc_len, model), F32),
        jax.ShapeDtypeStruct((2, model), F32),
    ] + [square] * 5
    out_specs = [anywhere, anywhere, vmem, vmem] + [anywhere] * 5
    hidden = 4 * model
    chunk_rows = hidden // CHUNKS
    rows_low = [low(seq, model)] * 6 + [low(seq, chunk_rows)] * 2
    params = dict(vmem_limit_bytes=63 * 1024 * 1024)
    if joined:
        part = chunk_rows // (SIDE_DP * SIDE_FSDP)
        lead = (SIDE_DP, 2, 2, 2)
        out_shape += [
            jax.ShapeDtypeStruct((2, CHUNKS * part, model), F32),
            jax.ShapeDtypeStruct(wide.shape, BF16),
        ]
        out_specs += [vmem, anywhere]
        gather_sems = 2 * CHUNKS * Gather.SEMS
        aliases = {4 + len(ins) - 1: len(out_shape) - 1}
        src = low(2, *lead, part, model)
        count = 2 * CHUNKS
        reduce_sems = count * Reduce.SEMS
        extra = [
            pltpu.VMEM((count,) + buffer.shape, BF16) for buffer in Reduce.scratch(part, model)
        ] + [
            pltpu.SemaphoreType.DMA((reduce_sems,)), pltpu.SemaphoreType.DMA((reduce_sems,)),
            pltpu.SemaphoreType.DMA((gather_sems,)), pltpu.SemaphoreType.DMA((gather_sems,)),
        ]
        params.update(collective_id=2, has_side_effects=True)
    else:
        out_shape += [jax.ShapeDtypeStruct((2, CHUNKS, chunk_rows, model), BF16)]
        out_specs += [anywhere]
        src = low(2, chunk_rows, model)
        extra = []
        aliases = {}
    return pl.pallas_call(
        functools.partial(middle_kernel, joined),
        in_specs=[smem, vmem] + ([smem, anywhere] if joined else []) + [anywhere] * len(ins),
        out_specs=out_specs,
        out_shape=out_shape,
        scratch_shapes=rows_low
        + [
            low(seq, H * enc_len), full(seq, model), full(seq, model), full(seq, model),
            full(seq, model), low(enc_len, model), low(enc_len, model), low(enc_len, model),
            full(enc_len, model), full(enc_len, model),
        ]
        + [low(model, model)] * 5
        + [
            low(2, 2, chunk_rows, model), src,
            pltpu.SemaphoreType.DMA((10,)), pltpu.SemaphoreType.DMA((2, 2)),
            pltpu.SemaphoreType.DMA((2,)),
        ]
        + extra,
        input_output_aliases=aliases,
        compiler_params=pltpu.CompilerParams(**params),
        name="middle",
    )(length, gains, *([dealing, other] if joined else []), *ins)


def gather_weights(shards, axes):
    pile = lax.all_gather(jnp.concatenate(shards, axis=0), axes, axis=0)
    full, at = [], 0
    for shard in shards:
        full.append(pile[:, at : at + shard.shape[0]].reshape(-1, pile.shape[-1]))
        at += shard.shape[0]
    return full


def reduce_grads(grads, axes):
    dev_count = lax.axis_size("dp") * lax.axis_size("fsdp")
    split = [g.reshape(dev_count, -1, g.shape[-1]) for g in grads]
    pile = lax.psum_scatter(
        jnp.concatenate(split, axis=1), axes, scatter_dimension=0, tiled=False
    ).astype(F32)
    sums, at = [], 0
    for s in split:
        sums.append(pile[at : at + s.shape[1]])
        at += s.shape[1]
    return sums


HIST = 2 * LANES


def self_backward_kernel(
    far_count, x_ref, gain_ref, mid_gain_ref, a_ref, g1_ref, q_ref, k_ref, v_ref, p_ref,
    wo_ref, wq_ref, wk_ref, wv_ref, *refs,
):
    joined = far_count is not None
    if joined:
        egrad_ref, far_refs = refs[0], refs[1 : far_count + 1]
        ingrad_ref, sum_ref, near_sum_ref, small_ref, egrad_other = refs[
            far_count + 1 : far_count + 6
        ]
        rest = refs[far_count + 6 :]
    else:
        ingrad_ref, gw_ref, small_ref, hist_out = refs[:4]
        rest = refs[4:]
    low_ref, near_acc, dk_acc, dv_acc, dq_scr, hist_ref = rest[:6]
    rest = rest[6:]
    step = pl.program_id(0)
    last = pl.num_programs(0) - 1
    seq, model = x_ref.shape
    width = q_ref.shape[1]
    heads = width // DH
    steps = model // width
    events = {}
    if joined:
        src_ref, own_ref, near_small, far_small, send, recv, local = rest[-7:]
        link = Link(send, recv)
        part = sum_ref.shape[0] // far_count
        pieces = []
        for i in range(far_count + steps):
            far = i < far_count
            pieces.append(
                Reduce(
                    far_refs[i] if far else src_ref.at[(i - far_count) % 2],
                    (sum_ref if far else near_sum_ref).at[
                        (i if far else i - far_count) * part
                        : (i + 1 if far else i + 1 - far_count) * part
                    ],
                    own_ref.at[i] if far else None,
                    *rest[Reduce.BUFFERS * i : Reduce.BUFFERS * (i + 1)], link,
                    local.at[i], early=far_count <= i < far_count + steps - 2,
                )
            )
        small = SumSmall(small_ref, near_small, far_small, link)
        swap = Swap(egrad_ref, egrad_other, link, Place())
        far_times = [(0, 1, 3, 4, 7), (0, 1, 3, 5, 7), (0, 1, 4, 5, 8), (0, 2, 4, 5, 7)]
        far_times += [(0, 3, 5, 7, 9)] * (far_count - len(far_times))
        near_times = [(2, 3, 4, 8), (3, 5, 6, 9), (4, 5, 6, 8), (5, 6, 8, 10), (5, 6, 8, 10)]
        near_times += [(7, 8, 9, 10)] * (steps - len(near_times))
        for i in range(far_count):
            for k, time in enumerate(far_times[i]):
                events.setdefault(time, []).append((-k, pieces[i]))
        for i in range(steps):
            for k, time in enumerate(near_times[i]):
                events.setdefault(time, []).append((-k - 1, pieces[far_count + i]))

    def tick(time):
        for k, piece in sorted(events.get(time, []), key=lambda event: event[0]):
            piece.stage(-k)

    @pl.when(step == 0)
    def _():
        if joined:
            greet_peers()
            tick(0)
            swap.start(0)
        low_ref[...] = g1_ref[...].astype(BF16)
        hist_ref[...] = jnp.zeros_like(hist_ref)

    for g in range(1, steps):
        if events.get(g):
            pl.when(step == g)(functools.partial(tick, g))

    d_all = nt(low_ref[...], wo_ref[...]).astype(BF16)
    zero = jnp.zeros((), BF16)
    for pair in range(width // LANES):
        cols = slice(pair * LANES, (pair + 1) * LANES)
        dk_acc[...] = jnp.zeros_like(dk_acc)
        dv_acc[...] = jnp.zeros_like(dv_acc)
        dq_blocks = [None] * (seq // ROWS)
        for which in range(2):
            local_head = pair * 2 + which
            head = step * heads + local_head
            own = head_lane((seq, LANES), which)
            d_out = jnp.where(own, d_all[:, cols], zero)
            queries = jnp.where(own, q_ref[:, cols], zero)
            keys = jnp.where(own, k_ref[:, cols], zero)
            for blk in range(seq // ROWS):
                rows = slice(blk * ROWS, (blk + 1) * ROWS)
                span = (blk + 1) * ROWS
                prob_low = p_ref[local_head, rows, :span]
                prob = prob_low.astype(F32)
                dp = nt(d_out[rows], v_ref[:span, cols])
                ds = prob * (dp - jnp.sum(prob * dp, axis=1, keepdims=True))
                if blk == 0:
                    near_acc[:, :LANES] = jnp.zeros((ROWS, LANES), F32)
                    near_acc[:, LANES:] = ds
                else:
                    near_acc[...] += ds[:, span - ROWS - LANES :]
                ds_low = ds.astype(BF16)
                part_q = nn(ds_low, keys[:span])
                dq_blocks[blk] = part_q if which == 0 else dq_blocks[blk] + part_q
                dk_acc[:span, :] += tn(ds_low, queries[rows])
                dv_acc[:span, :] += tn(prob_low, d_out[rows])
            padded = jnp.concatenate([near_acc[...], jnp.zeros((ROWS, LANES), F32)], axis=1)
            count = ROWS
            while count > 1:
                count //= 2
                padded = padded[:count] + pltpu.roll(padded[count:], 4 * LANES - count, 1)
            hist_ref[pl.ds(head, 1), :] = padded[:, :HIST]
        dq = jnp.concatenate([block.astype(BF16) for block in dq_blocks], axis=0)
        dk = dk_acc[...].astype(BF16)
        dv = dv_acc[...].astype(BF16)
        at = pl.ds(pl.multiple_of(step * width + pair * LANES, LANES), LANES)
        for i, part_grad in enumerate((dq, dk, dv)):
            dq_scr[i, :, at] = part_grad

    @pl.when(step == last)
    def _():
        small_ref[...] = jnp.zeros_like(small_ref)
        small_ref[1:3, :model] = mid_gain_ref[...]
        small_ref[:, model : model + HIST] = hist_ref[0:8, :]
        small_ref[:, model + HIST :] = hist_ref[8:16, :]
        if joined:
            small.stage(0)

    grads = tn(a_ref[...], jnp.concatenate([dq, dk, dv], axis=1))
    if joined:
        for g in range(steps):

            @pl.when(step == g)
            def _():
                if g >= 2:
                    pieces[far_count + g - 2].sent(0)
                src_ref[g % 2] = grads.reshape(src_ref.shape[1:]).astype(BF16)
                pieces[far_count + g].stage(0)
                if g == steps - 1:
                    tick(steps)
    else:
        gw_ref[0] = grads.astype(BF16)

    @pl.when(step == last)
    def _():
        ingrad_ref[...] = nt(dq_scr[0], wq_ref[...])
        if joined:
            tick(steps + 1)
            small.stage(1)
        ingrad_ref[...] += nt(dq_scr[1], wk_ref[...])
        if joined:
            small.stage(2)
        ingrad_ref[...] += nt(dq_scr[2], wv_ref[...])
        if joined:
            tick(steps + 2)
            small.stage(3)
        unit, inv = unit_rows(x_ref[...].astype(F32))
        through, gain_part = norm_back(ingrad_ref[...], unit, inv, gain_ref[0:1, :])
        ingrad_ref[...] = g1_ref[...] + through
        if joined:
            tick(steps + 3)
            small.stage(4)
            swap.arrive(0)
            tick(steps + 4)
            link.drain()
        else:
            small_ref[0:1, :model] = gain_part
            hist_out[...] = hist_ref[...]


def self_backward(
    x, gain, mid_gain, a1, g1, q, k, v, p, wo, wq, wk, wv, far_grads, egrad=None
):
    seq, model = x.shape
    width = 128
    heads = width // DH
    steps = model // width
    joined = far_grads is not None
    held = lambda shape: pl.BlockSpec(
        shape, lambda i: (0,) * len(shape), pipeline_mode=pl.Buffered(1)
    )
    whole = lambda shape: pl.BlockSpec(shape, lambda i: (0,) * len(shape))
    columns = pl.BlockSpec((seq, width), lambda i: (0, i))
    weight_rows = pl.BlockSpec((width, model), lambda i: (i, 0))
    in_specs = [
        held((seq, model)), held((8, model)), held((2, model)), held((seq, model)),
        held((seq, model)), columns, columns, columns,
        pl.BlockSpec((heads, seq, seq), lambda i: (i, 0, 0)),
        weight_rows, held((model, model)), held((model, model)), held((model, model)),
    ]
    small = (8, model + 2 * HIST)
    out_specs = [whole((seq, model))]
    out_shape = [jax.ShapeDtypeStruct((seq, model), F32)]
    scratch = [
        pltpu.VMEM((seq, model), BF16),
        pltpu.VMEM((ROWS, ROWS + LANES), F32),
        pltpu.VMEM((seq, LANES), F32),
        pltpu.VMEM((seq, LANES), F32),
        pltpu.VMEM((3, seq, model), BF16),
        pltpu.VMEM((16, HIST), F32),
    ]
    extra = []
    params = dict(vmem_limit_bytes=63 * 1024 * 1024)
    if joined:
        count = len(far_grads)
        part = model // (SIDE_DP * SIDE_FSDP)
        across = 3 * width
        extra = [egrad] + [g.reshape(SIDE_DP, 2, 2, 2, part, model) for g in far_grads]
        in_specs += [pl.BlockSpec(memory_space=pl.ANY)] * (count + 1)
        shapes = ((count * part, model), (steps * part, across), small, egrad.shape)
        out_specs += [whole(s) for s in shapes[:3]] + [pl.BlockSpec(memory_space=pl.ANY)]
        out_shape += [jax.ShapeDtypeStruct(s, F32) for s in shapes]
        for i in range(count + steps):
            scratch += Reduce.scratch(part, model if i < count else across)
        sems = (count + steps) * Reduce.SEMS + SumSmall.SEMS + Swap.SEMS
        scratch += [
            pltpu.VMEM((2, SIDE_DP, 2, 2, 2, part, across), BF16),
            pltpu.VMEM((count, SIDE_DP, 2, 2, part, model), BF16),
            pltpu.VMEM((3,) + small, F32),
            pltpu.VMEM((SIDE_DP - 1,) + small, F32),
            pltpu.SemaphoreType.DMA((sems,)), pltpu.SemaphoreType.DMA((sems,)),
            pltpu.SemaphoreType.DMA((count + steps,)),
        ]
        params.update(collective_id=3, has_side_effects=True)
    else:
        count = None
        out_specs += [
            pl.BlockSpec((1, model, 3 * width), lambda i: (i, 0, 0)), whole(small),
            whole((16, HIST)),
        ]
        out_shape += [
            jax.ShapeDtypeStruct((steps, model, 3 * width), BF16),
            jax.ShapeDtypeStruct(small, F32),
            jax.ShapeDtypeStruct((16, HIST), F32),
        ]
    return pl.pallas_call(
        functools.partial(self_backward_kernel, count),
        grid=(steps,),
        in_specs=in_specs,
        out_specs=out_specs,
        out_shape=out_shape,
        scratch_shapes=scratch,
        compiler_params=pltpu.CompilerParams(**params),
        cost_estimate=pl.CostEstimate(
            flops=14 * seq * model * model + 8 * seq * seq * model,
            bytes_accessed=2 * H * seq * seq + 24 * seq * model,
            transcendentals=0,
        ),
        name="self_backward",
    )(x, gain, mid_gain, a1, g1, q, k, v, p, wo, wq, wk, wv, *extra)


def exact(left_op, right_op, dims):
    return lax.dot_general(
        left_op, right_op, (dims, ((), ())), preferred_element_type=F32,
        precision=lax.Precision.HIGHEST,
    )


def finish_kernel(
    dealing_ref, raw_ref, wq_ref, wk_ref, wv_ref, ccq_ref, sum_ref, near_ref, small_ref, wide_ref,
    egrad_ref, other_ref, out_in, ingrad_in, *refs,
):
    (
        out_ref, ingrad_ref, enc_ref, gq_ref, gk_ref, gv_ref, go_ref, gcq_ref, gck_ref, gcv_ref,
        gco_ref, gin_ref, gdown_ref, self_ref, cross_ref, ffn_ref, table_ref, through, sems,
    ) = refs
    pieces = []
    for i, (src, dst) in enumerate(((out_in, out_ref), (ingrad_in, ingrad_ref))):
        for j in range(src.shape[0] // ROWS):
            rows = slice(j * ROWS, (j + 1) * ROWS)
            pieces.append(
                (
                    pltpu.make_async_copy(src.at[rows], through.at[i, rows], sems.at[0, i, j]),
                    pltpu.make_async_copy(through.at[i, rows], dst.at[rows], sems.at[1, i, j]),
                )
            )
    for inward, _outward in pieces:
        inward.start()
    for inward, outward in pieces:
        inward.wait()
        outward.start()
    mine = own_index()
    part, model = gq_ref.shape
    steps = near_ref.shape[0] // part
    width = near_ref.shape[1] // 3
    for ref, i in ((gcq_ref, 0), (gck_ref, 1), (gcv_ref, 2), (gco_ref, 3), (go_ref, 4)):
        ref[...] = sum_ref[i * part : (i + 1) * part, :]
    for g in range(steps):
        for i, ref in enumerate((gq_ref, gk_ref, gv_ref)):
            ref[:, g * width : (g + 1) * width] = near_ref[
                g * part : (g + 1) * part, i * width : (i + 1) * width
            ]
    gin_ref[...] = wide_ref[0]
    gdown_ref[...] = wide_ref[1]
    enc_ref[...] = jnp.where(dealing_ref[mine] == mine, egrad_ref[...], other_ref[...])
    ones = jnp.ones((8, model), F32)
    gains = raw_ref[...].astype(F32)
    weighted = (
        gq_ref[...] * wq_ref[...].astype(F32) + gk_ref[...] * wk_ref[...].astype(F32)
        + gv_ref[...] * wv_ref[...].astype(F32)
    )
    self_ref[...] = exact(ones, weighted, ((1,), (1,)))[0:1, :] / gains[0:1, :part]
    weighted = gcq_ref[...] * ccq_ref[...].astype(F32)
    cross_ref[...] = exact(ones, weighted, ((1,), (1,)))[0:1, :] / gains[1:2, :part]
    entry = lax.broadcasted_iota(jnp.int32, (part, model), 0)
    column = lax.broadcasted_iota(jnp.int32, (part, model), 1)
    place = jnp.where(column == entry + mine * part, 1.0, 0.0)
    ffn_ref[...] = exact(small_ref[:, :model], place, ((1,), (1,)))[2:3, :]
    lane = lax.broadcasted_iota(jnp.int32, (16, HIST), 1)
    distance = LANES - lane
    bucket = bucket_of(jnp.maximum(distance, 0))
    usable = (distance >= 0) & (bucket < NB - 1)
    picked = usable & ((bucket == mine) | (mine == NB - 1))
    sign = jnp.where(mine == NB - 1, -1.0, 1.0)
    hist = jnp.concatenate(
        [small_ref[:, model : model + HIST], small_ref[:, model + HIST :]], axis=0
    )
    sums = exact(ones[:, :HIST], jnp.where(picked, hist, 0.0), ((1,), (1,)))
    table_ref[...] = sign * sums[0:1, : table_ref.shape[1]]
    for _inward, outward in pieces:
        outward.wait()


def finish(dealing, raw, shards, sums, near, small, wide, egrad, other, out, in_grad):
    part, model = shards[0].shape
    anywhere = pl.BlockSpec(memory_space=pl.ANY)
    vmem = pl.BlockSpec(memory_space=pltpu.VMEM)
    f32 = lambda *shape: jax.ShapeDtypeStruct(shape, F32)
    square = f32(part, model)
    hidden_part = wide.shape[1]
    return pl.pallas_call(
        finish_kernel,
        in_specs=[pl.BlockSpec(memory_space=pltpu.SMEM)] + [vmem] * 11 + [anywhere] * 2,
        out_specs=[anywhere] * 2 + [vmem] * 15,
        out_shape=[f32(*out.shape), f32(*in_grad.shape), f32(*egrad.shape)]
        + [square] * 8
        + [f32(hidden_part, model)] * 2
        + [f32(1, part)] * 3
        + [f32(1, NB * H // (SIDE_DP * SIDE_FSDP))],
        scratch_shapes=[
            pltpu.VMEM((2,) + out.shape, F32),
            pltpu.SemaphoreType.DMA((2, 2, out.shape[0] // ROWS)),
        ],
        compiler_params=pltpu.CompilerParams(vmem_limit_bytes=62 * 1024 * 1024),
        name="finish",
    )(dealing, raw, *shards, sums, near, small, wide, egrad, other, out, in_grad)


def body(
    tokens, encoder_states, lengths, dealing, cotangent,
    w_query, w_key, w_value, w_out, c_query, c_key, c_value, c_out, w_in, w_down,
    gain_self, gain_cross, gain_ffn, bias_table,
):
    axes = ("dp", "fsdp")
    fsdp_size = lax.axis_size("fsdp")
    dp_size = lax.axis_size("dp")
    dev_count = dp_size * fsdp_size
    dp_index = lax.axis_index("dp")
    own = dp_index * fsdp_size + lax.axis_index("fsdp")
    seq_len, model = tokens.shape[1:]
    route = [(a, a ^ 1) for a in range(dp_size)]

    x = tokens[0]
    cot = cotangent[0]
    gain_part = gain_self.shape[0]
    joined = dp_size == SIDE_DP and fsdp_size == SIDE_FSDP
    in_rows = w_in.T
    shards = [
        w_query, w_key, w_value, w_out, c_query, c_key, c_value, c_out, in_rows, w_down
    ]
    if joined:
        raw = jnp.stack(
            [gain_self, gain_cross, gain_ffn, jnp.pad(bias_table, (0, gain_part - bias_table.shape[0]))]
        )
        raw = jnp.pad(raw, ((0, 4), (0, 0)))
        done = self_forward(lengths, x, shards, None, raw, encoder_states[0])
        q, k, v, o, p, a1, wq, wk, wv, gains = done[:10]
        wo, cq, ck, cv, co = (w.reshape(model, model) for w in done[10:15])
        done = middle(
            lengths, x, o, cot, encoder_states[0], gains, wo, cq, ck, cv, co, done[15], True,
            dealing, done[16],
        )
        out, g1, egrad, mid_gain_grad = done[:4]
        wide_sums = done[9]
        done = self_backward(
            x, gains, mid_gain_grad, a1, g1, q, k, v, p, wo, wq, wk, wv,
            list(done[4:9]), egrad,
        )
        in_grad, sums, near_sums, small, egrad_other = done
        done = finish(
            dealing, raw, [w_query, w_key, w_value, c_query], sums, near_sums, small, wide_sums,
            egrad, egrad_other, out, in_grad,
        )
        return (
            tuple(d[None] for d in done[:3]) + tuple(done[3:11]) + (done[11].T, done[12])
            + tuple(d[0] for d in done[13:])
        )

    in_place = lax.dynamic_slice_in_dim(dealing, own, 1) == own
    enc_other = lax.ppermute(encoder_states[0], "dp", route)
    enc = jnp.where(in_place[:, None], encoder_states[0], enc_other)
    length = lax.dynamic_slice_in_dim(lengths, own, 1)
    column = jnp.arange(model, dtype=jnp.int32)[None, :]
    gain_rows = jnp.stack(
        [jnp.tile(g, model // gain_part) for g in (gain_self, gain_cross, gain_ffn)]
    )
    gain_rows = jnp.where(column // gain_part == own, gain_rows, jnp.zeros((), BF16))
    table_row = jnp.pad(bias_table, (0, model - bias_table.shape[0]))[None, :]
    small = jnp.pad(jnp.concatenate([gain_rows, table_row], axis=0), ((0, 4), (0, 0)))
    wq, wk, wv, wo, cq, ck, cv, co, win_t, wdown, small_all = gather_weights(
        shards + [small], axes
    )
    wide = jnp.stack([w.reshape(CHUNKS, -1, model) for w in (win_t, wdown)])
    small_all = small_all.reshape(dev_count, 8, model).astype(F32)
    gains = jnp.sum(small_all, axis=0)
    table = small_all[:, 3, : bias_table.shape[0]].reshape(NB, H)
    table = jnp.pad(table, ((0, 0), (0, LANES - H)))
    q, k, v, o, p, a1 = self_forward(length, x, None, [gains, wq, wk, wv, table])
    done = middle(length, x, o, cot, enc, gains, wo, cq, ck, cv, co, wide, False)
    out, g1, egrad, mid_gain_grad = done[:4]
    squares = list(done[4:9])
    sum_in, sum_down = reduce_grads([g.reshape(-1, model) for g in done[9]], axes)
    done = self_backward(
        x, gains, mid_gain_grad, a1, g1, q, k, v, p, wo, wq, wk, wv, None
    )
    in_grad = done[0]
    gw, small, hist = done[1:]
    g_wq, g_wk, g_wv = (
        jnp.concatenate(
            [g[:, i * LANES : (i + 1) * LANES] for g in gw], axis=1
        )
        for i in range(3)
    )
    distance = jnp.arange(LANES, dtype=jnp.int32)
    bucket_hot = bucket_of(distance)[:, None] == jnp.arange(NB, dtype=jnp.int32)[None, :]
    near_hot = bucket_hot.astype(F32) * (jnp.arange(NB) < NB - 1).astype(F32)
    by_dist = hist[:H, 1 : LANES + 1][:, ::-1]
    near_sums = jnp.dot(near_hot.T, by_dist.T, precision=lax.Precision.HIGHEST)
    grad_table = jnp.where(
        (jnp.arange(NB) < NB - 1)[:, None],
        near_sums, -jnp.sum(near_sums, axis=0, keepdims=True),
    )
    small_grads = jnp.concatenate(
        [small[i, :model].reshape(dev_count, -1) for i in range(3)]
        + [grad_table.reshape(dev_count, -1)],
        axis=1,
    )
    small_count = small_grads.shape[1]
    small_low = jnp.pad(small_grads.astype(BF16), ((0, 0), (0, model - small_count)))
    small_low = jnp.pad(small_low[:, None, :], ((0, 0), (0, 7), (0, 0))).reshape(-1, model)
    sum_cq, sum_ck, sum_cv, sum_co, sum_wo, sum_wq, sum_wk, sum_wv, sum_small = reduce_grads(
        squares + [g_wq, g_wk, g_wv, small_low], axes
    )
    ends = sum_small[0]
    end_self, end_cross, end_ffn = (
        ends[i * gain_part : (i + 1) * gain_part] for i in range(3)
    )
    end_table = ends[3 * gain_part : small_count]

    egrad_other = lax.ppermute(egrad, "dp", route)
    encoder_grad = jnp.where(in_place[:, None], egrad, egrad_other)
    return (
        out[None], in_grad[None], encoder_grad[None],
        sum_wq, sum_wk, sum_wv, sum_wo, sum_cq, sum_ck, sum_cv, sum_co, sum_in.T, sum_down,
        end_self, end_cross, end_ffn, end_table,
    )


def solution(mesh):
    rows3 = P(("dp", "fsdp"), None, None)
    rows2 = P(("dp", "fsdp"), None)
    cols2 = P(None, ("dp", "fsdp"))
    line = P(("dp", "fsdp"))
    in_specs = (
        (rows3, rows3, P(), P(), rows3) + (rows2,) * 8 + (cols2, rows2) + (line,) * 4
    )
    out_specs = (rows3,) * 3 + (rows2,) * 8 + (cols2, rows2) + (line,) * 4
    return jax.shard_map(body, mesh=mesh, in_specs=in_specs, out_specs=out_specs, check_vma=False)
```

```python
import functools
import math

import jax
import jax.numpy as jnp
from jax import lax
from jax.experimental import pallas as pl
from jax.experimental.pallas import tpu as pltpu
from jax.sharding import PartitionSpec as P

H = 12
DH = 64
NB = 32
MAXDIST = 128
EPSILON = 1e-06
MASKED = -1e30
LANES = 128
CHUNKS = 3
ROWS = 256
FORWARD_ROWS = 512
HIDDEN_ROWS = 256
BACK_ROWS = 512
CROSS_ROWS = 512
F32 = jnp.float32
BF16 = jnp.bfloat16
GELU_C = math.sqrt(2.0 / math.pi)
GELU_A = 0.044715


def bucket_of(distance):
    exact_count = NB // 2
    bucket = jnp.minimum(distance, exact_count)
    for level_idx in range(1, exact_count):
        threshold = int(
            math.ceil(exact_count * (MAXDIST / exact_count) ** (level_idx / exact_count))
        )
        bucket = bucket + (distance >= threshold).astype(jnp.int32)
    return bucket


def nn(left_op, right_op):
    return lax.dot_general(
        left_op, right_op, (((1,), (0,)), ((), ())), preferred_element_type=F32
    )


def nt(left_op, right_op):
    return lax.dot_general(
        left_op, right_op, (((1,), (1,)), ((), ())), preferred_element_type=F32
    )


def tn(left_op, right_op):
    return lax.dot_general(
        left_op, right_op, (((0,), (0,)), ((), ())), preferred_element_type=F32
    )


def unit_rows(values_in):
    inv_rms = lax.rsqrt(jnp.mean(values_in * values_in, axis=-1, keepdims=True) + EPSILON)
    return values_in * inv_rms, inv_rms


def norm_back(grad_in, unit, inv_rms, gain_vec):
    scaled = grad_in * gain_vec
    through = inv_rms * (scaled - unit * jnp.mean(scaled * unit, axis=-1, keepdims=True))
    return through, jnp.sum(grad_in * unit, axis=0, keepdims=True)


def head_lane(shape, which):
    lane = lax.broadcasted_iota(jnp.int32, shape, len(shape) - 1)
    return (lane // DH) == which


SIDE_DP = 4
SIDE_FSDP = 8
MESH = pl.DeviceIdType.MESH


def coords():
    along = lax.axis_index("fsdp")
    return lax.axis_index("dp"), along // 4, lax.rem(along // 2, 2), lax.rem(along, 2)


def device(z, y, x, c):
    return (z, y * 4 + x * 2 + c)


def greet_peers():
    z, y, x, c = coords()
    peers = [device(lax.rem(z + k, SIDE_DP), y, x, c) for k in range(1, SIDE_DP)]
    peers += [device(z, y, 1 - x, c), device(z, 1 - y, x, c), device(z, y, x, 1 - c)]
    barrier = pltpu.get_barrier_semaphore()
    for peer in peers:
        pl.semaphore_signal(barrier, inc=1, device_id=peer, device_id_type=MESH)
    pl.semaphore_wait(barrier, len(peers))


def own_index():
    return lax.axis_index("dp") * SIDE_FSDP + lax.axis_index("fsdp")


class Link:
    def __init__(self, send, recv):
        self.send, self.recv, self.used, self.pieces = send, recv, 0, []

    def take(self, piece):
        self.pieces.append(piece)
        self.used += piece.SEMS
        return self.used - piece.SEMS

    def drain(self):
        for piece in self.pieces:
            piece.drain()


class Place:
    def __init__(self):
        z, y, x, c = self.at = coords()
        self.to_y = device(z, 1 - y, x, c)
        self.to_x = device(z, y, 1 - x, c)
        self.to_core = device(z, y, x, 1 - c)
        self.other_z = [lax.rem(z + k, SIDE_DP) for k in range(1, SIDE_DP)]
        self.to_z = [device(other, y, x, c) for other in self.other_z]
        self.ny, self.nx, self.nc = 1 - y, 1 - x, 1 - c


class Piece:
    def __init__(self, link, local, place=None, first=None):
        self.link, self.local = link, local
        self.first = link.take(self) if first is None else first
        self.half_a, self.half_b = slice(0, SIDE_DP // 2), slice(SIDE_DP // 2, SIDE_DP)
        place = place or Place()
        self.at, self.to_y, self.to_x, self.to_core = (
            place.at, place.to_y, place.to_x, place.to_core
        )
        self.other_z, self.to_z = place.other_z, place.to_z
        self.ny, self.nx, self.nc = place.ny, place.nx, place.nc

    def copy(self, slot, src, dst, peer):
        return pltpu.make_async_remote_copy(
            src_ref=src, dst_ref=dst, send_sem=self.link.send.at[self.first + slot],
            recv_sem=self.link.recv.at[self.first + slot], device_id=peer, device_id_type=MESH,
        )

    def start(self, k):
        for copy in self.moves(k):
            copy.start()

    def arrive(self, k):
        for copy in self.moves(k):
            copy.wait_recv()

    def sent(self, k):
        for copy in self.moves(k):
            copy.wait_send()

    def drain(self):
        for k in self.UNSENT:
            self.sent(k)

    def stage(self, k):
        (self.s0, self.s1, self.s2, self.s3, self.s4)[k]()


class Gather(Piece):
    SEMS = 13
    UNSENT = (0, 1, 2, 3, 4, 5)

    def __init__(self, src, out, link, local, place=None, first=None):
        super().__init__(link, local, place, first)
        self.src, self.out = src, out

    def moves(self, k):
        z, y, x, c = self.at
        out, a, b = self.out, self.half_a, self.half_b
        if k == 0:
            here = out.at[z, y, x, c]
            return [self.copy(i, self.src, here, peer) for i, peer in enumerate(self.to_z)]
        same = lambda slot, ref, peer: self.copy(slot, ref, ref, peer)
        if k == 1:
            return [
                same(3, out.at[a, y, x, c], self.to_x),
                same(4, out.at[b, y, x, c], self.to_y),
            ]
        if k == 2:
            return [
                same(5, out.at[a, y, :, c], self.to_y),
                same(6, out.at[b, :, x, c], self.to_x),
            ]
        if k == 3:
            return [same(7, out.at[:, y, x, c], self.to_core)]
        if k == 4:
            return [
                same(8, out.at[a, y, self.nx, c], self.to_core),
                same(9, out.at[b, self.ny, x, c], self.to_core),
            ]
        return [
            same(10, out.at[a, self.ny, :, c], self.to_core),
            same(11, out.at[b, :, self.nx, c], self.to_core),
        ]

    def keep(self):
        return pltpu.make_async_copy(self.src, self.out.at[self.at], self.local)

    def s0(self):
        self.start(0)
        self.keep().start()

    def s1(self):
        self.keep().wait()
        self.arrive(0)
        self.start(1)
        self.start(3)

    def s2(self):
        self.arrive(1)
        self.start(2)
        self.start(4)

    def s3(self):
        self.arrive(2)
        self.start(5)

    def s4(self):
        for k in (3, 4, 5):
            self.arrive(k)


class Reduce(Piece):
    SEMS = 8
    BUFFERS = 6

    def __init__(
        self, src, out, own, held, l1a, l1b, l2a, l2b, l3, link, local, place=None, first=None,
        early=False,
    ):
        super().__init__(link, local, place, first)
        self.src, self.out, self.own, self.held = src, out, own, held
        self.l1a, self.l1b, self.l2a, self.l2b, self.l3 = l1a, l1b, l2a, l2b, l3
        self.UNSENT = (1, 2, 3) if early else (0, 1, 2, 3)

    @staticmethod
    def scratch(rows, width):
        buffer = lambda *lead: pltpu.VMEM(lead + (rows, width), BF16)
        half = SIDE_DP // 2
        return [
            buffer(SIDE_DP, 2, 2), buffer(half, 2), buffer(half, 2), buffer(half), buffer(half),
            buffer(SIDE_DP - 1),
        ]

    def moves(self, k):
        z, y, x, c = self.at
        held, a, b = self.held, self.half_a, self.half_b
        if k == 0:
            return [self.copy(0, self.src.at[:, :, :, self.nc], held, self.to_core)]
        if k == 1:
            return [
                self.copy(1, held.at[a, self.ny], self.l1a, self.to_y),
                self.copy(2, held.at[b, :, self.nx], self.l1b, self.to_x),
            ]
        if k == 2:
            return [
                self.copy(3, held.at[a, y, self.nx], self.l2a, self.to_x),
                self.copy(4, held.at[b, self.ny, x], self.l2b, self.to_y),
            ]
        return [
            self.copy(5 + i, held.at[other, y, x], self.l3.at[i], peer)
            for i, (other, peer) in enumerate(zip(self.other_z, self.to_z))
        ]

    def keep(self):
        return pltpu.make_async_copy(self.src.at[:, :, :, self.at[3]], self.own, self.local)

    def s0(self):
        self.start(0)
        if self.own is not None:
            self.keep().start()

    def s1(self):
        held = self.held
        if self.own is not None:
            self.keep().wait()
            self.arrive(0)
            held[...] = held[...] + self.own[...]
        else:
            self.arrive(0)
            held[...] = held[...] + self.src[:, :, :, self.at[3]]
        self.start(1)

    def s2(self):
        z, y, x, c = self.at
        self.arrive(1)
        held, a, b = self.held, self.half_a, self.half_b
        held[a, y] = held[a, y] + self.l1a[...]
        held[b, :, x] = held[b, :, x] + self.l1b[...]
        self.start(2)

    def s3(self):
        z, y, x, c = self.at
        self.arrive(2)
        held, a, b = self.held, self.half_a, self.half_b
        held[a, y, x] = held[a, y, x] + self.l2a[...]
        held[b, y, x] = held[b, y, x] + self.l2b[...]
        self.start(3)

    def s4(self):
        z, y, x, c = self.at
        self.arrive(3)
        total = self.held[z, y, x].astype(F32)
        for k in range(SIDE_DP - 1):
            total = total + self.l3[k].astype(F32)
        self.out[...] = total


class Swap(Piece):
    SEMS = 1
    UNSENT = (0,)

    def __init__(self, src, out, link, place):
        super().__init__(link, None, place)
        z, y, x, c = self.at
        self.src, self.out = src, out
        self.peer = device(z + 1 - 2 * lax.rem(z, 2), y, x, c)

    def moves(self, k):
        return [self.copy(0, self.src, self.out, self.peer)]


class SumSmall(Piece):
    SEMS = 6
    UNSENT = ()

    def __init__(self, total, near, far, link):
        super().__init__(link, None)
        self.total, self.near, self.far = total, near, far

    def moves(self, k):
        if k < 3:
            peer = (self.to_core, self.to_y, self.to_x)[k]
            return [self.copy(k, self.total, self.near.at[k], peer)]
        return [
            self.copy(3 + i, self.total, self.far.at[i], peer) for i, peer in enumerate(self.to_z)
        ]

    def add(self, k):
        self.arrive(k)
        self.sent(k)
        if k < 3:
            self.total[...] = self.total[...] + self.near[k]
        else:
            total = self.total[...]
            for i in range(SIDE_DP - 1):
                total = total + self.far[i]
            self.total[...] = total

    def s0(self):
        self.start(0)

    def s1(self):
        self.add(0)
        self.start(1)

    def s2(self):
        self.add(1)
        self.start(2)

    def s3(self):
        self.add(2)
        self.start(3)

    def s4(self):
        self.add(3)


FORWARD_SQUARES = 5


def bias_tables(table):
    lane = lax.broadcasted_iota(jnp.int32, (NB, 4 * LANES), 1)
    bucket = bucket_of(jnp.maximum(LANES - lane, 0))
    bucket = jnp.where(lane <= LANES, bucket, NB - 1)
    row = lax.broadcasted_iota(jnp.int32, (NB, 4 * LANES), 0)
    last = jnp.where(row == NB - 1, 1.0, 0.0)
    hot = jnp.where(row == bucket, 1.0, 0.0) - last
    near = tn(table.astype(BF16), hot.astype(BF16))
    far = tn(table.astype(BF16), last[:, :LANES].astype(BF16))
    return near[:16], far[:16]


def self_forward_kernel(joined, length_ref, x_ref, *refs):
    step = pl.program_id(0)
    last = pl.num_programs(0) - 1
    length = length_ref[own_index() if joined else 0]
    if joined:
        (raw_ref, enc_hbm), shards, refs = refs[:2], refs[2:12], refs[12:]
    else:
        (gain_in, wq_ref, wk_ref, wv_ref, table_in), refs = refs[:5], refs[5:]
    (q_ref, k_ref, v_ref, o_ref, p_ref, a_ref), refs = refs[:6], refs[6:]
    if joined:
        (wq_ref, wk_ref, wv_ref, gain_ref), refs = refs[:4], refs[4:]
        squares, (wide_ref, enc_other) = (
            refs[:FORWARD_SQUARES], refs[FORWARD_SQUARES : FORWARD_SQUARES + 2]
        )
        tile_ref, near_ref, far_ref, got_ref, small_src, got_small, send, recv, local = refs[
            FORWARD_SQUARES + 2 :
        ]
        link, place = Link(send, recv), Place()
        first = [Gather(shards[i], got_ref.at[i], link, local.at[i], place) for i in range(3)]
        first.append(Gather(small_src, got_small, link, local.at[3], place))
        swap = Swap(enc_hbm, enc_other, link, place)
        second = [
            Gather(shards[3 + i], squares[i], link, local.at[4 + i], place)
            for i in range(FORWARD_SQUARES)
        ]
        part = wide_ref.shape[-2]
        third = [
            Gather(
                shards[8 + m].at[k * part : (k + 1) * part], wide_ref.at[k, m], link,
                local.at[9 + 2 * k + m], place,
            )
            for k in range(CHUNKS)
            for m in range(2)
        ]
    else:
        tile_ref, near_ref, far_ref = refs
    seq, model = x_ref.shape
    width = q_ref.shape[1]

    def normed():
        return unit_rows(x_ref[...].astype(F32))[0]

    def set_tables(table):
        near, far = bias_tables(table)
        near_ref[...] = near
        far_ref[...] = far

    @pl.when(step == 0)
    def _():
        if not joined:
            a_ref[...] = (normed() * gain_in[0:1, :]).astype(BF16)
            set_tables(table_in[...])
            return
        rows_in, model_cols = raw_ref.shape[1], model
        entry = lax.broadcasted_iota(jnp.int32, (rows_in, model_cols), 0)
        column = lax.broadcasted_iota(jnp.int32, (rows_in, model_cols), 1)
        spread = lambda at: nn(raw_ref[...], jnp.where(column == entry + at, 1.0, 0.0).astype(BF16))
        is_table = lax.broadcasted_iota(jnp.int32, (8, model_cols), 0) == 3
        small_src[...] = jnp.where(
            is_table, spread(0), spread(own_index() * rows_in)
        ).astype(BF16)
        greet_peers()
        for piece in first:
            piece.stage(0)
        swap.start(0)
        unit = normed()
        for piece in first:
            piece.stage(1)
        for piece in second:
            piece.stage(0)
        for piece in first:
            piece.stage(2)
        first[3].stage(3)
        first[3].stage(4)
        small = got_small[...].astype(F32).reshape(NB, 8, model)
        gains = jnp.sum(small, axis=0)
        gain_ref[...] = gains
        which = lax.broadcasted_iota(jnp.int32, (NB, 8, LANES), 1)
        set_tables(jnp.sum(jnp.where(which == 3, small[:, :, :LANES], 0.0), axis=1))
        a_ref[...] = (unit * gains[0:1, :]).astype(BF16)
        for piece in first[:3]:
            piece.stage(3)
        for i, full_ref in enumerate((wq_ref, wk_ref, wv_ref)):
            first[i].stage(4)
            full_ref[...] = got_ref[i].astype(F32).reshape(model, model).astype(BF16)
        for piece in second:
            piece.stage(1)
        for piece in third[:2]:
            piece.stage(0)

    if joined:

        @pl.when(step == 1)
        def _():
            for piece in second:
                piece.stage(2)
            for piece in third[2:4]:
                piece.stage(0)

        @pl.when(step == 2)
        def _():
            for piece in third[:2]:
                piece.stage(1)
            for piece in third[4:]:
                piece.stage(0)

    for w_ref, out_ref in ((wq_ref, q_ref), (wk_ref, k_ref), (wv_ref, v_ref)):
        if joined:
            weights = w_ref[:, pl.ds(pl.multiple_of(step * width, LANES), width)]
        else:
            weights = w_ref[...]
        out_ref[...] = nn(a_ref[...], weights).astype(BF16)

    key_pos = lax.broadcasted_iota(jnp.int32, (seq, 1), 0)
    key_dead = key_pos >= length
    row = lax.broadcasted_iota(jnp.int32, (ROWS, ROWS + LANES), 0)
    col = lax.broadcasted_iota(jnp.int32, (ROWS, ROWS + LANES), 1)
    ahead = col - LANES > row
    for pair in range(width // LANES):
        cols = slice(pair * LANES, (pair + 1) * LANES)
        outs = [None] * (seq // ROWS)
        for which in range(2):
            local = pair * 2 + which
            head = step * (width // DH) + local
            spun = pltpu.roll(
                jnp.broadcast_to(near_ref[pl.ds(head, 1), :], (ROWS, 4 * LANES)),
                0, 1, stride=1, stride_axis=0,
            )
            tile_ref[...] = jnp.where(ahead, MASKED, spun[:, : ROWS + LANES])
            own = head_lane((seq, LANES), which)
            extra = lax.broadcasted_iota(jnp.int32, (seq, LANES), 1) == (DH if which == 0 else 0)
            far = jnp.where(key_dead, MASKED, far_ref[pl.ds(head, 1), 0:1]).astype(BF16)
            keys = jnp.where(own, k_ref[:, cols], jnp.where(extra, far, jnp.zeros((), BF16)))
            values = jnp.where(own, v_ref[:, cols], jnp.zeros((), BF16))
            queries = jnp.where(own, q_ref[:, cols], jnp.where(extra, 1.0, 0.0).astype(BF16))
            for blk in range(seq // ROWS):
                rows = slice(blk * ROWS, (blk + 1) * ROWS)
                span = (blk + 1) * ROWS
                cut = max(span - ROWS - LANES, 0)
                scores = nt(queries[rows], keys[:span])
                if cut:
                    near = scores[:, cut:] + tile_ref[...]
                    scores = jnp.concatenate([scores[:, :cut], near], axis=1)
                elif span == ROWS:
                    scores = scores + tile_ref[:, LANES:]
                else:
                    near = scores[:, ROWS - LANES :] + tile_ref[...]
                    scores = jnp.concatenate([scores[:, : ROWS - LANES], near], axis=1)
                top = jnp.max(scores, axis=1, keepdims=True)
                weights = jnp.exp(scores - top)
                total = jnp.sum(weights, axis=1, keepdims=True)
                probs = (weights * (1.0 / total)).astype(BF16)
                p_ref[local, rows, :span] = probs
                mixed = nn(probs, values[:span])
                outs[blk] = mixed if outs[blk] is None else outs[blk] + mixed
        for blk in range(seq // ROWS):
            o_ref[blk * ROWS : (blk + 1) * ROWS, cols] = outs[blk].astype(BF16)

    if joined:

        @pl.when(step == last)
        def _():
            for stage in (3, 4):
                for piece in second:
                    piece.stage(stage)
            for piece in third[:2]:
                piece.arrive(1)
                piece.arrive(3)
            for piece in third[2:]:
                piece.keep().wait()
                piece.arrive(0)
            swap.arrive(0)
            for piece in first + second + [swap]:
                piece.drain()
            for i, piece in enumerate(third):
                for k in (0, 1, 3) if i < 2 else (0,):
                    piece.sent(k)


def self_forward(length, x, shards, full, raw=None, enc=None):
    seq, model = x.shape
    width = 256
    heads = width // DH
    steps = model // width
    joined = full is None
    whole = lambda shape: pl.BlockSpec(shape, lambda i: (0,) * len(shape))
    held = lambda shape: pl.BlockSpec(
        shape, lambda i: (0,) * len(shape), pipeline_mode=pl.Buffered(1)
    )
    anywhere = pl.BlockSpec(memory_space=pl.ANY)
    smem = pl.BlockSpec(memory_space=pltpu.SMEM)
    columns = pl.BlockSpec((seq, width), lambda i: (0, i))
    weight = pl.BlockSpec((model, width), lambda i: (0, i))
    in_specs = [smem, held((seq, model))]
    out_specs = [
        columns, columns, columns, columns,
        pl.BlockSpec((heads, seq, seq), lambda i: (i, 0, 0)), whole((seq, model)),
    ]
    out_shape = [jax.ShapeDtypeStruct((seq, model), BF16)] * 4 + [
        jax.ShapeDtypeStruct((H, seq, seq), BF16), jax.ShapeDtypeStruct((seq, model), BF16),
    ]
    scratch = [
        pltpu.VMEM((ROWS, ROWS + LANES), F32), pltpu.VMEM((16, 4 * LANES), F32),
        pltpu.VMEM((16, LANES), F32),
    ]
    params = dict(vmem_limit_bytes=62 * 1024 * 1024)
    if joined:
        lead = (SIDE_DP, 2, 2, 2)
        part = shards[0].shape[0]
        wide = (CHUNKS, 2) + lead + (shards[8].shape[0] // CHUNKS, model)
        ins = [raw, enc] + list(shards)
        in_specs += [whole(raw.shape)] + [anywhere] * (len(ins) - 1)
        square = jax.ShapeDtypeStruct((model, model), BF16)
        out_shape += [square] * 3 + [jax.ShapeDtypeStruct((8, model), F32)]
        out_specs += [whole((model, model))] * 3 + [whole((8, model))]
        out_shape += [jax.ShapeDtypeStruct(lead + (part, model), BF16)] * FORWARD_SQUARES
        out_shape += [jax.ShapeDtypeStruct(wide, BF16), jax.ShapeDtypeStruct(enc.shape, BF16)]
        out_specs += [anywhere] * (FORWARD_SQUARES + 2)
        count = 4 + FORWARD_SQUARES + 2 * CHUNKS
        scratch += [
            pltpu.VMEM((3,) + lead + (part, model), BF16), pltpu.VMEM((8, model), BF16),
            pltpu.VMEM(lead + (8, model), BF16),
            pltpu.SemaphoreType.DMA((count * Gather.SEMS + 1,)),
            pltpu.SemaphoreType.DMA((count * Gather.SEMS + 1,)),
            pltpu.SemaphoreType.DMA((count,)),
        ]
        params.update(collective_id=1, has_side_effects=True)
    else:
        ins = list(full)
        in_specs += [whole((8, model)), weight, weight, weight, whole((NB, LANES))]
    return pl.pallas_call(
        functools.partial(self_forward_kernel, joined),
        grid=(steps,),
        in_specs=in_specs,
        out_specs=out_specs,
        out_shape=out_shape,
        scratch_shapes=scratch,
        compiler_params=pltpu.CompilerParams(**params),
        cost_estimate=pl.CostEstimate(
            flops=6 * seq * model * model + 4 * seq * seq * model,
            bytes_accessed=2 * H * seq * seq + 16 * seq * model,
            transcendentals=H * seq * seq,
        ),
        name="self_forward",
    )(length, x, *ins)


def middle_kernel(joined, length_ref, gain_ref, *refs):
    if joined:
        (dealing_ref, other_hbm), refs = refs[:2], refs[2:]
    length = length_ref[own_index() if joined else 0]
    (x_hbm, o_hbm, cot_hbm, enc_hbm, wo_hbm, cq_hbm, ck_hbm, cv_hbm, co_hbm), refs = (
        refs[:9], refs[9:]
    )
    wide_hbm, refs = refs[0], refs[1:]
    (out_hbm, g1_hbm, egrad_ref, gain_grad_ref), refs = refs[:4], refs[4:]
    squares, refs = refs[:5], refs[5:]
    sum_ref, refs = refs[0], refs[1:]
    if joined:
        wide_hbm, refs = refs[0], refs[1:]
    (
        o_ref, g_ref, a2_ref, cq_scr, mix_ref, a3_ref, r_ref, du_ref, prob_ref,
        x1_ref, x2_ref, acc_ref, dy_ref, enc_ref, keys_ref, values_ref, dk_acc, dv_acc,
        wo_ref, cq_ref, ck_ref, cv_ref, co_ref, wide_ref, src_ref, load_sem, wide_sem, out_sem,
    ), refs = refs[:28], refs[28:]
    seq, model = o_ref.shape
    xr_ref = du_ref.at[:, :model]
    blocks = seq // ROWS
    pairs = model // LANES
    zero = jnp.zeros((), BF16)
    gain_cross = gain_ref[1:2, :]
    gain_ffn = gain_ref[2:3, :]

    loads = [
        pltpu.make_async_copy(src, dst, load_sem.at[i])
        for i, (src, dst) in enumerate(
            (
                (enc_hbm, enc_ref), (ck_hbm, ck_ref), (cv_hbm, cv_ref), (o_hbm, o_ref),
                (wo_hbm, wo_ref), (x_hbm, xr_ref), (cq_hbm, cq_ref), (cot_hbm, g_ref),
                (co_hbm, co_ref),
            )
            + (((other_hbm, keys_ref),) if joined else ())
        )
    ]
    for copy in loads:
        copy.start()

    chunk_rows = wide_ref.shape[2]

    def wide_loads(k):
        slot = lax.rem(k, 2)
        found = []
        for m in range(2):
            dst = wide_ref.at[slot, m]
            if joined:
                src = wide_hbm.at[k, m].reshape(chunk_rows, model)
            else:
                src = wide_hbm.at[m, k]
            found.append(pltpu.make_async_copy(src, dst, wide_sem.at[slot, m]))
        return found

    if joined:
        held, l1a, l1b, l2a, l2b, l3, rsend, rrecv, gsend, grecv = refs
        gather_link = Link(gsend, grecv)
        reduce_link = Link(rsend, rrecv)
        place = Place()
        part = chunk_rows // (SIDE_DP * SIDE_FSDP)

        def incoming(k):
            return [
                Gather(
                    None, wide_hbm.at[k, m], gather_link, None, place,
                    (2 * k + m) * Gather.SEMS,
                )
                for m in range(2)
            ]

        def leaving(k):
            at = pl.multiple_of(k * part, 8)
            found = []
            for m in range(2):
                i = 2 * k + m
                found.append(
                    Reduce(
                        src_ref.at[m], sum_ref.at[m, pl.ds(at, part)], None, held.at[i],
                        l1a.at[i], l1b.at[i], l2a.at[i], l2b.at[i], l3.at[i], reduce_link, None,
                        place, i * Reduce.SEMS,
                    )
                )
            return found

    def arriving(k, wait=(), start=(), when=None):
        if not joined:
            return

        def go():
            for piece in incoming(k):
                for round_idx in wait:
                    piece.arrive(round_idx)
            for piece in incoming(k):
                for round_idx in start:
                    piece.start(round_idx)

        go() if when is None else pl.when(when)(go)

    def reduce_stage(k, stage, when=None):
        if not joined:
            return

        def go():
            for piece in leaving(k):
                piece.stage(stage)

        go() if when is None else pl.when(when)(go)

    if joined:
        greet_peers()
        arriving(0, start=(2, 4))
        arriving(1, start=(1, 3))
    else:
        for copy in wide_loads(0):
            copy.start()

    for copy in loads[:3] + loads[9:]:
        copy.wait()
    if joined:
        mine = own_index()
        enc_ref[...] = jnp.where(dealing_ref[mine] == mine, enc_ref[...], keys_ref[...])
    keys_ref[...] = nn(enc_ref[...], ck_ref[...]).astype(BF16)
    values_ref[...] = nn(enc_ref[...], cv_ref[...]).astype(BF16)
    gain_grad_ref[...] = jnp.zeros_like(gain_grad_ref)
    for copy in loads[3:9]:
        copy.wait()

    def forward_rows(i, _):
        rows = pl.ds(pl.multiple_of(i * FORWARD_ROWS, FORWARD_ROWS), FORWARD_ROWS)
        pos = i * FORWARD_ROWS + lax.broadcasted_iota(jnp.int32, (FORWARD_ROWS, 1), 0)
        valid = jnp.where(pos < length, 1.0, 0.0).astype(F32)
        x1 = xr_ref[rows, :].astype(F32) + nn(o_ref[rows, :], wo_ref[...])
        x1_ref[rows, :] = x1
        unit2, _inv2 = unit_rows(x1)
        a2 = (unit2 * gain_cross).astype(BF16)
        a2_ref[rows, :] = a2
        cq = nn(a2, cq_ref[...]).astype(BF16)
        cq_scr[rows, :] = cq
        mixed = []
        for pair in range(pairs):
            cols = slice(pair * LANES, (pair + 1) * LANES)
            total_out = None
            for which in range(2):
                own = head_lane((FORWARD_ROWS, LANES), which)
                own_key = head_lane((keys_ref.shape[0], LANES), which)
                scores = nt(jnp.where(own, cq[:, cols], zero), keys_ref[:, cols])
                top = jnp.max(scores, axis=1, keepdims=True)
                weights = jnp.exp(scores - top)
                prob = (weights * (1.0 / jnp.sum(weights, axis=1, keepdims=True))).astype(BF16)
                at = (2 * pair + which) * keys_ref.shape[0]
                prob_ref[rows, at : at + keys_ref.shape[0]] = prob
                piece = nn(prob, jnp.where(own_key, values_ref[:, cols], zero))
                total_out = piece if total_out is None else total_out + piece
            mixed.append(total_out.astype(BF16))
        mix = jnp.concatenate(mixed, axis=1)
        mix_ref[rows, :] = mix
        x2 = x1 + nn(mix, co_ref[...])
        x2_ref[rows, :] = x2
        acc_ref[rows, :] = x2
        unit3, _inv3 = unit_rows(x2)
        a3_ref[rows, :] = (unit3 * gain_ffn).astype(BF16)
        g_ref[rows, :] = (g_ref[rows, :].astype(F32) * valid).astype(BF16)
        return 0

    lax.fori_loop(0, seq // FORWARD_ROWS, forward_rows, 0)

    def chunk(k, _):
        slot = lax.rem(k, 2)
        for copy in wide_loads(k):
            copy.wait()
        for i in range(seq // HIDDEN_ROWS):
            rows = slice(i * HIDDEN_ROWS, (i + 1) * HIDDEN_ROWS)
            z = nt(a3_ref[rows, :], wide_ref[slot, 0])
            zz = z * z
            t = jnp.tanh(GELU_C * z * (1.0 + GELU_A * zz))
            half = 0.5 + 0.5 * t
            r = (z * half).astype(BF16)
            r_ref[rows, :] = r
            slope = half + (0.5 * GELU_C) * z * (1.0 - t * t) * (1.0 + (3.0 * GELU_A) * zz)
            du = (nt(g_ref[rows, :], wide_ref[slot, 1]) * slope).astype(BF16)
            du_ref[rows, :] = du
            acc_ref[rows, :] += nn(r, wide_ref[slot, 1])
            dy_ref[rows, :] += nn(du, wide_ref[slot, 0])
            if i == seq // HIDDEN_ROWS // 2 - 1:
                arriving(2, wait=(2,), start=(5,), when=k == 1)
                reduce_stage(k - 1, 1, k >= 1)
        arriving(1, wait=(2,), start=(5,), when=k == 0)
        arriving(2, wait=(1,), start=(2, 4), when=k == 0)
        reduce_stage(k - 2, 3, k >= 2)

        @pl.when(k >= 1)
        def _():
            if joined:
                for piece in leaving(k - 1):
                    piece.sent(0)
            else:
                for copy in grad_copies(k - 1):
                    copy.wait()

        def next_loads():
            for copy in wide_loads(k + 1):
                copy.start()

        if not joined:
            pl.when(k + 1 < CHUNKS)(next_loads)
        shape = src_ref.shape[1:]
        src_ref[0] = tn(du_ref[...], a3_ref[...]).reshape(shape).astype(BF16)
        src_ref[1] = tn(r_ref[...], g_ref[...]).reshape(shape).astype(BF16)
        if joined:
            reduce_stage(k, 0)
            arriving(k + 1, wait=(3, 4, 5), when=k + 1 < CHUNKS)
            pl.when(k + 1 < CHUNKS)(next_loads)
            reduce_stage(k - 1, 2, k >= 1)
        else:
            for copy in grad_copies(k):
                copy.start()
        return 0

    def grad_copies(k):
        return [
            pltpu.make_async_copy(src_ref.at[m], sum_ref.at[m, k], out_sem.at[m])
            for m in range(2)
        ]

    dy_ref[...] = jnp.zeros_like(dy_ref)
    if joined:
        arriving(0, wait=(2,), start=(5,))
        arriving(1, wait=(1,), start=(2, 4))
        arriving(2, start=(1, 3))
        arriving(0, wait=(4, 5))
        for copy in wide_loads(0):
            copy.start()
    lax.fori_loop(0, CHUNKS, chunk, 0)

    g1_low_ref = a3_ref
    g2_low_ref = g_ref
    dcq_ref = cq_scr
    final = CHUNKS - 1

    dmix_ref = du_ref.at[:, :model]

    def out_copies(rows):
        return [
            pltpu.make_async_copy(acc_ref.at[rows, :], out_hbm.at[rows, :], out_sem.at[0]),
            pltpu.make_async_copy(dy_ref.at[rows, :], g1_hbm.at[rows, :], out_sem.at[1]),
        ]

    everything = pl.ds(0, seq)
    if not joined:
        for copy in grad_copies(final):
            copy.wait()
    for i in range(seq // BACK_ROWS):
        rows = slice(i * BACK_ROWS, (i + 1) * BACK_ROWS)
        pos = i * BACK_ROWS + lax.broadcasted_iota(jnp.int32, (BACK_ROWS, 1), 0)
        valid = jnp.where(pos < length, 1.0, 0.0).astype(F32)
        acc_ref[rows, :] = acc_ref[rows, :] * valid
        unit3, inv3 = unit_rows(x2_ref[rows, :])
        through, gain_part = norm_back(dy_ref[rows, :], unit3, inv3, gain_ffn)
        gain_grad_ref[1:2, :] += gain_part
        g2 = g_ref[rows, :].astype(F32) + through
        dy_ref[rows, :] = g2
        g2_low = g2.astype(BF16)
        g2_low_ref[rows, :] = g2_low
        dmix_ref[rows, :] = nt(g2_low, co_ref[...]).astype(BF16)
    out_copies(everything)[0].start()
    reduce_stage(2, 1)
    reduce_stage(1, 3)
    reduce_stage(0, 4)
    def backward_pair(pair, _):
        cols = pl.ds(pl.multiple_of(pair * LANES, LANES), LANES)
        dk = dv = None
        for i in range(seq // CROSS_ROWS):
            rows = slice(i * CROSS_ROWS, (i + 1) * CROSS_ROWS)
            dq = None
            for which in range(2):
                own = head_lane((CROSS_ROWS, LANES), which)
                own_key = head_lane((keys_ref.shape[0], LANES), which)
                at = pl.multiple_of((2 * pair + which) * keys_ref.shape[0], LANES)
                prob_low = prob_ref[rows, pl.ds(at, keys_ref.shape[0])]
                prob = prob_low.astype(F32)
                d_out = jnp.where(own, dmix_ref[rows, cols], zero)
                dp = nt(d_out, values_ref[:, cols])
                ds = prob * (dp - jnp.sum(prob * dp, axis=1, keepdims=True))
                ds_low = ds.astype(BF16)
                dv_part = tn(prob_low, d_out)
                dk_part = tn(ds_low, jnp.where(own, cq_scr[rows, cols], zero))
                piece = nn(ds_low, jnp.where(own_key, keys_ref[:, cols], zero))
                dq = piece if dq is None else dq + piece
                dk = dk_part if dk is None else dk + dk_part
                dv = dv_part if dv is None else dv + dv_part
            dcq_ref[rows, cols] = dq.astype(BF16)
        dk_acc[:, cols] = dk
        dv_acc[:, cols] = dv
        return 0

    lax.fori_loop(0, pairs, backward_pair, 0)
    reduce_stage(2, 2)
    for i in range(seq // BACK_ROWS):
        rows = slice(i * BACK_ROWS, (i + 1) * BACK_ROWS)
        unit2, inv2 = unit_rows(x1_ref[rows, :])
        through, gain_part = norm_back(
            nt(dcq_ref[rows, :], cq_ref[...]), unit2, inv2, gain_cross
        )
        gain_grad_ref[0:1, :] += gain_part
        g1 = dy_ref[rows, :] + through
        dy_ref[rows, :] = g1
        g1_low_ref[rows, :] = g1.astype(BF16)
    out_copies(everything)[1].start()

    reduce_stage(1, 4)
    dk = dk_acc[...].astype(BF16)
    dv = dv_acc[...].astype(BF16)
    egrad_ref[...] = nt(dk, ck_ref[...]) + nt(dv, cv_ref[...])
    made = (
        (cq_ref, lambda: tn(a2_ref[...], dcq_ref[...])),
        (ck_ref, lambda: tn(enc_ref[...], dk)),
        (cv_ref, lambda: tn(enc_ref[...], dv)),
        (co_ref, lambda: tn(mix_ref[...], g2_low_ref[...])),
        (wo_ref, lambda: tn(o_ref[...], g1_low_ref[...])),
    )
    writes = []
    for i, (buffer, make) in enumerate(made):
        buffer[...] = make().astype(BF16)
        if i == 2:
            reduce_stage(final, 3)
        writes.append(pltpu.make_async_copy(buffer, squares[i], load_sem.at[i]))
        writes[-1].start()
    reduce_stage(final, 4)
    for copy in writes:
        copy.wait()
    for copy in out_copies(everything):
        copy.wait()
    if joined:
        for k, rounds in enumerate(((2, 4, 5), (1, 2, 3, 4, 5), (1, 2, 3, 4, 5))):
            for piece in incoming(k):
                for round_idx in rounds:
                    piece.sent(round_idx)
        for k in range(CHUNKS):
            for piece in leaving(k):
                for round_idx in (0, 1, 2, 3) if k == final else (1, 2, 3):
                    piece.sent(round_idx)


def middle(
    length, x, o, cot, enc, gains, wo, cq, ck, cv, co, wide, joined, dealing=None, other=None
):
    seq, model = x.shape
    enc_len = enc.shape[0]
    anywhere = pl.BlockSpec(memory_space=pl.ANY)
    vmem = pl.BlockSpec(memory_space=pltpu.VMEM)
    smem = pl.BlockSpec(memory_space=pltpu.SMEM)
    low = lambda *shape: pltpu.VMEM(shape, BF16)
    full = lambda *shape: pltpu.VMEM(shape, F32)
    ins = [x, o, cot, enc, wo, cq, ck, cv, co, wide]
    square = jax.ShapeDtypeStruct((model, model), BF16)
    out_shape = [
        jax.ShapeDtypeStruct((seq, model), F32),
        jax.ShapeDtypeStruct((seq, model), F32),
        jax.ShapeDtypeStruct((enc_len, model), F32),
        jax.ShapeDtypeStruct((2, model), F32),
    ] + [square] * 5
    out_specs = [anywhere, anywhere, vmem, vmem] + [anywhere] * 5
    hidden = 4 * model
    chunk_rows = hidden // CHUNKS
    rows_low = [low(seq, model)] * 6 + [low(seq, chunk_rows)] * 2
    params = dict(vmem_limit_bytes=63 * 1024 * 1024)
    if joined:
        part = chunk_rows // (SIDE_DP * SIDE_FSDP)
        lead = (SIDE_DP, 2, 2, 2)
        out_shape += [
            jax.ShapeDtypeStruct((2, CHUNKS * part, model), F32),
            jax.ShapeDtypeStruct(wide.shape, BF16),
        ]
        out_specs += [vmem, anywhere]
        gather_sems = 2 * CHUNKS * Gather.SEMS
        aliases = {4 + len(ins) - 1: len(out_shape) - 1}
        src = low(2, *lead, part, model)
        count = 2 * CHUNKS
        reduce_sems = count * Reduce.SEMS
        extra = [
            pltpu.VMEM((count,) + buffer.shape, BF16) for buffer in Reduce.scratch(part, model)
        ] + [
            pltpu.SemaphoreType.DMA((reduce_sems,)), pltpu.SemaphoreType.DMA((reduce_sems,)),
            pltpu.SemaphoreType.DMA((gather_sems,)), pltpu.SemaphoreType.DMA((gather_sems,)),
        ]
        params.update(collective_id=2, has_side_effects=True)
    else:
        out_shape += [jax.ShapeDtypeStruct((2, CHUNKS, chunk_rows, model), BF16)]
        out_specs += [anywhere]
        src = low(2, chunk_rows, model)
        extra = []
        aliases = {}
    return pl.pallas_call(
        functools.partial(middle_kernel, joined),
        in_specs=[smem, vmem] + ([smem, anywhere] if joined else []) + [anywhere] * len(ins),
        out_specs=out_specs,
        out_shape=out_shape,
        scratch_shapes=rows_low
        + [
            low(seq, H * enc_len), full(seq, model), full(seq, model), full(seq, model),
            full(seq, model), low(enc_len, model), low(enc_len, model), low(enc_len, model),
            full(enc_len, model), full(enc_len, model),
        ]
        + [low(model, model)] * 5
        + [
            low(2, 2, chunk_rows, model), src,
            pltpu.SemaphoreType.DMA((10,)), pltpu.SemaphoreType.DMA((2, 2)),
            pltpu.SemaphoreType.DMA((2,)),
        ]
        + extra,
        input_output_aliases=aliases,
        compiler_params=pltpu.CompilerParams(**params),
        name="middle",
    )(length, gains, *([dealing, other] if joined else []), *ins)


def gather_weights(shards, axes):
    pile = lax.all_gather(jnp.concatenate(shards, axis=0), axes, axis=0)
    full, at = [], 0
    for shard in shards:
        full.append(pile[:, at : at + shard.shape[0]].reshape(-1, pile.shape[-1]))
        at += shard.shape[0]
    return full


def reduce_grads(grads, axes):
    dev_count = lax.axis_size("dp") * lax.axis_size("fsdp")
    split = [g.reshape(dev_count, -1, g.shape[-1]) for g in grads]
    pile = lax.psum_scatter(
        jnp.concatenate(split, axis=1), axes, scatter_dimension=0, tiled=False
    ).astype(F32)
    sums, at = [], 0
    for s in split:
        sums.append(pile[at : at + s.shape[1]])
        at += s.shape[1]
    return sums


HIST = 2 * LANES


def self_backward_kernel(
    far_count, x_ref, gain_ref, mid_gain_ref, a_ref, g1_ref, q_ref, k_ref, v_ref, p_ref,
    wo_ref, wq_ref, wk_ref, wv_ref, *refs,
):
    joined = far_count is not None
    if joined:
        egrad_ref, far_refs = refs[0], refs[1 : far_count + 1]
        ingrad_ref, sum_ref, near_sum_ref, small_ref, egrad_other = refs[
            far_count + 1 : far_count + 6
        ]
        rest = refs[far_count + 6 :]
    else:
        ingrad_ref, gw_ref, small_ref, hist_out = refs[:4]
        rest = refs[4:]
    low_ref, near_acc, dk_acc, dv_acc, dq_scr, hist_ref = rest[:6]
    rest = rest[6:]
    step = pl.program_id(0)
    last = pl.num_programs(0) - 1
    seq, model = x_ref.shape
    width = q_ref.shape[1]
    heads = width // DH
    steps = model // width
    events = {}
    if joined:
        src_ref, own_ref, near_small, far_small, send, recv, local = rest[-7:]
        link = Link(send, recv)
        part = sum_ref.shape[0] // far_count
        pieces = []
        for i in range(far_count + steps):
            far = i < far_count
            pieces.append(
                Reduce(
                    far_refs[i] if far else src_ref.at[(i - far_count) % 2],
                    (sum_ref if far else near_sum_ref).at[
                        (i if far else i - far_count) * part
                        : (i + 1 if far else i + 1 - far_count) * part
                    ],
                    own_ref.at[i] if far else None,
                    *rest[Reduce.BUFFERS * i : Reduce.BUFFERS * (i + 1)], link,
                    local.at[i], early=far_count <= i < far_count + steps - 2,
                )
            )
        small = SumSmall(small_ref, near_small, far_small, link)
        swap = Swap(egrad_ref, egrad_other, link, Place())
        far_times = [(0, 1, 3, 4, 7), (0, 1, 3, 5, 7), (0, 1, 4, 5, 8), (0, 2, 4, 5, 7)]
        far_times += [(0, 3, 5, 7, 9)] * (far_count - len(far_times))
        near_times = [(2, 3, 4, 8), (3, 5, 6, 9), (4, 5, 6, 8), (5, 6, 8, 10), (5, 6, 8, 10)]
        near_times += [(7, 8, 9, 10)] * (steps - len(near_times))
        for i in range(far_count):
            for k, time in enumerate(far_times[i]):
                events.setdefault(time, []).append((-k, pieces[i]))
        for i in range(steps):
            for k, time in enumerate(near_times[i]):
                events.setdefault(time, []).append((-k - 1, pieces[far_count + i]))

    def tick(time):
        for k, piece in sorted(events.get(time, []), key=lambda event: event[0]):
            piece.stage(-k)

    @pl.when(step == 0)
    def _():
        if joined:
            greet_peers()
            tick(0)
            swap.start(0)
        low_ref[...] = g1_ref[...].astype(BF16)
        hist_ref[...] = jnp.zeros_like(hist_ref)

    for g in range(1, steps):
        if events.get(g):
            pl.when(step == g)(functools.partial(tick, g))

    d_all = nt(low_ref[...], wo_ref[...]).astype(BF16)
    zero = jnp.zeros((), BF16)
    for pair in range(width // LANES):
        cols = slice(pair * LANES, (pair + 1) * LANES)
        dk_acc[...] = jnp.zeros_like(dk_acc)
        dv_acc[...] = jnp.zeros_like(dv_acc)
        dq_blocks = [None] * (seq // ROWS)
        for which in range(2):
            local_head = pair * 2 + which
            head = step * heads + local_head
            own = head_lane((seq, LANES), which)
            d_out = jnp.where(own, d_all[:, cols], zero)
            queries = jnp.where(own, q_ref[:, cols], zero)
            keys = jnp.where(own, k_ref[:, cols], zero)
            for blk in range(seq // ROWS):
                rows = slice(blk * ROWS, (blk + 1) * ROWS)
                span = (blk + 1) * ROWS
                prob_low = p_ref[local_head, rows, :span]
                prob = prob_low.astype(F32)
                dp = nt(d_out[rows], v_ref[:span, cols])
                ds = prob * (dp - jnp.sum(prob * dp, axis=1, keepdims=True))
                if blk == 0:
                    near_acc[:, :LANES] = jnp.zeros((ROWS, LANES), F32)
                    near_acc[:, LANES:] = ds
                else:
                    near_acc[...] += ds[:, span - ROWS - LANES :]
                ds_low = ds.astype(BF16)
                part_q = nn(ds_low, keys[:span])
                dq_blocks[blk] = part_q if which == 0 else dq_blocks[blk] + part_q
                dk_acc[:span, :] += tn(ds_low, queries[rows])
                dv_acc[:span, :] += tn(prob_low, d_out[rows])
            padded = jnp.concatenate([near_acc[...], jnp.zeros((ROWS, LANES), F32)], axis=1)
            count = ROWS
            while count > 1:
                count //= 2
                padded = padded[:count] + pltpu.roll(padded[count:], 4 * LANES - count, 1)
            hist_ref[pl.ds(head, 1), :] = padded[:, :HIST]
        dq = jnp.concatenate([block.astype(BF16) for block in dq_blocks], axis=0)
        dk = dk_acc[...].astype(BF16)
        dv = dv_acc[...].astype(BF16)
        at = pl.ds(pl.multiple_of(step * width + pair * LANES, LANES), LANES)
        for i, part_grad in enumerate((dq, dk, dv)):
            dq_scr[i, :, at] = part_grad

    @pl.when(step == last)
    def _():
        small_ref[...] = jnp.zeros_like(small_ref)
        small_ref[1:3, :model] = mid_gain_ref[...]
        small_ref[:, model : model + HIST] = hist_ref[0:8, :]
        small_ref[:, model + HIST :] = hist_ref[8:16, :]
        if joined:
            small.stage(0)

    grads = tn(a_ref[...], jnp.concatenate([dq, dk, dv], axis=1))
    if joined:
        for g in range(steps):

            @pl.when(step == g)
            def _():
                if g >= 2:
                    pieces[far_count + g - 2].sent(0)
                src_ref[g % 2] = grads.reshape(src_ref.shape[1:]).astype(BF16)
                pieces[far_count + g].stage(0)
                if g == steps - 1:
                    tick(steps)
    else:
        gw_ref[0] = grads.astype(BF16)

    @pl.when(step == last)
    def _():
        ingrad_ref[...] = nt(dq_scr[0], wq_ref[...])
        if joined:
            tick(steps + 1)
            small.stage(1)
        ingrad_ref[...] += nt(dq_scr[1], wk_ref[...])
        if joined:
            small.stage(2)
        ingrad_ref[...] += nt(dq_scr[2], wv_ref[...])
        if joined:
            tick(steps + 2)
            small.stage(3)
        unit, inv = unit_rows(x_ref[...].astype(F32))
        through, gain_part = norm_back(ingrad_ref[...], unit, inv, gain_ref[0:1, :])
        ingrad_ref[...] = g1_ref[...] + through
        if joined:
            tick(steps + 3)
            small.stage(4)
            swap.arrive(0)
            tick(steps + 4)
            link.drain()
        else:
            small_ref[0:1, :model] = gain_part
            hist_out[...] = hist_ref[...]


def self_backward(
    x, gain, mid_gain, a1, g1, q, k, v, p, wo, wq, wk, wv, far_grads, egrad=None
):
    seq, model = x.shape
    width = 128
    heads = width // DH
    steps = model // width
    joined = far_grads is not None
    held = lambda shape: pl.BlockSpec(
        shape, lambda i: (0,) * len(shape), pipeline_mode=pl.Buffered(1)
    )
    whole = lambda shape: pl.BlockSpec(shape, lambda i: (0,) * len(shape))
    columns = pl.BlockSpec((seq, width), lambda i: (0, i))
    weight_rows = pl.BlockSpec((width, model), lambda i: (i, 0))
    in_specs = [
        held((seq, model)), held((8, model)), held((2, model)), held((seq, model)),
        held((seq, model)), columns, columns, columns,
        pl.BlockSpec((heads, seq, seq), lambda i: (i, 0, 0)),
        weight_rows, held((model, model)), held((model, model)), held((model, model)),
    ]
    small = (8, model + 2 * HIST)
    out_specs = [whole((seq, model))]
    out_shape = [jax.ShapeDtypeStruct((seq, model), F32)]
    scratch = [
        pltpu.VMEM((seq, model), BF16),
        pltpu.VMEM((ROWS, ROWS + LANES), F32),
        pltpu.VMEM((seq, LANES), F32),
        pltpu.VMEM((seq, LANES), F32),
        pltpu.VMEM((3, seq, model), BF16),
        pltpu.VMEM((16, HIST), F32),
    ]
    extra = []
    params = dict(vmem_limit_bytes=63 * 1024 * 1024)
    if joined:
        count = len(far_grads)
        part = model // (SIDE_DP * SIDE_FSDP)
        across = 3 * width
        extra = [egrad] + [g.reshape(SIDE_DP, 2, 2, 2, part, model) for g in far_grads]
        in_specs += [pl.BlockSpec(memory_space=pl.ANY)] * (count + 1)
        shapes = ((count * part, model), (steps * part, across), small, egrad.shape)
        out_specs += [whole(s) for s in shapes[:3]] + [pl.BlockSpec(memory_space=pl.ANY)]
        out_shape += [jax.ShapeDtypeStruct(s, F32) for s in shapes]
        for i in range(count + steps):
            scratch += Reduce.scratch(part, model if i < count else across)
        sems = (count + steps) * Reduce.SEMS + SumSmall.SEMS + Swap.SEMS
        scratch += [
            pltpu.VMEM((2, SIDE_DP, 2, 2, 2, part, across), BF16),
            pltpu.VMEM((count, SIDE_DP, 2, 2, part, model), BF16),
            pltpu.VMEM((3,) + small, F32),
            pltpu.VMEM((SIDE_DP - 1,) + small, F32),
            pltpu.SemaphoreType.DMA((sems,)), pltpu.SemaphoreType.DMA((sems,)),
            pltpu.SemaphoreType.DMA((count + steps,)),
        ]
        params.update(collective_id=3, has_side_effects=True)
    else:
        count = None
        out_specs += [
            pl.BlockSpec((1, model, 3 * width), lambda i: (i, 0, 0)), whole(small),
            whole((16, HIST)),
        ]
        out_shape += [
            jax.ShapeDtypeStruct((steps, model, 3 * width), BF16),
            jax.ShapeDtypeStruct(small, F32),
            jax.ShapeDtypeStruct((16, HIST), F32),
        ]
    return pl.pallas_call(
        functools.partial(self_backward_kernel, count),
        grid=(steps,),
        in_specs=in_specs,
        out_specs=out_specs,
        out_shape=out_shape,
        scratch_shapes=scratch,
        compiler_params=pltpu.CompilerParams(**params),
        cost_estimate=pl.CostEstimate(
            flops=14 * seq * model * model + 8 * seq * seq * model,
            bytes_accessed=2 * H * seq * seq + 24 * seq * model,
            transcendentals=0,
        ),
        name="self_backward",
    )(x, gain, mid_gain, a1, g1, q, k, v, p, wo, wq, wk, wv, *extra)


def exact(left_op, right_op, dims):
    return lax.dot_general(
        left_op, right_op, (dims, ((), ())), preferred_element_type=F32,
        precision=lax.Precision.HIGHEST,
    )


FINISH_SMALL = 11


def finish_kernel(dealing_ref, *refs):
    sources, refs = refs[:FINISH_SMALL], refs[FINISH_SMALL:]
    loaded, load_sems, refs = refs[-FINISH_SMALL - 1 : -1], refs[-1], refs[: -FINISH_SMALL - 1]
    (
        raw_ref, wq_ref, wk_ref, wv_ref, ccq_ref, sum_ref, near_ref, small_ref, wide_ref,
        egrad_ref, other_ref,
    ) = loaded
    loads = [
        pltpu.make_async_copy(src, dst, load_sems.at[i])
        for i, (src, dst) in enumerate(zip(sources, loaded))
    ]
    for copy in loads:
        copy.start()
    (
        enc_ref, gq_ref, gk_ref, gv_ref, go_ref, gcq_ref, gck_ref, gcv_ref,
        gco_ref, gin_ref, gdown_ref, self_ref, cross_ref, ffn_ref, table_ref,
    ) = refs
    for copy in loads:
        copy.wait()
    mine = own_index()
    part, model = gq_ref.shape
    steps = near_ref.shape[0] // part
    width = near_ref.shape[1] // 3
    for ref, i in ((gcq_ref, 0), (gck_ref, 1), (gcv_ref, 2), (gco_ref, 3), (go_ref, 4)):
        ref[...] = sum_ref[i * part : (i + 1) * part, :]
    for g in range(steps):
        for i, ref in enumerate((gq_ref, gk_ref, gv_ref)):
            ref[:, g * width : (g + 1) * width] = near_ref[
                g * part : (g + 1) * part, i * width : (i + 1) * width
            ]
    gin_ref[...] = wide_ref[0]
    gdown_ref[...] = wide_ref[1]
    enc_ref[...] = jnp.where(dealing_ref[mine] == mine, egrad_ref[...], other_ref[...])
    ones = jnp.ones((8, model), F32)
    gains = raw_ref[...].astype(F32)
    weighted = (
        gq_ref[...] * wq_ref[...].astype(F32) + gk_ref[...] * wk_ref[...].astype(F32)
        + gv_ref[...] * wv_ref[...].astype(F32)
    )
    self_ref[...] = exact(ones, weighted, ((1,), (1,)))[0:1, :] / gains[0:1, :part]
    weighted = gcq_ref[...] * ccq_ref[...].astype(F32)
    cross_ref[...] = exact(ones, weighted, ((1,), (1,)))[0:1, :] / gains[1:2, :part]
    entry = lax.broadcasted_iota(jnp.int32, (part, model), 0)
    column = lax.broadcasted_iota(jnp.int32, (part, model), 1)
    place = jnp.where(column == entry + mine * part, 1.0, 0.0)
    ffn_ref[...] = exact(small_ref[:, :model], place, ((1,), (1,)))[2:3, :]
    lane = lax.broadcasted_iota(jnp.int32, (16, HIST), 1)
    distance = LANES - lane
    bucket = bucket_of(jnp.maximum(distance, 0))
    usable = (distance >= 0) & (bucket < NB - 1)
    picked = usable & ((bucket == mine) | (mine == NB - 1))
    sign = jnp.where(mine == NB - 1, -1.0, 1.0)
    hist = jnp.concatenate(
        [small_ref[:, model : model + HIST], small_ref[:, model + HIST :]], axis=0
    )
    sums = exact(ones[:, :HIST], jnp.where(picked, hist, 0.0), ((1,), (1,)))
    table_ref[...] = sign * sums[0:1, : table_ref.shape[1]]


def finish(dealing, raw, shards, sums, near, small, wide, egrad, other):
    part, model = shards[0].shape
    anywhere = pl.BlockSpec(memory_space=pl.ANY)
    vmem = pl.BlockSpec(memory_space=pltpu.VMEM)
    f32 = lambda *shape: jax.ShapeDtypeStruct(shape, F32)
    square = f32(part, model)
    hidden_part = wide.shape[1]
    inputs = [raw, *shards, sums, near, small, wide, egrad, other]
    return pl.pallas_call(
        finish_kernel,
        in_specs=[pl.BlockSpec(memory_space=pltpu.SMEM)] + [anywhere] * len(inputs),
        out_specs=[vmem] * 15,
        out_shape=[f32(*egrad.shape)]
        + [square] * 8
        + [f32(hidden_part, model)] * 2
        + [f32(1, part)] * 3
        + [f32(1, NB * H // (SIDE_DP * SIDE_FSDP))],
        scratch_shapes=[pltpu.VMEM(a.shape, a.dtype) for a in inputs]
        + [pltpu.SemaphoreType.DMA((len(inputs),))],
        compiler_params=pltpu.CompilerParams(vmem_limit_bytes=62 * 1024 * 1024),
        name="finish",
    )(dealing, *inputs)


def body(
    tokens, encoder_states, lengths, dealing, cotangent,
    w_query, w_key, w_value, w_out, c_query, c_key, c_value, c_out, w_in, w_down,
    gain_self, gain_cross, gain_ffn, bias_table,
):
    axes = ("dp", "fsdp")
    fsdp_size = lax.axis_size("fsdp")
    dp_size = lax.axis_size("dp")
    dev_count = dp_size * fsdp_size
    dp_index = lax.axis_index("dp")
    own = dp_index * fsdp_size + lax.axis_index("fsdp")
    seq_len, model = tokens.shape[1:]
    route = [(a, a ^ 1) for a in range(dp_size)]

    x = tokens[0]
    cot = cotangent[0]
    gain_part = gain_self.shape[0]
    joined = dp_size == SIDE_DP and fsdp_size == SIDE_FSDP
    in_rows = w_in.T
    shards = [
        w_query, w_key, w_value, w_out, c_query, c_key, c_value, c_out, in_rows, w_down
    ]
    if joined:
        raw = jnp.stack(
            [gain_self, gain_cross, gain_ffn, jnp.pad(bias_table, (0, gain_part - bias_table.shape[0]))]
        )
        raw = jnp.pad(raw, ((0, 4), (0, 0)))
        done = self_forward(lengths, x, shards, None, raw, encoder_states[0])
        q, k, v, o, p, a1, wq, wk, wv, gains = done[:10]
        wo, cq, ck, cv, co = (w.reshape(model, model) for w in done[10:15])
        done = middle(
            lengths, x, o, cot, encoder_states[0], gains, wo, cq, ck, cv, co, done[15], True,
            dealing, done[16],
        )
        out, g1, egrad, mid_gain_grad = done[:4]
        wide_sums = done[9]
        done = self_backward(
            x, gains, mid_gain_grad, a1, g1, q, k, v, p, wo, wq, wk, wv,
            list(done[4:9]), egrad,
        )
        in_grad, sums, near_sums, small, egrad_other = done
        done = finish(
            dealing, raw, [w_query, w_key, w_value, c_query], sums, near_sums, small, wide_sums,
            egrad, egrad_other,
        )
        return (
            (out[None], in_grad[None], done[0][None]) + tuple(done[1:9]) + (done[9].T, done[10])
            + tuple(d[0] for d in done[11:])
        )

    in_place = lax.dynamic_slice_in_dim(dealing, own, 1) == own
    enc_other = lax.ppermute(encoder_states[0], "dp", route)
    enc = jnp.where(in_place[:, None], encoder_states[0], enc_other)
    length = lax.dynamic_slice_in_dim(lengths, own, 1)
    column = jnp.arange(model, dtype=jnp.int32)[None, :]
    gain_rows = jnp.stack(
        [jnp.tile(g, model // gain_part) for g in (gain_self, gain_cross, gain_ffn)]
    )
    gain_rows = jnp.where(column // gain_part == own, gain_rows, jnp.zeros((), BF16))
    table_row = jnp.pad(bias_table, (0, model - bias_table.shape[0]))[None, :]
    small = jnp.pad(jnp.concatenate([gain_rows, table_row], axis=0), ((0, 4), (0, 0)))
    wq, wk, wv, wo, cq, ck, cv, co, win_t, wdown, small_all = gather_weights(
        shards + [small], axes
    )
    wide = jnp.stack([w.reshape(CHUNKS, -1, model) for w in (win_t, wdown)])
    small_all = small_all.reshape(dev_count, 8, model).astype(F32)
    gains = jnp.sum(small_all, axis=0)
    table = small_all[:, 3, : bias_table.shape[0]].reshape(NB, H)
    table = jnp.pad(table, ((0, 0), (0, LANES - H)))
    q, k, v, o, p, a1 = self_forward(length, x, None, [gains, wq, wk, wv, table])
    done = middle(length, x, o, cot, enc, gains, wo, cq, ck, cv, co, wide, False)
    out, g1, egrad, mid_gain_grad = done[:4]
    squares = list(done[4:9])
    sum_in, sum_down = reduce_grads([g.reshape(-1, model) for g in done[9]], axes)
    done = self_backward(
        x, gains, mid_gain_grad, a1, g1, q, k, v, p, wo, wq, wk, wv, None
    )
    in_grad = done[0]
    gw, small, hist = done[1:]
    g_wq, g_wk, g_wv = (
        jnp.concatenate(
            [g[:, i * LANES : (i + 1) * LANES] for g in gw], axis=1
        )
        for i in range(3)
    )
    distance = jnp.arange(LANES, dtype=jnp.int32)
    bucket_hot = bucket_of(distance)[:, None] == jnp.arange(NB, dtype=jnp.int32)[None, :]
    near_hot = bucket_hot.astype(F32) * (jnp.arange(NB) < NB - 1).astype(F32)
    by_dist = hist[:H, 1 : LANES + 1][:, ::-1]
    near_sums = jnp.dot(near_hot.T, by_dist.T, precision=lax.Precision.HIGHEST)
    grad_table = jnp.where(
        (jnp.arange(NB) < NB - 1)[:, None],
        near_sums, -jnp.sum(near_sums, axis=0, keepdims=True),
    )
    small_grads = jnp.concatenate(
        [small[i, :model].reshape(dev_count, -1) for i in range(3)]
        + [grad_table.reshape(dev_count, -1)],
        axis=1,
    )
    small_count = small_grads.shape[1]
    small_low = jnp.pad(small_grads.astype(BF16), ((0, 0), (0, model - small_count)))
    small_low = jnp.pad(small_low[:, None, :], ((0, 0), (0, 7), (0, 0))).reshape(-1, model)
    sum_cq, sum_ck, sum_cv, sum_co, sum_wo, sum_wq, sum_wk, sum_wv, sum_small = reduce_grads(
        squares + [g_wq, g_wk, g_wv, small_low], axes
    )
    ends = sum_small[0]
    end_self, end_cross, end_ffn = (
        ends[i * gain_part : (i + 1) * gain_part] for i in range(3)
    )
    end_table = ends[3 * gain_part : small_count]

    egrad_other = lax.ppermute(egrad, "dp", route)
    encoder_grad = jnp.where(in_place[:, None], egrad, egrad_other)
    return (
        out[None], in_grad[None], encoder_grad[None],
        sum_wq, sum_wk, sum_wv, sum_wo, sum_cq, sum_ck, sum_cv, sum_co, sum_in.T, sum_down,
        end_self, end_cross, end_ffn, end_table,
    )


def solution(mesh):
    rows3 = P(("dp", "fsdp"), None, None)
    rows2 = P(("dp", "fsdp"), None)
    cols2 = P(None, ("dp", "fsdp"))
    line = P(("dp", "fsdp"))
    in_specs = (
        (rows3, rows3, P(), P(), rows3) + (rows2,) * 8 + (cols2, rows2) + (line,) * 4
    )
    out_specs = (rows3,) * 3 + (rows2,) * 8 + (cols2, rows2) + (line,) * 4
    return jax.shard_map(body, mesh=mesh, in_specs=in_specs, out_specs=out_specs, check_vma=False)
```
